32 devices in a mesh: dp: 8 (over z, x), grp: 4 (over y, core).
Axes of the slice: x: 2, y: 2, z: 4, core: 2. Of those that a mesh axis runs over, the one named last changes fastest.
Arguments:
- x_in: bfloat16 [4096, 1600], P('dp'), may hold values from -6 to 6
- attn_in: bfloat16 [4096, 1600], P('dp', 'grp'), may hold values from -6 to 6
- grad_qkv: bfloat16 [4096, 4800], P('dp', 'grp'), may hold values from -80 to 80
- grad_out: bfloat16 [4096, 1600], P('dp'), may hold values from -80 to 80
- owner: int32 [64], replicated, may hold values from 0 to 7, as said below
- step: int32 [1], replicated, may hold values from 1 to 29
- master: float32 [4, 128, 200, 200], P('grp', 'dp'), may hold values from -0.125 to 0.125
- moment: float32 [4, 128, 200, 200], P('grp', 'dp'), may hold values from -0.3125 to 0.3125
- second: float32 [4, 128, 200, 200], P('grp', 'dp'), may hold values from 0.003 to 0.1
- stat_left: float32 [4, 128, 200, 200], P('grp', 'dp'), may hold values from -8 to 32, as said below
- stat_right: float32 [4, 128, 200, 200], P('grp', 'dp'), may hold values from -8 to 32, as said below
- root_left: float32 [4, 128, 200, 200], P('grp', 'dp'), may hold values from -1 to 4, as said below
- root_right: float32 [4, 128, 200, 200], P('grp', 'dp'), may hold values from -1 to 4, as said below
- qkv_bias: float32 [4800], P('grp'), may hold values from -3 to 3
- qkv_bias_m: float32 [4800], P('grp'), may hold values from -1.25 to 1.25
- qkv_bias_v: float32 [4800], P('grp'), may hold values from 0.01 to 0.3
- proj_bias: float32 [1600], replicated, may hold values from -3 to 3
- proj_bias_m: float32 [1600], replicated, may hold values from -1.25 to 1.25
- proj_bias_v: float32 [1600], replicated, may hold values from 0.01 to 0.3
Outputs:
- master_new: float32 [4, 128, 200, 200], P('grp', 'dp')
- moment_new: float32 [4, 128, 200, 200], P('grp', 'dp')
- second_new: float32 [4, 128, 200, 200], P('grp', 'dp')
- stat_left_new: float32 [4, 128, 200, 200], P('grp', 'dp')
- stat_right_new: float32 [4, 128, 200, 200], P('grp', 'dp')
- qkv_weight: bfloat16 [1600, 4800], P(None, 'grp')
- proj_weight: bfloat16 [1600, 1600], P('grp')
- qkv_bias_new: float32 [4800], P('grp')
- qkv_bias_m_new: float32 [4800], P('grp')
- qkv_bias_v_new: float32 [4800], P('grp')
- proj_bias_new: float32 [1600], replicated
- proj_bias_m_new: float32 [1600], replicated
- proj_bias_v_new: float32 [1600], replicated
The draws below stay inside these ranges and needn't reach their ends.
Inputs may be any that keep to these rules, and one draw needn't show every extreme that they name: `owner`: every index of dp owns at most 16 blocks, and one owns exactly 16. `stat_left`: symmetric. `stat_right`: symmetric. `root_left`: symmetric. `root_right`: symmetric.
All inputs are finite; a program needn't handle non-finite values.
Results may differ from the reference program's by a relative error of at most 0.0004.
Values may be sent and summed in bfloat16 or wider, within the bound.
A program may use at most 192 MiB of HBM per device.

```python
import math
import jax
import jax.numpy as jnp
from jax import lax

D = 1600
BLK = 200
TOKENS = 4096
NQ = 48
NBLK = 64
SLOTS = 16
N_DP = 8
N_GRP = 4


def draw_owner(key, part):
    spots = N_DP * SLOTS
    key_full, key_order, key_blocks = jax.random.split(jax.random.fold_in(key, 17), 3)
    full_device = jax.random.randint(key_full, (), 0, N_DP)
    device_of = jnp.arange(spots, dtype=jnp.int32) // SLOTS
    shuffled = jax.random.permutation(key_order, spots).astype(jnp.int32)
    scores = jnp.where(device_of == full_device, jnp.arange(spots, dtype=jnp.int32) - spots, shuffled)
    order = jnp.argsort(scores, stable=True)
    chosen = (order[:NBLK] // SLOTS).astype(jnp.int32)
    block_order = jax.random.permutation(key_blocks, NBLK)
    return jnp.zeros((NBLK,), jnp.int32).at[block_order].set(chosen)


def symmetric_blocks(key, low, high, level):
    shape = (N_GRP, N_DP * SLOTS, BLK, BLK)
    key_diag, key_off = jax.random.split(key)
    diag = jnp.exp(jax.random.uniform(key_diag, shape[:3], jnp.float32, jnp.log(low), jnp.log(high)))
    off = jnp.clip(jax.random.normal(key_off, shape, jnp.float32), -4.0, 4.0)
    off = (off + jnp.swapaxes(off, 2, 3)) * (0.3 / (2.0 * BLK) ** 0.5)
    unit = jnp.eye(BLK, dtype=jnp.float32)
    return level * (unit * diag[..., None] + (1.0 - unit) * off)


def draw_stat_left(key, part):
    return symmetric_blocks(jax.random.fold_in(key, 21), 0.5, 2.0, 0.04 * BLK)


def draw_stat_right(key, part):
    return symmetric_blocks(jax.random.fold_in(key, 22), 0.5, 2.0, 0.04 * BLK)


def draw_root_left(key, part):
    return symmetric_blocks(jax.random.fold_in(key, 23), 1.0, 2.0, 1.0)


def draw_root_right(key, part):
    return symmetric_blocks(jax.random.fold_in(key, 24), 1.0, 2.0, 1.0)


def shard_levels(own_key, dims, shards, smallest, largest):
    factor_of, own = 1.0, jax.random.fold_in(own_key, 6)
    for dim, parts in shards:
        heights = jnp.exp(jax.random.uniform(jax.random.fold_in(own, dim), (parts,), jnp.float32, smallest / len(shards), largest / len(shards)))
        factor_of = factor_of * jnp.repeat(heights, dims[dim] // parts).reshape([-1 if axis == dim else 1 for axis in range(len(dims))])
    return factor_of


def bell_draw(key, dims, deviation, most, pieces=(), kind=jnp.bfloat16):
    gain = shard_levels(key, dims, pieces, -0.22, 0.18) if pieces else 1.0
    drawn = jax.random.normal(key, dims, jnp.float32) * deviation * gain
    return jnp.minimum(jnp.maximum(drawn, -most), most).astype(kind)


def setup_inputs(seed: int = 0) -> dict:
    streams_of = jax.random.split(jax.random.key(seed), 20)
    return {
        "x_in": bell_draw(streams_of[0], (TOKENS, D), 1.0, 6.0, ((0, 8),)),
        "attn_in": bell_draw(streams_of[1], (TOKENS, D), 1.0, 6.0, ((0, 8), (1, 4))),
        "grad_qkv": bell_draw(streams_of[2], (TOKENS, 3 * D), (0.2 * TOKENS ** 0.5), 80.0, ((0, 8), (1, 4))),
        "grad_out": bell_draw(streams_of[3], (TOKENS, D), (0.2 * TOKENS ** 0.5), 80.0, ((0, 8),)),
        "owner": draw_owner(jax.random.fold_in(streams_of[19], 71), 0),
        "step": jax.random.randint(streams_of[5], (1,), 1, 30).astype(jnp.int32),
        "master": bell_draw(streams_of[6], (N_GRP, N_DP * SLOTS, BLK, BLK), 0.02, 0.125, ((0, 4), (1, 8)), jnp.float32),
        "moment": bell_draw(streams_of[7], (N_GRP, N_DP * SLOTS, BLK, BLK), 0.05, 0.3125, ((0, 4), (1, 8)), jnp.float32),
        "second": jnp.clip(jnp.exp(math.log(0.1) - 3.506558 * jax.random.uniform(streams_of[8], (N_GRP, N_DP * SLOTS, BLK, BLK), jnp.float32) ** shard_levels(streams_of[8], (N_GRP, N_DP * SLOTS, BLK, BLK), ((0, 4), (1, 8)), -0.2, 0.2)), 0.003, 0.1),
        "stat_left": draw_stat_left(jax.random.fold_in(streams_of[19], 71), 0),
        "stat_right": draw_stat_right(jax.random.fold_in(streams_of[19], 71), 0),
        "root_left": draw_root_left(jax.random.fold_in(streams_of[19], 71), 0),
        "root_right": draw_root_right(jax.random.fold_in(streams_of[19], 71), 0),
        "qkv_bias": bell_draw(streams_of[13], (3 * D,), 0.5, 3.0, ((0, 4),), jnp.float32),
        "qkv_bias_m": bell_draw(streams_of[14], (3 * D,), 0.2, 1.25, ((0, 4),), jnp.float32),
        "qkv_bias_v": jnp.clip(jnp.exp(math.log(0.3) - 3.4011974 * jax.random.uniform(streams_of[15], (3 * D,), jnp.float32) ** shard_levels(streams_of[15], (3 * D,), ((0, 4),), -0.2, 0.2)), 0.01, 0.3),
        "proj_bias": bell_draw(streams_of[16], (D,), 0.5, 3.0, (), jnp.float32),
        "proj_bias_m": bell_draw(streams_of[17], (D,), 0.2, 1.25, (), jnp.float32),
        "proj_bias_v": jnp.clip(jnp.exp(jax.random.uniform(streams_of[18], (D,), jnp.float32, math.log(0.01), math.log(0.3))), 0.01, 0.3),
    }


beta_one = 0.9
beta_two = 0.95
beta_stat = 0.9
learn_rate = 0.02
weight_decay = 0.1
epsilon = 1e-08
graft_floor = 1e-06

def positions(owner):
    blocks = jnp.arange(NBLK, dtype=jnp.int32)
    same_owner = owner[None, :] == owner[:, None]
    earlier = blocks[None, :] < blocks[:, None]
    slot_rank = lax.optimization_barrier(jnp.sum(jnp.where(same_owner & earlier, 1, 0).astype(jnp.int32), axis=1))
    return (owner * SLOTS + slot_rank).astype(jnp.int32)

def to_blocks(qkv_part, proj_part):
    rows_q = D // BLK
    cols_q = qkv_part.shape[1] // BLK
    first = qkv_part.reshape(rows_q, BLK, cols_q, BLK).transpose(0, 2, 1, 3).reshape(rows_q * cols_q, BLK, BLK)
    rows_p = proj_part.shape[0] // BLK
    second_part = proj_part.reshape(rows_p, BLK, rows_q, BLK).transpose(0, 2, 1, 3).reshape(rows_p * rows_q, BLK, BLK)
    return jnp.concatenate([first, second_part], axis=0)

def from_blocks(blocks):
    rows_q = D // BLK
    cols_q = 3 * D // (N_GRP * BLK)
    rows_p = D // (N_GRP * BLK)
    first = blocks[:NQ].reshape(rows_q, cols_q, BLK, BLK).transpose(0, 2, 1, 3).reshape(D, cols_q * BLK)
    second_part = blocks[NQ:].reshape(rows_p, rows_q, BLK, BLK).transpose(0, 2, 1, 3).reshape(rows_p * BLK, D)
    return (first, second_part)

def adamw(param, first_m, second_m, grad, fix_one, fix_two):
    new_m = beta_one * first_m + (1.0 - beta_one) * grad
    new_v = beta_two * second_m + (1.0 - beta_two) * grad * grad
    new_p = param - learn_rate * (new_m / fix_one) / (jnp.sqrt(new_v / fix_two) + epsilon)
    return (new_p, new_m, new_v)

def reference(x_in, attn_in, grad_qkv, grad_out, owner, step, master, moment, second, stat_left, stat_right, root_left, root_right, qkv_bias, qkv_bias_m, qkv_bias_v, proj_bias, proj_bias_m, proj_bias_v):
    exact = lax.Precision.HIGHEST
    count_f = step[0].astype(jnp.float32)
    fix_one = 1.0 - jnp.power(jnp.float32(beta_one), count_f)
    fix_two = 1.0 - jnp.power(jnp.float32(beta_two), count_f)
    grad_q = jnp.dot(x_in.T, grad_qkv, preferred_element_type=jnp.float32) / TOKENS
    grad_p = jnp.dot(attn_in.T, grad_out, preferred_element_type=jnp.float32) / TOKENS
    width_q = 3 * D // N_GRP
    width_p = D // N_GRP
    grads = jnp.stack([to_blocks(grad_q[:, group * width_q:(group + 1) * width_q], grad_p[group * width_p:(group + 1) * width_p, :]) for group in range(N_GRP)])
    position = positions(owner)
    is_qkv = jnp.arange(NBLK) < NQ
    old_w = master[:, position]
    old_m = moment[:, position]
    old_v = second[:, position]
    old_l = stat_left[:, position]
    old_r = stat_right[:, position]
    left_root = root_left[:, position]
    right_root = root_right[:, position]
    new_v = beta_two * old_v + (1.0 - beta_two) * grads * grads
    adam_dir = grads / (jnp.sqrt(new_v / fix_two) + epsilon)
    half = jnp.einsum('gbij,gbjk->gbik', left_root, grads, precision=exact)
    shampoo_dir = jnp.einsum('gbij,gbjk->gbik', half, right_root, precision=exact)
    adam_sq = lax.optimization_barrier(jnp.sum(adam_dir * adam_dir, axis=(2, 3)))
    shampoo_sq = lax.optimization_barrier(jnp.sum(shampoo_dir * shampoo_dir, axis=(2, 3)))
    adam_tot = jnp.stack([jnp.sum(jnp.where(is_qkv[None, :], adam_sq, 0.0)), jnp.sum(jnp.where(is_qkv[None, :], 0.0, adam_sq))])
    shampoo_tot = jnp.stack([jnp.sum(jnp.where(is_qkv[None, :], shampoo_sq, 0.0)), jnp.sum(jnp.where(is_qkv[None, :], 0.0, shampoo_sq))])
    graft = jnp.sqrt(adam_tot / (shampoo_tot + graft_floor))
    block_graft = jnp.where(is_qkv, graft[0], graft[1])
    new_m = beta_one * old_m + (1.0 - beta_one) * (block_graft[None, :, None, None] * shampoo_dir)
    new_w = old_w - learn_rate * (new_m + weight_decay * old_w)
    new_l = beta_stat * old_l + (1.0 - beta_stat) * jnp.einsum('gbik,gbjk->gbij', grads, grads, precision=exact)
    new_r = beta_stat * old_r + (1.0 - beta_stat) * jnp.einsum('gbki,gbkj->gbij', grads, grads, precision=exact)
    master_new = master.at[:, position].set(new_w)
    moment_new = moment.at[:, position].set(new_m)
    second_new = second.at[:, position].set(new_v)
    left_new = stat_left.at[:, position].set(new_l)
    right_new = stat_right.at[:, position].set(new_r)
    light = new_w.astype(jnp.bfloat16)
    qkv_parts = []
    proj_parts = []
    for group in range(N_GRP):
        first, second_part = from_blocks(light[group])
        qkv_parts.append(first)
        proj_parts.append(second_part)
    qkv_weight = jnp.concatenate(qkv_parts, axis=1)
    proj_weight = jnp.concatenate(proj_parts, axis=0)
    grad_qb = lax.optimization_barrier(jnp.sum(grad_qkv.astype(jnp.float32), axis=0)) / TOKENS
    grad_pb = lax.optimization_barrier(jnp.sum(grad_out.astype(jnp.float32), axis=0)) / TOKENS
    qb_new, qm_new, qv_new = adamw(qkv_bias, qkv_bias_m, qkv_bias_v, grad_qb, fix_one, fix_two)
    pb_new, pm_new, pv_new = adamw(proj_bias, proj_bias_m, proj_bias_v, grad_pb, fix_one, fix_two)
    return (master_new, moment_new, second_new, left_new, right_new, qkv_weight, proj_weight, qb_new, qm_new, qv_new, pb_new, pm_new, pv_new)
```

```python
import jax
import jax.numpy as jnp
from jax import lax
from jax.experimental import pallas as pl
from jax.experimental.pallas import tpu as pltpu
from jax.sharding import PartitionSpec as P

D = 1600


beta_one = 0.9
beta_two = 0.95
beta_stat = 0.9
learn_rate = 0.02
weight_decay = 0.1
epsilon = 1e-08
graft_floor = 1e-06


def positions(owner, slot_count):
    total_blocks = owner.shape[0]
    blocks = jnp.arange(total_blocks, dtype=jnp.int32)
    same_owner = owner[None, :] == owner[:, None]
    earlier = blocks[None, :] < blocks[:, None]
    slot_rank = jnp.sum(jnp.where(same_owner & earlier, 1, 0).astype(jnp.int32), axis=1)
    return owner * slot_count + slot_rank


def adamw(param, first_m, second_m, grad, fix_one, fix_two):
    new_m = beta_one * first_m + (1.0 - beta_one) * grad
    new_v = beta_two * second_m + (1.0 - beta_two) * grad * grad
    new_p = param - learn_rate * (new_m / fix_one) / (jnp.sqrt(new_v / fix_two) + epsilon)
    return (new_p, new_m, new_v)


def place_kernel(
    split, cols_q, rows_q, slots, holder_ref, used_ref, left_ref, right_ref, tile_ref, peak_ref
):
    o = pl.program_id(0)
    peak_ref[...] = jnp.zeros_like(peak_ref)
    side = left_ref.shape[1]
    for s in range(slots):
        b = holder_ref[o * slots + s]

        @pl.when(used_ref[o * slots + s] > 0)
        def _():
            first = b < split
            later = jnp.maximum(b - split, 0)
            i = jnp.where(first, b // cols_q, rows_q + later // rows_q)
            j = jnp.where(first, b % cols_q, cols_q + later % rows_q)
            tile = lax.dot_general(
                left_ref[i],
                right_ref[j],
                (((1,), (1,)), ((), ())),
                preferred_element_type=jnp.float32,
            )
            tile_ref[0, :, s * side : (s + 1) * side] = tile
            peak_ref[0, s : s + 1, :] = jnp.full((1, 128), jnp.max(jnp.abs(tile)), jnp.float32)


def place_tiles(left, right, holder, used, split, cols_q, rows_q, groups, slots):
    side, depth = left.shape[1:]
    return pl.pallas_call(
        lambda *refs: place_kernel(split, cols_q, rows_q, slots, *refs),
        out_shape=(
            jax.ShapeDtypeStruct((groups, side, slots * side), jnp.float32),
            jax.ShapeDtypeStruct((groups, slots, 128), jnp.float32),
        ),
        grid_spec=pltpu.PrefetchScalarGridSpec(
            num_scalar_prefetch=2,
            grid=(groups,),
            in_specs=[
                pl.BlockSpec(left.shape, lambda o, h, u: (0, 0, 0)),
                pl.BlockSpec(right.shape, lambda o, h, u: (0, 0, 0)),
            ],
            out_specs=[
                pl.BlockSpec((1, side, slots * side), lambda o, h, u: (o, 0, 0)),
                pl.BlockSpec((1, slots, 128), lambda o, h, u: (o, 0, 0)),
            ],
        ),
        compiler_params=pltpu.CompilerParams(vmem_limit_bytes=32 * 1024 * 1024),
    )(holder, used, left, right)


def join_kernel(count, pos_ref, *refs):
    out_ref = refs[count]
    parts = [refs[k][0].astype(jnp.float32) for k in range(count)]
    out_ref[...] = jnp.concatenate(parts, axis=1).astype(out_ref.dtype)


def join_tiles(tiles, position, base, rows, cols):
    side = tiles.shape[1]

    def spot(k):
        return lambda r, pos: (pos[base + r * cols + k], 0, 0)

    return pl.pallas_call(
        lambda *refs: join_kernel(cols, *refs),
        out_shape=jax.ShapeDtypeStruct((rows * side, cols * side), tiles.dtype),
        grid_spec=pltpu.PrefetchScalarGridSpec(
            num_scalar_prefetch=1,
            grid=(rows,),
            in_specs=[pl.BlockSpec((1, side, side), spot(k)) for k in range(cols)],
            out_specs=pl.BlockSpec((side, cols * side), lambda r, pos: (r, 0)),
        ),
        compiler_params=pltpu.CompilerParams(vmem_limit_bytes=32 * 1024 * 1024),
    )(position, *([tiles] * cols))


def sum_kernel(axes, sizes, in_ref, out_ref, *scratch):
    buffers = scratch[: len(axes)]
    send_sems = scratch[len(axes) : 2 * len(axes)]
    recv_sems = scratch[2 * len(axes) :]
    barrier = pltpu.get_barrier_semaphore()
    for axis, size in zip(axes, sizes):
        me = lax.axis_index(axis)
        for k in range(1, size):
            pl.semaphore_signal(
                barrier,
                inc=1,
                device_id={axis: lax.rem(me + k, size)},
                device_id_type=pl.DeviceIdType.MESH,
            )
    pl.semaphore_wait(barrier, sum(size - 1 for size in sizes))
    value = in_ref[...]
    for n, (axis, size) in enumerate(zip(axes, sizes)):
        me = lax.axis_index(axis)
        buffers[n][me] = value
        copies = []
        for k in range(1, size):
            copy = pltpu.make_async_remote_copy(
                src_ref=buffers[n].at[me],
                dst_ref=buffers[n].at[me],
                send_sem=send_sems[n].at[k - 1],
                recv_sem=recv_sems[n].at[k - 1],
                device_id={axis: lax.rem(me + k, size)},
                device_id_type=pl.DeviceIdType.MESH,
            )
            copy.start()
            copies.append(copy)
        for copy in copies:
            copy.wait()
        value = buffers[n][0]
        for k in range(1, size):
            value = value + buffers[n][k]
    out_ref[...] = value


def sum_over(value, axes, collective_id):
    sizes = [lax.axis_size(axis) for axis in axes]
    scratch = [pltpu.VMEM((size,) + value.shape, jnp.float32) for size in sizes]
    scratch += [pltpu.SemaphoreType.DMA((size - 1,)) for size in sizes]
    scratch += [pltpu.SemaphoreType.DMA((size - 1,)) for size in sizes]
    return pl.pallas_call(
        lambda *refs: sum_kernel(axes, sizes, *refs),
        out_shape=jax.ShapeDtypeStruct(value.shape, jnp.float32),
        in_specs=[pl.BlockSpec(memory_space=pltpu.VMEM)],
        out_specs=pl.BlockSpec(memory_space=pltpu.VMEM),
        scratch_shapes=scratch,
        compiler_params=pltpu.CompilerParams(collective_id=collective_id, has_side_effects=True),
    )(value)


def on_device_any(
    x_in,
    attn_in,
    grad_qkv,
    grad_out,
    owner,
    step,
    master,
    moment,
    second,
    stat_left,
    stat_right,
    root_left,
    root_right,
    qkv_bias,
    qkv_bias_m,
    qkv_bias_v,
    proj_bias,
    proj_bias_m,
    proj_bias_v,
):
    exact = lax.Precision.HIGHEST
    groups = lax.axis_size("dp")
    own_index = lax.axis_index("dp")
    total_blocks = owner.shape[0]
    slot_count = master.shape[1]
    block_size = master.shape[2]
    tokens = x_in.shape[0] * groups
    rows_q = D // block_size
    cols_q = grad_qkv.shape[1] // block_size
    rows_p = attn_in.shape[1] // block_size
    first_kind = rows_q * cols_q
    count_f = step[0].astype(jnp.float32)
    fix_one = 1.0 - jnp.power(jnp.float32(beta_one), count_f)
    fix_two = 1.0 - jnp.power(jnp.float32(beta_two), count_f)
    blocks = jnp.arange(total_blocks, dtype=jnp.int32)
    position = positions(owner, slot_count)
    spots = groups * slot_count
    matches = position[None, :] == jnp.arange(spots, dtype=jnp.int32)[:, None]
    filled = jnp.any(matches, axis=1)
    holder = jnp.sum(jnp.where(matches, blocks[None, :], 0), axis=1)
    my_blocks = lax.dynamic_slice_in_dim(holder, own_index * slot_count, slot_count)
    my_filled = lax.dynamic_slice_in_dim(filled, own_index * slot_count, slot_count)
    filled_f = my_filled.astype(jnp.float32)
    keep = my_filled[:, None, None]

    depth = x_in.shape[0]
    left = jnp.concatenate(
        [
            x_in.T.reshape(rows_q, block_size, depth),
            attn_in.T.reshape(rows_p, block_size, depth),
        ]
    )
    right = jnp.concatenate(
        [
            grad_qkv.T.reshape(cols_q, block_size, depth),
            grad_out.T.reshape(rows_q, block_size, depth),
        ]
    )
    local_tiles, peaks = place_tiles(
        left,
        right,
        holder,
        filled.astype(jnp.int32),
        first_kind,
        cols_q,
        rows_q,
        groups,
        slot_count,
    )

    width_q, width_p = grad_qkv.shape[1], grad_out.shape[1]
    small = jnp.concatenate(
        [
            jnp.sum(grad_qkv, axis=0, dtype=jnp.float32),
            jnp.sum(grad_out, axis=0, dtype=jnp.float32),
            peaks[:, :, 0].reshape(spots),
        ]
    )
    used = small.shape[0]
    padded = -(-used // 1024) * 1024
    small = jnp.pad(small, (0, padded - used)).reshape(8, padded // 8)
    small = sum_over(small, ("dp",), 0).reshape(padded)
    qkv_total = small[:width_q]
    proj_total = small[width_q : width_q + width_p]
    bound = small[width_q + width_p : used]
    spot_bound = jnp.where(bound > 0.0, bound, 1.0).reshape(groups, 1, slot_count)
    spot_bound = jnp.repeat(spot_bound, block_size, axis=2)
    shrink = 16384.0 / spot_bound
    grow = spot_bound / 16384.0

    pair = own_index // 2
    side = own_index % 2
    pairs = groups // 2
    tiles = local_tiles

    def chunk(array, where):
        return lax.dynamic_index_in_dim(array, where, 0, keepdims=False)

    across = [(d, d ^ 1) for d in range(groups)]
    arrivals = []
    order = list(range(1, pairs))
    if pairs == 4:
        order = [1, 3, 2]
    order = order + [0]
    received = []
    for step_off in order:
        theirs = lax.rem(pair + step_off, pairs) * 2 + 1 - side
        sent = (chunk(tiles, theirs) * chunk(shrink, theirs)).astype(jnp.float16)
        received.append(lax.ppermute(sent, "dp", across))
    after = jnp.int32(0)
    for step_off, got in zip(order, received):
        ours = lax.rem(pair + step_off, pairs) * 2 + side
        both = chunk(tiles, ours + after) * chunk(shrink, ours) + got.astype(jnp.float32)
        if step_off == 0:
            mine = both
        else:
            hop = [(d, ((d // 2 + step_off) % pairs) * 2 + d % 2) for d in range(groups)]
            both = both.astype(jnp.float16)
            arrivals.append(lax.ppermute(both, "dp", hop))
            probe = arrivals[-1][0, 0].astype(jnp.float32)
            after = jnp.minimum((probe == probe).astype(jnp.int32), 0)
    for arrived in arrivals:
        mine = mine + arrived.astype(jnp.float32)
    mine = mine * (chunk(grow, own_index) / tokens)
    mine = mine.reshape(block_size, slot_count, block_size).transpose(1, 0, 2)
    grads = jnp.where(keep, mine, 0.0)
    old_w = master[0]
    old_m = moment[0]
    old_v = second[0]
    old_l = stat_left[0]
    old_r = stat_right[0]
    new_v = beta_two * old_v + (1.0 - beta_two) * grads * grads
    adam_dir = grads / (jnp.sqrt(new_v / fix_two) + epsilon)
    half = jnp.einsum("sij,sjk->sik", root_left[0], grads, precision=exact)
    shampoo_dir = jnp.einsum("sij,sjk->sik", half, root_right[0], precision=exact)
    is_qkv = my_blocks < first_kind
    adam_sq = jnp.sum(adam_dir * adam_dir, axis=(1, 2)) * filled_f
    shampoo_sq = jnp.sum(shampoo_dir * shampoo_dir, axis=(1, 2)) * filled_f
    sums = [
        jnp.sum(jnp.where(is_qkv, adam_sq, 0.0)),
        jnp.sum(jnp.where(is_qkv, 0.0, adam_sq)),
        jnp.sum(jnp.where(is_qkv, shampoo_sq, 0.0)),
        jnp.sum(jnp.where(is_qkv, 0.0, shampoo_sq)),
    ]
    lane = lax.broadcasted_iota(jnp.int32, (8, 128), 1)
    part = jnp.zeros((8, 128), jnp.float32)
    for n, value in enumerate(sums):
        part = jnp.where(lane == n, value, part)
    total = sum_over(part, ("grp", "dp"), 1)
    graft = jnp.sqrt(total[0, 0:2] / (total[0, 2:4] + graft_floor))
    block_graft = jnp.where(is_qkv, graft[0], graft[1])
    new_m = beta_one * old_m + (1.0 - beta_one) * (block_graft[:, None, None] * shampoo_dir)
    new_w = old_w - learn_rate * (new_m + weight_decay * old_w)
    new_l = beta_stat * old_l + (1.0 - beta_stat) * jnp.einsum(
        "sik,sjk->sij", grads, grads, precision=exact
    )
    new_r = beta_stat * old_r + (1.0 - beta_stat) * jnp.einsum(
        "ski,skj->sij", grads, grads, precision=exact
    )
    master_new = jnp.where(keep, new_w, old_w)
    moment_new = jnp.where(keep, new_m, old_m)
    second_new = jnp.where(keep, new_v, old_v)
    left_new = jnp.where(keep, new_l, old_l)
    right_new = jnp.where(keep, new_r, old_r)
    new_weights = master_new.astype(jnp.bfloat16)
    spread = [new_weights]
    turns = None
    if pairs == 4:
        up = [(d, d + 2) for d in range(groups - 2)]
        down = [(d + 2, d) for d in range(groups - 2)]
        from_low, from_high = [new_weights], [new_weights]
        for k in range(1, pairs):
            from_low.append(lax.ppermute(from_low[-1], "dp", up))
            from_high.append(lax.ppermute(from_high[-1], "dp", down))
        rows = []
        for z in range(pairs):
            found = [(k, 0) for k in range(1, z + 1)] + [(k, 1) for k in range(1, pairs - z)]
            rows.append(sorted(found))
        turns = [[0] * pairs for _ in range(pairs)]
        other = [lax.ppermute(new_weights, "dp", across)]
        for m in range(pairs - 1):
            value = None
            probe = other[-1][0, 0, 0].astype(jnp.float32)
            here = pair + jnp.minimum((probe == probe).astype(jnp.int32), 0)
            for z in range(pairs):
                k, way = rows[z][m]
                turns[z][z + k if way else z - k] = m + 1
                part_w = (from_low, from_high)[way][k]
                value = part_w if value is None else jnp.where(here == z, part_w, value)
            spread.append(value)
            other.append(lax.ppermute(value, "dp", across))
    else:
        for step_off in range(1, pairs):
            hop = [(d, ((d // 2 + step_off) % pairs) * 2 + d % 2) for d in range(groups)]
            spread.append(lax.ppermute(new_weights, "dp", hop))
        other = [lax.ppermute(part_w, "dp", across) for part_w in spread]
    everyone = jnp.concatenate(spread + other)
    place_owner = owner // 2
    turn = lax.rem(pair - place_owner + pairs, pairs)
    if turns is not None:
        turn = jnp.zeros_like(owner)
        for z in range(pairs):
            for origin in range(pairs):
                hit = (pair == z) & (place_owner == origin)
                turn = jnp.where(hit, turns[z][origin], turn)
    held = jnp.where(owner % 2 == side, turn, pairs + turn)
    where_held = held * slot_count + (position - owner * slot_count)
    qkv_weight = join_tiles(everyone, where_held, 0, rows_q, cols_q)
    proj_weight = join_tiles(everyone, where_held, first_kind, rows_p, rows_q)
    qb_new, qm_new, qv_new = adamw(
        qkv_bias, qkv_bias_m, qkv_bias_v, qkv_total / tokens, fix_one, fix_two
    )
    pb_new, pm_new, pv_new = adamw(
        proj_bias, proj_bias_m, proj_bias_v, proj_total / tokens, fix_one, fix_two
    )
    return (
        master_new[None],
        moment_new[None],
        second_new[None],
        left_new[None],
        right_new[None],
        qkv_weight,
        proj_weight,
        qb_new,
        qm_new,
        qv_new,
        pb_new,
        pm_new,
        pv_new,
    )


SIDE = 200
COLUMN = 32
HALF = 16
WIDE = HALF * SIDE
CHUNK = 640
PER_HALF = WIDE // CHUNK
CHUNKS = 2 * PER_HALF
ROWS = 208
MOVES = 8
MOVE_WIDE = 1664
PLANES = 4
STEPS = 8.0
TOP = 32000.0
MESH = pl.DeviceIdType.MESH


def pick(table, hits):
    return jnp.sum(jnp.where(hits, table, 0), axis=-1)


def layout_tables(owner, me, kind_split, cols_q, rows_q):
    total = owner.shape[0]
    blocks = jnp.arange(total, dtype=jnp.int32)
    devices = jnp.arange(2 * PLANES, dtype=jnp.int32)
    own = owner[:, None] == devices[None, :]
    same = owner[None, :] == owner[:, None]
    slot = jnp.sum((same & (blocks[None, :] < blocks[:, None])).astype(jnp.int32), axis=1)
    n = jnp.sum(own.astype(jnp.int32), axis=0).reshape(PLANES, 2)
    n0, n1 = n[:, 0], n[:, 1]
    total0 = jnp.sum(n0)
    full = (total0 < COLUMN).astype(jnp.int32)
    surplus = jnp.abs(total0 - COLUMN)
    crowded = jnp.where(full == 0, n0, n1)
    other = jnp.where(full == 0, n1, n0)
    room = jnp.minimum(jnp.minimum(MOVES, crowded), HALF - other)
    levels = jnp.arange(MOVES + 1, dtype=jnp.int32)
    filled_to = jnp.sum(jnp.minimum(room[None, :], levels[:, None]), axis=1)
    level = jnp.sum((filled_to <= surplus).astype(jnp.int32)) - 1
    base = jnp.minimum(room, level)
    rest = surplus - jnp.sum(base)
    can = (room > level).astype(jnp.int32)
    planes = jnp.arange(PLANES, dtype=jnp.int32)
    before = jnp.sum(jnp.where(planes[None, :] < planes[:, None], can[None, :], 0), axis=1)
    move = base + jnp.where((can > 0) & (before < rest), 1, 0)
    sides = jnp.arange(2, dtype=jnp.int32)
    gives = sides[None, :] == full
    height = n + jnp.where(gives, -move[:, None], move[:, None])
    earlier = planes[None, :] < planes[:, None]
    start = jnp.sum(jnp.where(earlier[:, :, None], height[None], 0), axis=1)
    stay = (n - jnp.where(gives, move[:, None], 0)).reshape(-1)
    flat_n, flat_start = n.reshape(-1), start.reshape(-1)
    swapped_n = n[:, ::-1].reshape(-1)
    swapped_start = start[:, ::-1].reshape(-1)
    stay_b = pick(stay[None, :], own)
    moved = slot >= stay_b
    place = jnp.where(
        moved,
        pick((swapped_start + swapped_n - stay)[None, :], own),
        pick(flat_start[None, :], own),
    ) + slot
    column = jnp.where(moved, 1 - owner % 2, owner % 2)
    line = column * COLUMN + place
    side = me % 2
    mine = devices == me
    my_n, my_stay, my_start = pick(flat_n, mine), pick(stay, mine), pick(flat_start, mine)
    my_height = pick(height.reshape(-1), mine)
    spots = jnp.arange(2 * COLUMN, dtype=jnp.int32)
    wanted = (spots + side * COLUMN) % (2 * COLUMN)
    at = pick(blocks[None, :], line[None, :] == wanted[:, None])
    later = jnp.maximum(at - kind_split, 0)
    first = at < kind_split
    left_at = jnp.where(first, at // cols_q, rows_q + later // rows_q)
    right_at = jnp.where(first, at % cols_q, cols_q + later % rows_q)
    slots = jnp.arange(HALF, dtype=jnp.int32)
    holds = slots < my_n
    source = jnp.where(slots < my_stay, my_start + slots, COLUMN + slots - my_stay)
    source = jnp.where(holds, jnp.minimum(source, COLUMN + MOVES - 1), 0)
    turn = jnp.arange(MOVES, dtype=jnp.int32)
    give_at = jnp.minimum(my_start + my_n + turn, COLUMN - 1)
    give_slot = jnp.minimum(my_stay + turn, HALF - 1)
    spot = jnp.arange(COLUMN, dtype=jnp.int32) - my_start
    from_slot = jnp.where(spot < my_stay, spot, jnp.where(my_n > my_stay, 0, HALF + spot - my_n))
    from_slot = jnp.clip(from_slot, 0, HALF + MOVES - 1)
    my_blocks = pick(blocks[None, :], own_slot(owner, slot, me, slots))
    seen = jnp.where(column == side, place, COLUMN + place)
    edges = jnp.stack([my_start * SIDE, (my_start + my_height) * SIDE])
    return left_at, right_at, source, give_at, give_slot, from_slot, holds, my_blocks, seen, edges


def own_slot(owner, slot, me, slots):
    return (owner[None, :] == me) & (slot[None, :] == slots[:, None])


def pack(value):
    top = jnp.max(jnp.abs(value), axis=0, keepdims=True)
    code = jnp.ceil(jnp.log(jnp.maximum(top, 1e-30)) * (STEPS / LN2))
    scale = TOP / jnp.exp(code * (LN2 / STEPS))
    whole = jnp.round(value * scale).astype(jnp.int32)
    codes = jnp.broadcast_to(code.astype(jnp.int32), (ROWS - SIDE, value.shape[1]))
    return jnp.concatenate([whole, codes], axis=0).astype(jnp.int16)


def unpack(coded):
    wide = coded.astype(jnp.int32).astype(jnp.float32)
    scale = jnp.exp(wide[SIDE : SIDE + 1] * (LN2 / STEPS)) * (1.0 / TOP)
    return wide[:SIDE] * scale


LN2 = 0.6931471805599453


def lanes(k):
    return pl.ds(pl.multiple_of((k % PER_HALF) * CHUNK, 128), CHUNK)


def greet(peers):
    barrier = pltpu.get_barrier_semaphore()
    count = 0
    for condition, device in peers:
        if condition is None:
            pl.semaphore_signal(barrier, inc=1, device_id=device, device_id_type=MESH)
            count = count + 1
        else:

            @pl.when(condition)
            def _():
                pl.semaphore_signal(barrier, inc=1, device_id=device, device_id_type=MESH)

            count = count + condition.astype(jnp.int32)
    pl.semaphore_wait(barrier, count)


def remote(src, dst, send, recv, device):
    return pltpu.make_async_remote_copy(
        src_ref=src, dst_ref=dst, send_sem=send, recv_sem=recv, device_id=device, device_id_type=MESH
    )


def loop(low, high, body):
    lax.fori_loop(low, high, lambda k, carry: (body(k), carry)[1], 0)


def reduce_kernel(
    tokens,
    left_at,
    right_at,
    source,
    give_at,
    holds,
    left,
    right,
    out,
    stage,
    pair,
    sent_x,
    got_x,
    sent_up,
    got_up,
    sent_down,
    got_down,
    tiles,
    stage_m,
    sent_m,
    got_m,
    sems,
    sems_m,
):
    me = lax.axis_index("dp")
    z, side = me // 2, me % 2
    across = {"dp": me + 1 - 2 * side}
    upper = {"dp": jnp.minimum(me + 2, 2 * PLANES - 1)}
    lower = {"dp": jnp.maximum(me - 2, 0)}
    last = PLANES - 1
    greet([(None, across), (z < last, upper), (z > 0, lower)])

    def copy_x(k):
        return remote(sent_x.at[k], got_x.at[k], sems.at[0, k], sems.at[1, k], across)

    def copy_up(k):
        return remote(sent_up.at[k], got_up.at[k], sems.at[2, k], sems.at[3, k], upper)

    def copy_down(k):
        return remote(sent_down.at[k], got_down.at[k], sems.at[4, k], sems.at[5, k], lower)

    def tile(n, j, into):
        product = lax.dot_general(
            left[left_at[n]],
            right[right_at[n]],
            (((1,), (1,)), ((), ())),
            preferred_element_type=jnp.float32,
        )
        into[:, j * SIDE : (j + 1) * SIDE] = product

    def other_half(h):
        done = 0
        for q in range(PER_HALF):
            need = -(-(q + 1) * CHUNK // SIDE)
            for j in range(done, need):
                tile(COLUMN + h * HALF + j, j, stage)
            done = need
            k = h * PER_HALF + q
            sent_x[k] = pack(stage[:, q * CHUNK : (q + 1) * CHUNK])
            copy_x(k).start()

    loop(0, 2, other_half)

    def own_half(h):
        for j in range(HALF):
            tile(h * HALF + j, j, pair.at[h])

    loop(0, 2, own_half)

    def step(t):
        @pl.when(t < CHUNKS)
        def _():
            copy_x(t).wait_recv()
            pair[t // PER_HALF, :, lanes(t)] += unpack(got_x[t])

        up = t - z

        @pl.when((up >= 0) & (up < CHUNKS))
        def _():
            h = up // PER_HALF

            @pl.when(z == 0)
            def _():
                sent_up[up] = pack(pair[h, :, lanes(up)])

            @pl.when(z > 0)
            def _():
                copy_up(up).wait_recv()

                @pl.when(z < last)
                def _():
                    sent_up[up] = pack(pair[h, :, lanes(up)] + unpack(got_up[up]))

            @pl.when(z < last)
            def _():
                copy_up(up).start()

        down = t - (last - z)

        @pl.when((down >= 0) & (down < CHUNKS))
        def _():
            h = down // PER_HALF

            @pl.when(z == last)
            def _():
                sent_down[down] = pack(pair[h, :, lanes(down)])

            @pl.when(z < last)
            def _():
                copy_down(down).wait_recv()

                @pl.when(z > 0)
                def _():
                    sent_down[down] = pack(pair[h, :, lanes(down)] + unpack(got_down[down]))

            @pl.when(z > 0)
            def _():
                copy_down(down).start()

        full = t - last

        @pl.when(full >= 0)
        def _():
            h = full // PER_HALF

            @pl.when(z > 0)
            def _():
                pair[h, :, lanes(full)] += unpack(got_up[full])

            @pl.when(z < last)
            def _():
                pair[h, :, lanes(full)] += unpack(got_down[full])

            @pl.when(full % PER_HALF == PER_HALF - 1)
            def _():
                for j in range(HALF):
                    tiles[h * HALF + j] = pair[h, :, j * SIDE : (j + 1) * SIDE]

    loop(0, CHUNKS + last, step)

    stage_m[:, MOVES * SIDE :] = jnp.zeros((SIDE, MOVE_WIDE - MOVES * SIDE), jnp.float32)
    for k in range(MOVES):
        stage_m[:, k * SIDE : (k + 1) * SIDE] = tiles[give_at[k]]
    sent_m[...] = pack(stage_m[...])
    move = remote(sent_m, got_m, sems_m.at[0], sems_m.at[1], across)
    move.start()

    def drain(k):
        copy_x(k).wait_send()

        @pl.when(z < last)
        def _():
            copy_up(k).wait_send()

        @pl.when(z > 0)
        def _():
            copy_down(k).wait_send()

    loop(0, CHUNKS, drain)
    move.wait()
    stage_m[...] = unpack(got_m[...])
    for k in range(MOVES):
        tiles[COLUMN + k] = stage_m[:, k * SIDE : (k + 1) * SIDE]

    def finish(s):
        out[s] = jnp.where(holds[s] > 0, tiles[source[s]] * (1.0 / tokens), 0.0)

    loop(0, HALF, finish)


def vmem():
    return pl.BlockSpec(memory_space=pltpu.VMEM)


def smem():
    return pl.BlockSpec(memory_space=pltpu.SMEM)


def hbm():
    return pl.BlockSpec(memory_space=pl.ANY)


def reduce_tiles(left, right, left_at, right_at, source, give_at, holds, tokens):
    coded = pltpu.VMEM((CHUNKS, ROWS, CHUNK), jnp.int16)
    return pl.pallas_call(
        lambda *refs: reduce_kernel(tokens, *refs),
        out_shape=jax.ShapeDtypeStruct((HALF, SIDE, SIDE), jnp.float32),
        in_specs=[smem()] * 5 + [vmem()] * 2,
        out_specs=vmem(),
        scratch_shapes=[
            pltpu.VMEM((SIDE, WIDE), jnp.float32),
            pltpu.VMEM((2, SIDE, WIDE), jnp.float32),
            coded,
            coded,
            coded,
            coded,
            coded,
            coded,
            pltpu.VMEM((COLUMN + MOVES, SIDE, SIDE), jnp.float32),
            pltpu.VMEM((SIDE, MOVE_WIDE), jnp.float32),
            pltpu.VMEM((ROWS, MOVE_WIDE), jnp.int16),
            pltpu.VMEM((ROWS, MOVE_WIDE), jnp.int16),
            pltpu.SemaphoreType.DMA((6, CHUNKS)),
            pltpu.SemaphoreType.DMA((2,)),
        ],
        compiler_params=pltpu.CompilerParams(
            collective_id=0, has_side_effects=True, vmem_limit_bytes=VMEM_LIMIT
        ),
    )(left_at, right_at, source, give_at, holds, left, right)


VMEM_LIMIT = 58 * 1024 * 1024
SMALL_ROWS = 32
BIAS_ROWS = 24


def dot3(a, b, dims):
    return lax.dot_general(
        a, b, (dims, ((), ())), precision=lax.Precision.HIGHEST, preferred_element_type=jnp.float32
    )


def step_kernel(
    holds,
    kinds,
    give_slot,
    from_slot,
    edges,
    fixes,
    grads,
    small,
    master,
    moment,
    second,
    stat_left,
    stat_right,
    root_left,
    root_right,
    master_out,
    moment_out,
    second_out,
    left_out,
    right_out,
    small_out,
    blocks,
    state_w,
    state_m,
    state_v,
    state_l,
    state_r,
    state_a,
    state_b,
    sums,
    sums_dp,
    sums_grp,
    light,
    sent_m,
    got_m,
    own,
    got_up,
    got_down,
    known,
    got_x,
    load_sems,
    store_sems,
    sum_sems,
    grp_sems,
    move_sems,
    sems,
):
    me = lax.axis_index("dp")
    z, side = me // 2, me % 2
    n_dp, n_grp = lax.axis_size("dp"), lax.axis_size("grp")
    my_grp = lax.axis_index("grp")
    across = {"dp": me + 1 - 2 * side}
    upper = {"dp": jnp.minimum(me + 2, 2 * PLANES - 1)}
    lower = {"dp": jnp.maximum(me - 2, 0)}
    last = PLANES - 1
    held = [state_v, state_a, state_b, state_w, state_m, state_l, state_r]
    given = [second, root_left, root_right, master, moment, stat_left, stat_right]
    loads = []
    for n, (ref, scratch) in enumerate(zip(given, held)):
        copy = pltpu.make_async_copy(ref.at[0], scratch, load_sems.at[n])
        copy.start()
        loads.append(copy)

    def store(scratch, ref, n):
        return pltpu.make_async_copy(scratch, ref.at[0], store_sems.at[n])

    peers = [(None, {"dp": lax.rem(me + k, n_dp)}) for k in range(1, n_dp)]
    peers += [(None, {"grp": lax.rem(my_grp + k, n_grp)}) for k in range(1, n_grp)]
    greet(peers)

    fix_two = fixes[0]
    for copy in loads[:3]:
        copy.wait()

    def direction(s, sums_now):
        adam_q, adam_p, shampoo_q, shampoo_p = sums_now
        grad = grads[s]
        old = state_v[s]
        new = beta_two * old + (1.0 - beta_two) * grad * grad
        adam = grad / (jnp.sqrt(new / fix_two) + epsilon)
        half = dot3(state_a[s], grad, ((1,), (0,)))
        shampoo = dot3(half, state_b[s], ((1,), (0,)))
        state_v[s] = jnp.where(holds[s] > 0, new, old)
        state_a[s] = shampoo
        adam_sq = jnp.sum(adam * adam, axis=0, keepdims=True)
        shampoo_sq = jnp.sum(shampoo * shampoo, axis=0, keepdims=True)
        q = kinds[s] > 0
        return (
            adam_q + jnp.where(q, adam_sq, 0.0),
            adam_p + jnp.where(q, 0.0, adam_sq),
            shampoo_q + jnp.where(q, shampoo_sq, 0.0),
            shampoo_p + jnp.where(q, 0.0, shampoo_sq),
        )

    nothing = jnp.zeros((1, SIDE), jnp.float32)
    parts = lax.fori_loop(0, HALF, direction, (nothing,) * 4)
    store(state_v, second_out, 0).start()
    sums[0, :BIAS_ROWS] = small[...]
    row = lax.broadcasted_iota(jnp.int32, (SMALL_ROWS - BIAS_ROWS, 128), 0)
    packed = jnp.zeros((SMALL_ROWS - BIAS_ROWS, 128), jnp.float32)
    for n, part in enumerate(parts):
        packed = jnp.where(row == n, jnp.sum(part), packed)
    sums[0, BIAS_ROWS:] = packed

    copies = []
    for k in range(1, n_dp):
        copy = remote(
            sums.at[0], sums_dp.at[k - 1], sum_sems.at[0, k - 1], sum_sems.at[1, k - 1],
            {"dp": lax.rem(me + k, n_dp)},
        )
        copy.start()
        copies.append(copy)
    for copy in loads[3:5]:
        copy.wait()
    for copy in copies:
        copy.wait()
    for d in range(n_dp):
        value = jnp.where(me == d, sums[0], sums_dp[lax.rem(me - d + n_dp + n_dp - 1, n_dp) % (n_dp - 1)])
        total = value if d == 0 else total + value
    small_out[...] = total[:BIAS_ROWS]
    sums_grp[my_grp] = total[BIAS_ROWS:]
    copies = []
    for k in range(1, n_grp):
        copy = remote(
            sums_grp.at[my_grp], sums_grp.at[my_grp], grp_sems.at[0, k - 1], grp_sems.at[1, k - 1],
            {"grp": lax.rem(my_grp + k, n_grp)},
        )
        copy.start()
        copies.append(copy)
    for copy in copies:
        copy.wait()
    total = sums_grp[0]
    for g in range(1, n_grp):
        total = total + sums_grp[g]
    graft_q = jnp.sqrt(total[0:1] / (total[2:3] + graft_floor))[:, :1]
    graft_p = jnp.sqrt(total[1:2] / (total[3:4] + graft_floor))[:, :1]

    def update(s):
        graft = jnp.where(kinds[s] > 0, graft_q, graft_p)
        old_m, old_w = state_m[s], state_w[s]
        new_m = beta_one * old_m + (1.0 - beta_one) * (graft * state_a[s])
        new_w = old_w - learn_rate * (new_m + weight_decay * old_w)
        state_m[s] = jnp.where(holds[s] > 0, new_m, old_m)
        state_w[s] = jnp.where(holds[s] > 0, new_w, old_w)
        light[s] = jnp.where(kinds[s] > 0, new_w.T, new_w).astype(jnp.bfloat16)

    loop(0, HALF, update)
    store(state_m, moment_out, 1).start()
    store(state_w, master_out, 2).start()

    sent_m[...] = jnp.zeros_like(sent_m)
    for k in range(MOVES):
        sent_m[:SIDE, k * SIDE : (k + 1) * SIDE] = light[give_slot[k]]
    move = remote(sent_m, got_m, move_sems.at[0], move_sems.at[1], across)
    move.start()

    for copy in loads[5:7]:
        copy.wait()

    def stats(s):
        grad = grads[s]
        keep = holds[s] > 0
        new_l = beta_stat * state_l[s] + (1.0 - beta_stat) * dot3(grad, grad, ((1,), (1,)))
        new_r = beta_stat * state_r[s] + (1.0 - beta_stat) * dot3(grad, grad, ((0,), (0,)))
        state_l[s] = jnp.where(keep, new_l, state_l[s])
        state_r[s] = jnp.where(keep, new_r, state_r[s])

    move.wait()
    for k in range(MOVES):
        light[HALF + k] = got_m[:SIDE, k * SIDE : (k + 1) * SIDE]
    own[:, SIDE:] = jnp.zeros((2, ROWS - SIDE, WIDE), jnp.bfloat16)

    def fill(h):
        for j in range(HALF):
            own[h, :SIDE, j * SIDE : (j + 1) * SIDE] = light[from_slot[h * HALF + j]]

    loop(0, 2, fill)

    low, high = edges[0], edges[1]
    lane = lax.broadcasted_iota(jnp.int32, (1, CHUNK), 1)

    def part(ref, k):
        return ref.at[k // PER_HALF, :, lanes(k)]

    def copy_up(k, src):
        return remote(part(src, k), part(got_up, k), sems.at[0, k], sems.at[1, k], upper)

    def copy_down(k, src):
        return remote(part(src, k), part(got_down, k), sems.at[2, k], sems.at[3, k], lower)

    def copy_x(k):
        return remote(part(known, k), part(got_x, k), sems.at[4, k], sems.at[5, k], across)

    def step(t):
        up = t - z

        @pl.when((up >= 0) & (up < CHUNKS))
        def _():
            @pl.when(z == 0)
            def _():
                @pl.when(up < PER_HALF)
                def _():
                    copy_up(up, own).start()

            @pl.when(z > 0)
            def _():
                h = up // PER_HALF

                @pl.when((z > 1) | (up < PER_HALF))
                def _():
                    copy_up(up, own).wait_recv()
                    mask = lane + up * CHUNK < low
                    got_up[h, :, lanes(up)] = jnp.where(
                        mask, got_up[h, :, lanes(up)].astype(jnp.float32), own[h, :, lanes(up)].astype(jnp.float32)
                    ).astype(jnp.bfloat16)

                @pl.when((z == 1) & (up >= PER_HALF))
                def _():
                    got_up[h, :, lanes(up)] = own[h, :, lanes(up)]

                @pl.when(z < last)
                def _():
                    copy_up(up, got_up).start()

        down = t - (last - z)

        @pl.when((down >= 0) & (down < CHUNKS))
        def _():
            @pl.when(z == last)
            def _():
                @pl.when(down >= PER_HALF)
                def _():
                    copy_down(down, own).start()

            @pl.when(z < last)
            def _():
                h = down // PER_HALF

                @pl.when((z < last - 1) | (down >= PER_HALF))
                def _():
                    copy_down(down, own).wait_recv()
                    mask = lane + down * CHUNK >= high
                    got_down[h, :, lanes(down)] = jnp.where(
                        mask,
                        got_down[h, :, lanes(down)].astype(jnp.float32),
                        own[h, :, lanes(down)].astype(jnp.float32),
                    ).astype(jnp.bfloat16)

                @pl.when((z == last - 1) & (down < PER_HALF))
                def _():
                    got_down[h, :, lanes(down)] = own[h, :, lanes(down)]

                @pl.when(z > 0)
                def _():
                    copy_down(down, got_down).start()

        full = t - last

        @pl.when(full >= 0)
        def _():
            h = full // PER_HALF
            here = own[h, :, lanes(full)].astype(jnp.float32)
            below = lane + full * CHUNK < low
            above = lane + full * CHUNK >= high
            value = jnp.where(below, got_up[h, :, lanes(full)].astype(jnp.float32), here)
            value = jnp.where(above, got_down[h, :, lanes(full)].astype(jnp.float32), value)
            known[h, :, lanes(full)] = value.astype(jnp.bfloat16)
            copy_x(full).start()

            @pl.when(full % PER_HALF == PER_HALF - 1)
            def _():
                for j in range(HALF):
                    blocks[h * HALF + j] = known[h, :SIDE, j * SIDE : (j + 1) * SIDE]

        @pl.when(t < HALF // 2)
        def _():
            stats(2 * t)
            stats(2 * t + 1)

    loop(0, CHUNKS + last, step)
    store(state_l, left_out, 3).start()
    store(state_r, right_out, 4).start()

    def far_half(h):
        for q in range(PER_HALF):
            copy_x(h * PER_HALF + q).wait_recv()
        for j in range(HALF):
            blocks[COLUMN + h * HALF + j] = got_x[h, :SIDE, j * SIDE : (j + 1) * SIDE]

    loop(0, 2, far_half)

    def drain(k):
        copy_x(k).wait_send()

        @pl.when((z == 1) | (z == 2) | ((z == 0) & (k < PER_HALF)))
        def _():
            copy_up(k, own).wait_send()

        @pl.when((z == 1) | (z == 2) | ((z == last) & (k >= PER_HALF)))
        def _():
            copy_down(k, own).wait_send()

    loop(0, CHUNKS, drain)
    for n, (scratch, ref) in enumerate(
        zip(
            [state_v, state_m, state_w, state_l, state_r],
            [second_out, moment_out, master_out, left_out, right_out],
        )
    ):
        store(scratch, ref, n).wait()


def apply_step(tables, fixes, grads, small, states):
    n_dp, n_grp = lax.axis_size("dp"), lax.axis_size("grp")
    state = jax.ShapeDtypeStruct(states[0].shape, jnp.float32)
    held = pltpu.VMEM((HALF, SIDE, SIDE), jnp.float32)
    line = pltpu.VMEM((2, ROWS, WIDE), jnp.bfloat16)
    return pl.pallas_call(
        step_kernel,
        out_shape=(
            *([state] * 5),
            jax.ShapeDtypeStruct((BIAS_ROWS, 128), jnp.float32),
            jax.ShapeDtypeStruct((2 * COLUMN, SIDE, SIDE), jnp.bfloat16),
        ),
        in_specs=[smem()] * 6 + [vmem()] * 2 + [hbm()] * 7,
        out_specs=[hbm()] * 5 + [vmem()] * 2,
        scratch_shapes=[
            *([held] * 7),
            pltpu.VMEM((1, SMALL_ROWS, 128), jnp.float32),
            pltpu.VMEM((n_dp - 1, SMALL_ROWS, 128), jnp.float32),
            pltpu.VMEM((n_grp, SMALL_ROWS - BIAS_ROWS, 128), jnp.float32),
            pltpu.VMEM((HALF + MOVES, SIDE, SIDE), jnp.bfloat16),
            pltpu.VMEM((ROWS, MOVE_WIDE), jnp.bfloat16),
            pltpu.VMEM((ROWS, MOVE_WIDE), jnp.bfloat16),
            *([line] * 5),
            pltpu.SemaphoreType.DMA((7,)),
            pltpu.SemaphoreType.DMA((5,)),
            pltpu.SemaphoreType.DMA((2, n_dp - 1)),
            pltpu.SemaphoreType.DMA((2, n_grp - 1)),
            pltpu.SemaphoreType.DMA((2,)),
            pltpu.SemaphoreType.DMA((6, CHUNKS)),
        ],
        compiler_params=pltpu.CompilerParams(
            collective_id=1, has_side_effects=True, vmem_limit_bytes=VMEM_LIMIT
        ),
    )(*tables, fixes, grads, small, *states)


def join_fast_kernel(cols_q, rows_q, rows_p, seen, blocks, qkv, proj):
    def band(base, stride, count):
        parts = [blocks[seen[base + k * stride]].astype(jnp.float32) for k in range(count)]
        return jnp.concatenate(parts, axis=1).astype(jnp.bfloat16)

    for c in range(cols_q):
        qkv[c] = band(c, cols_q, rows_q)
    for r in range(rows_p):
        proj[r] = band(rows_q * cols_q + r * rows_q, 1, rows_q)


def join_fast(blocks, seen, rows_q, cols_q, rows_p):
    wide = rows_q * SIDE
    return pl.pallas_call(
        lambda *refs: join_fast_kernel(cols_q, rows_q, rows_p, *refs),
        out_shape=(
            jax.ShapeDtypeStruct((cols_q, SIDE, wide), jnp.bfloat16),
            jax.ShapeDtypeStruct((rows_p, SIDE, wide), jnp.bfloat16),
        ),
        in_specs=[smem(), vmem()],
        out_specs=[vmem()] * 2,
        compiler_params=pltpu.CompilerParams(vmem_limit_bytes=32 * 1024 * 1024),
    )(seen, blocks)


def on_device(
    x_in,
    attn_in,
    grad_qkv,
    grad_out,
    owner,
    step,
    master,
    moment,
    second,
    stat_left,
    stat_right,
    root_left,
    root_right,
    qkv_bias,
    qkv_bias_m,
    qkv_bias_v,
    proj_bias,
    proj_bias_m,
    proj_bias_v,
):
    groups = lax.axis_size("dp")
    slot_count, side = master.shape[1], master.shape[2]
    if (groups, slot_count, side, owner.shape[0]) != (2 * PLANES, HALF, SIDE, 2 * COLUMN):
        return on_device_any(
            x_in, attn_in, grad_qkv, grad_out, owner, step, master, moment, second, stat_left, stat_right,
            root_left, root_right, qkv_bias, qkv_bias_m, qkv_bias_v, proj_bias, proj_bias_m, proj_bias_v,
        )
    depth = x_in.shape[0]
    tokens = depth * groups
    rows_q = D // SIDE
    cols_q = grad_qkv.shape[1] // SIDE
    rows_p = attn_in.shape[1] // SIDE
    kind_split = rows_q * cols_q
    me = lax.axis_index("dp")
    count_f = step[0].astype(jnp.float32)
    fix_one = 1.0 - jnp.power(jnp.float32(beta_one), count_f)
    fix_two = 1.0 - jnp.power(jnp.float32(beta_two), count_f)
    left_at, right_at, source, give_at, give_slot, from_slot, holds, my_blocks, seen, edges = layout_tables(
        owner, me, kind_split, cols_q, rows_q
    )
    holds = holds.astype(jnp.int32)
    kinds = (my_blocks < kind_split).astype(jnp.int32)
    left = jnp.concatenate([x_in.T.reshape(rows_q, SIDE, depth), attn_in.T.reshape(rows_p, SIDE, depth)])
    right = jnp.concatenate([grad_qkv.T.reshape(cols_q, SIDE, depth), grad_out.T.reshape(rows_q, SIDE, depth)])
    grads = reduce_tiles(left, right, left_at, right_at, source, give_at, holds, tokens)
    width_q, width_p = grad_qkv.shape[1], grad_out.shape[1]
    small = jnp.concatenate(
        [
            jnp.sum(grad_qkv, axis=0, dtype=jnp.float32),
            jnp.sum(grad_out, axis=0, dtype=jnp.float32),
            jnp.zeros((BIAS_ROWS * 128 - width_q - width_p,), jnp.float32),
        ]
    ).reshape(BIAS_ROWS, 128)
    states = (master, moment, second, stat_left, stat_right, root_left, root_right)
    fixes = fix_two.reshape(1)
    master_new, moment_new, second_new, left_new, right_new, small_sum, blocks = apply_step(
        (holds, kinds, give_slot, from_slot, edges), fixes, grads, small, states
    )
    qkv, proj = join_fast(blocks, seen, rows_q, cols_q, rows_p)
    qkv_weight = qkv.reshape(cols_q * SIDE, rows_q * SIDE).T
    proj_weight = proj.reshape(rows_p * SIDE, rows_q * SIDE)
    small_sum = small_sum.reshape(-1)
    qkv_total = small_sum[:width_q]
    proj_total = small_sum[width_q : width_q + width_p]
    qb_new, qm_new, qv_new = adamw(
        qkv_bias, qkv_bias_m, qkv_bias_v, qkv_total / tokens, fix_one, fix_two
    )
    pb_new, pm_new, pv_new = adamw(
        proj_bias, proj_bias_m, proj_bias_v, proj_total / tokens, fix_one, fix_two
    )
    return (
        master_new,
        moment_new,
        second_new,
        left_new,
        right_new,
        qkv_weight,
        proj_weight,
        qb_new,
        qm_new,
        qv_new,
        pb_new,
        pm_new,
        pv_new,
    )


def solution(mesh):
    return jax.shard_map(
        on_device,
        mesh=mesh,
        in_specs=(
            P("dp", None),
            P("dp", "grp"),
            P("dp", "grp"),
            P("dp", None),
            P(),
            P(),
            P("grp", "dp", None, None),
            P("grp", "dp", None, None),
            P("grp", "dp", None, None),
            P("grp", "dp", None, None),
            P("grp", "dp", None, None),
            P("grp", "dp", None, None),
            P("grp", "dp", None, None),
            P("grp"),
            P("grp"),
            P("grp"),
            P(),
            P(),
            P(),
        ),
        out_specs=(
            P("grp", "dp", None, None),
            P("grp", "dp", None, None),
            P("grp", "dp", None, None),
            P("grp", "dp", None, None),
            P("grp", "dp", None, None),
            P(None, "grp"),
            P("grp", None),
            P("grp"),
            P("grp"),
            P("grp"),
            P(),
            P(),
            P(),
        ),
        check_vma=False,
    )
```

```python
import jax
import jax.numpy as jnp
from jax import lax
from jax.experimental import pallas as pl
from jax.experimental.pallas import tpu as pltpu
from jax.sharding import PartitionSpec as P

D = 1600


beta_one = 0.9
beta_two = 0.95
beta_stat = 0.9
learn_rate = 0.02
weight_decay = 0.1
epsilon = 1e-08
graft_floor = 1e-06


def positions(owner, slot_count):
    total_blocks = owner.shape[0]
    blocks = jnp.arange(total_blocks, dtype=jnp.int32)
    same_owner = owner[None, :] == owner[:, None]
    earlier = blocks[None, :] < blocks[:, None]
    slot_rank = jnp.sum(jnp.where(same_owner & earlier, 1, 0).astype(jnp.int32), axis=1)
    return owner * slot_count + slot_rank


def adamw(param, first_m, second_m, grad, fix_one, fix_two):
    new_m = beta_one * first_m + (1.0 - beta_one) * grad
    new_v = beta_two * second_m + (1.0 - beta_two) * grad * grad
    new_p = param - learn_rate * (new_m / fix_one) / (jnp.sqrt(new_v / fix_two) + epsilon)
    return (new_p, new_m, new_v)


def place_kernel(
    split, cols_q, rows_q, slots, holder_ref, used_ref, left_ref, right_ref, tile_ref, peak_ref
):
    o = pl.program_id(0)
    peak_ref[...] = jnp.zeros_like(peak_ref)
    side = left_ref.shape[1]
    for s in range(slots):
        b = holder_ref[o * slots + s]

        @pl.when(used_ref[o * slots + s] > 0)
        def _():
            first = b < split
            later = jnp.maximum(b - split, 0)
            i = jnp.where(first, b // cols_q, rows_q + later // rows_q)
            j = jnp.where(first, b % cols_q, cols_q + later % rows_q)
            tile = lax.dot_general(
                left_ref[i],
                right_ref[j],
                (((1,), (1,)), ((), ())),
                preferred_element_type=jnp.float32,
            )
            tile_ref[0, :, s * side : (s + 1) * side] = tile
            peak_ref[0, s : s + 1, :] = jnp.full((1, 128), jnp.max(jnp.abs(tile)), jnp.float32)


def place_tiles(left, right, holder, used, split, cols_q, rows_q, groups, slots):
    side, depth = left.shape[1:]
    return pl.pallas_call(
        lambda *refs: place_kernel(split, cols_q, rows_q, slots, *refs),
        out_shape=(
            jax.ShapeDtypeStruct((groups, side, slots * side), jnp.float32),
            jax.ShapeDtypeStruct((groups, slots, 128), jnp.float32),
        ),
        grid_spec=pltpu.PrefetchScalarGridSpec(
            num_scalar_prefetch=2,
            grid=(groups,),
            in_specs=[
                pl.BlockSpec(left.shape, lambda o, h, u: (0, 0, 0)),
                pl.BlockSpec(right.shape, lambda o, h, u: (0, 0, 0)),
            ],
            out_specs=[
                pl.BlockSpec((1, side, slots * side), lambda o, h, u: (o, 0, 0)),
                pl.BlockSpec((1, slots, 128), lambda o, h, u: (o, 0, 0)),
            ],
        ),
        compiler_params=pltpu.CompilerParams(vmem_limit_bytes=32 * 1024 * 1024),
    )(holder, used, left, right)


def join_kernel(count, pos_ref, *refs):
    out_ref = refs[count]
    parts = [refs[k][0].astype(jnp.float32) for k in range(count)]
    out_ref[...] = jnp.concatenate(parts, axis=1).astype(out_ref.dtype)


def join_tiles(tiles, position, base, rows, cols):
    side = tiles.shape[1]

    def spot(k):
        return lambda r, pos: (pos[base + r * cols + k], 0, 0)

    return pl.pallas_call(
        lambda *refs: join_kernel(cols, *refs),
        out_shape=jax.ShapeDtypeStruct((rows * side, cols * side), tiles.dtype),
        grid_spec=pltpu.PrefetchScalarGridSpec(
            num_scalar_prefetch=1,
            grid=(rows,),
            in_specs=[pl.BlockSpec((1, side, side), spot(k)) for k in range(cols)],
            out_specs=pl.BlockSpec((side, cols * side), lambda r, pos: (r, 0)),
        ),
        compiler_params=pltpu.CompilerParams(vmem_limit_bytes=32 * 1024 * 1024),
    )(position, *([tiles] * cols))


def sum_kernel(axes, sizes, in_ref, out_ref, *scratch):
    buffers = scratch[: len(axes)]
    send_sems = scratch[len(axes) : 2 * len(axes)]
    recv_sems = scratch[2 * len(axes) :]
    barrier = pltpu.get_barrier_semaphore()
    for axis, size in zip(axes, sizes):
        me = lax.axis_index(axis)
        for k in range(1, size):
            pl.semaphore_signal(
                barrier,
                inc=1,
                device_id={axis: lax.rem(me + k, size)},
                device_id_type=pl.DeviceIdType.MESH,
            )
    pl.semaphore_wait(barrier, sum(size - 1 for size in sizes))
    value = in_ref[...]
    for n, (axis, size) in enumerate(zip(axes, sizes)):
        me = lax.axis_index(axis)
        buffers[n][me] = value
        copies = []
        for k in range(1, size):
            copy = pltpu.make_async_remote_copy(
                src_ref=buffers[n].at[me],
                dst_ref=buffers[n].at[me],
                send_sem=send_sems[n].at[k - 1],
                recv_sem=recv_sems[n].at[k - 1],
                device_id={axis: lax.rem(me + k, size)},
                device_id_type=pl.DeviceIdType.MESH,
            )
            copy.start()
            copies.append(copy)
        for copy in copies:
            copy.wait()
        value = buffers[n][0]
        for k in range(1, size):
            value = value + buffers[n][k]
    out_ref[...] = value


def sum_over(value, axes, collective_id):
    sizes = [lax.axis_size(axis) for axis in axes]
    scratch = [pltpu.VMEM((size,) + value.shape, jnp.float32) for size in sizes]
    scratch += [pltpu.SemaphoreType.DMA((size - 1,)) for size in sizes]
    scratch += [pltpu.SemaphoreType.DMA((size - 1,)) for size in sizes]
    return pl.pallas_call(
        lambda *refs: sum_kernel(axes, sizes, *refs),
        out_shape=jax.ShapeDtypeStruct(value.shape, jnp.float32),
        in_specs=[pl.BlockSpec(memory_space=pltpu.VMEM)],
        out_specs=pl.BlockSpec(memory_space=pltpu.VMEM),
        scratch_shapes=scratch,
        compiler_params=pltpu.CompilerParams(collective_id=collective_id, has_side_effects=True),
    )(value)


def on_device_any(
    x_in,
    attn_in,
    grad_qkv,
    grad_out,
    owner,
    step,
    master,
    moment,
    second,
    stat_left,
    stat_right,
    root_left,
    root_right,
    qkv_bias,
    qkv_bias_m,
    qkv_bias_v,
    proj_bias,
    proj_bias_m,
    proj_bias_v,
):
    exact = lax.Precision.HIGHEST
    groups = lax.axis_size("dp")
    own_index = lax.axis_index("dp")
    total_blocks = owner.shape[0]
    slot_count = master.shape[1]
    block_size = master.shape[2]
    tokens = x_in.shape[0] * groups
    rows_q = D // block_size
    cols_q = grad_qkv.shape[1] // block_size
    rows_p = attn_in.shape[1] // block_size
    first_kind = rows_q * cols_q
    count_f = step[0].astype(jnp.float32)
    fix_one = 1.0 - jnp.power(jnp.float32(beta_one), count_f)
    fix_two = 1.0 - jnp.power(jnp.float32(beta_two), count_f)
    blocks = jnp.arange(total_blocks, dtype=jnp.int32)
    position = positions(owner, slot_count)
    spots = groups * slot_count
    matches = position[None, :] == jnp.arange(spots, dtype=jnp.int32)[:, None]
    filled = jnp.any(matches, axis=1)
    holder = jnp.sum(jnp.where(matches, blocks[None, :], 0), axis=1)
    my_blocks = lax.dynamic_slice_in_dim(holder, own_index * slot_count, slot_count)
    my_filled = lax.dynamic_slice_in_dim(filled, own_index * slot_count, slot_count)
    filled_f = my_filled.astype(jnp.float32)
    keep = my_filled[:, None, None]

    depth = x_in.shape[0]
    left = jnp.concatenate(
        [
            x_in.T.reshape(rows_q, block_size, depth),
            attn_in.T.reshape(rows_p, block_size, depth),
        ]
    )
    right = jnp.concatenate(
        [
            grad_qkv.T.reshape(cols_q, block_size, depth),
            grad_out.T.reshape(rows_q, block_size, depth),
        ]
    )
    local_tiles, peaks = place_tiles(
        left,
        right,
        holder,
        filled.astype(jnp.int32),
        first_kind,
        cols_q,
        rows_q,
        groups,
        slot_count,
    )

    width_q, width_p = grad_qkv.shape[1], grad_out.shape[1]
    small = jnp.concatenate(
        [
            jnp.sum(grad_qkv, axis=0, dtype=jnp.float32),
            jnp.sum(grad_out, axis=0, dtype=jnp.float32),
            peaks[:, :, 0].reshape(spots),
        ]
    )
    used = small.shape[0]
    padded = -(-used // 1024) * 1024
    small = jnp.pad(small, (0, padded - used)).reshape(8, padded // 8)
    small = sum_over(small, ("dp",), 0).reshape(padded)
    qkv_total = small[:width_q]
    proj_total = small[width_q : width_q + width_p]
    bound = small[width_q + width_p : used]
    spot_bound = jnp.where(bound > 0.0, bound, 1.0).reshape(groups, 1, slot_count)
    spot_bound = jnp.repeat(spot_bound, block_size, axis=2)
    shrink = 16384.0 / spot_bound
    grow = spot_bound / 16384.0

    pair = own_index // 2
    side = own_index % 2
    pairs = groups // 2
    tiles = local_tiles

    def chunk(array, where):
        return lax.dynamic_index_in_dim(array, where, 0, keepdims=False)

    across = [(d, d ^ 1) for d in range(groups)]
    arrivals = []
    order = list(range(1, pairs))
    if pairs == 4:
        order = [1, 3, 2]
    order = order + [0]
    received = []
    for step_off in order:
        theirs = lax.rem(pair + step_off, pairs) * 2 + 1 - side
        sent = (chunk(tiles, theirs) * chunk(shrink, theirs)).astype(jnp.float16)
        received.append(lax.ppermute(sent, "dp", across))
    after = jnp.int32(0)
    for step_off, got in zip(order, received):
        ours = lax.rem(pair + step_off, pairs) * 2 + side
        both = chunk(tiles, ours + after) * chunk(shrink, ours) + got.astype(jnp.float32)
        if step_off == 0:
            mine = both
        else:
            hop = [(d, ((d // 2 + step_off) % pairs) * 2 + d % 2) for d in range(groups)]
            both = both.astype(jnp.float16)
            arrivals.append(lax.ppermute(both, "dp", hop))
            probe = arrivals[-1][0, 0].astype(jnp.float32)
            after = jnp.minimum((probe == probe).astype(jnp.int32), 0)
    for arrived in arrivals:
        mine = mine + arrived.astype(jnp.float32)
    mine = mine * (chunk(grow, own_index) / tokens)
    mine = mine.reshape(block_size, slot_count, block_size).transpose(1, 0, 2)
    grads = jnp.where(keep, mine, 0.0)
    old_w = master[0]
    old_m = moment[0]
    old_v = second[0]
    old_l = stat_left[0]
    old_r = stat_right[0]
    new_v = beta_two * old_v + (1.0 - beta_two) * grads * grads
    adam_dir = grads / (jnp.sqrt(new_v / fix_two) + epsilon)
    half = jnp.einsum("sij,sjk->sik", root_left[0], grads, precision=exact)
    shampoo_dir = jnp.einsum("sij,sjk->sik", half, root_right[0], precision=exact)
    is_qkv = my_blocks < first_kind
    adam_sq = jnp.sum(adam_dir * adam_dir, axis=(1, 2)) * filled_f
    shampoo_sq = jnp.sum(shampoo_dir * shampoo_dir, axis=(1, 2)) * filled_f
    sums = [
        jnp.sum(jnp.where(is_qkv, adam_sq, 0.0)),
        jnp.sum(jnp.where(is_qkv, 0.0, adam_sq)),
        jnp.sum(jnp.where(is_qkv, shampoo_sq, 0.0)),
        jnp.sum(jnp.where(is_qkv, 0.0, shampoo_sq)),
    ]
    lane = lax.broadcasted_iota(jnp.int32, (8, 128), 1)
    part = jnp.zeros((8, 128), jnp.float32)
    for n, value in enumerate(sums):
        part = jnp.where(lane == n, value, part)
    total = sum_over(part, ("grp", "dp"), 1)
    graft = jnp.sqrt(total[0, 0:2] / (total[0, 2:4] + graft_floor))
    block_graft = jnp.where(is_qkv, graft[0], graft[1])
    new_m = beta_one * old_m + (1.0 - beta_one) * (block_graft[:, None, None] * shampoo_dir)
    new_w = old_w - learn_rate * (new_m + weight_decay * old_w)
    new_l = beta_stat * old_l + (1.0 - beta_stat) * jnp.einsum(
        "sik,sjk->sij", grads, grads, precision=exact
    )
    new_r = beta_stat * old_r + (1.0 - beta_stat) * jnp.einsum(
        "ski,skj->sij", grads, grads, precision=exact
    )
    master_new = jnp.where(keep, new_w, old_w)
    moment_new = jnp.where(keep, new_m, old_m)
    second_new = jnp.where(keep, new_v, old_v)
    left_new = jnp.where(keep, new_l, old_l)
    right_new = jnp.where(keep, new_r, old_r)
    new_weights = master_new.astype(jnp.bfloat16)
    spread = [new_weights]
    turns = None
    if pairs == 4:
        up = [(d, d + 2) for d in range(groups - 2)]
        down = [(d + 2, d) for d in range(groups - 2)]
        from_low, from_high = [new_weights], [new_weights]
        for k in range(1, pairs):
            from_low.append(lax.ppermute(from_low[-1], "dp", up))
            from_high.append(lax.ppermute(from_high[-1], "dp", down))
        rows = []
        for z in range(pairs):
            found = [(k, 0) for k in range(1, z + 1)] + [(k, 1) for k in range(1, pairs - z)]
            rows.append(sorted(found))
        turns = [[0] * pairs for _ in range(pairs)]
        other = [lax.ppermute(new_weights, "dp", across)]
        for m in range(pairs - 1):
            value = None
            probe = other[-1][0, 0, 0].astype(jnp.float32)
            here = pair + jnp.minimum((probe == probe).astype(jnp.int32), 0)
            for z in range(pairs):
                k, way = rows[z][m]
                turns[z][z + k if way else z - k] = m + 1
                part_w = (from_low, from_high)[way][k]
                value = part_w if value is None else jnp.where(here == z, part_w, value)
            spread.append(value)
            other.append(lax.ppermute(value, "dp", across))
    else:
        for step_off in range(1, pairs):
            hop = [(d, ((d // 2 + step_off) % pairs) * 2 + d % 2) for d in range(groups)]
            spread.append(lax.ppermute(new_weights, "dp", hop))
        other = [lax.ppermute(part_w, "dp", across) for part_w in spread]
    everyone = jnp.concatenate(spread + other)
    place_owner = owner // 2
    turn = lax.rem(pair - place_owner + pairs, pairs)
    if turns is not None:
        turn = jnp.zeros_like(owner)
        for z in range(pairs):
            for origin in range(pairs):
                hit = (pair == z) & (place_owner == origin)
                turn = jnp.where(hit, turns[z][origin], turn)
    held = jnp.where(owner % 2 == side, turn, pairs + turn)
    where_held = held * slot_count + (position - owner * slot_count)
    qkv_weight = join_tiles(everyone, where_held, 0, rows_q, cols_q)
    proj_weight = join_tiles(everyone, where_held, first_kind, rows_p, rows_q)
    qb_new, qm_new, qv_new = adamw(
        qkv_bias, qkv_bias_m, qkv_bias_v, qkv_total / tokens, fix_one, fix_two
    )
    pb_new, pm_new, pv_new = adamw(
        proj_bias, proj_bias_m, proj_bias_v, proj_total / tokens, fix_one, fix_two
    )
    return (
        master_new[None],
        moment_new[None],
        second_new[None],
        left_new[None],
        right_new[None],
        qkv_weight,
        proj_weight,
        qb_new,
        qm_new,
        qv_new,
        pb_new,
        pm_new,
        pv_new,
    )


SIDE = 200
COLUMN = 32
HALF = 16
TILE = 128
HALF_TILES = HALF * SIDE // TILE
TILES = 2 * HALF_TILES
PACE = 2
CHUNKS = TILES // PACE
ROWS = 208
MOVES = 8
MOVE_TILES = -(-MOVES * SIDE // TILE)
PLANES = 4
STEPS = 8.0
TOP = 32000.0
MESH = pl.DeviceIdType.MESH
TABLE_ROWS = 16
(
    LEFT_AT,
    RIGHT_AT,
    SOURCE,
    GIVE_AT,
    GIVE_SLOT,
    FROM_SLOT,
    HOLDS,
    KINDS,
    SEEN,
    EDGES,
) = range(10)


def count_from(value, step, most):
    whole = jnp.zeros_like(value)
    for k in range(step, most, step):
        whole = whole + (value >= k).astype(jnp.int32)
    return whole


def table_kernel(cols_q, rows_q, owner_ref, out):
    me = lax.axis_index("dp")
    total, devices = 2 * COLUMN, 2 * PLANES
    split = cols_q * rows_q

    def grid(rows, columns, axis):
        return lax.broadcasted_iota(jnp.int32, (rows, columns), axis)

    def down(mask, value):
        return jnp.sum(jnp.where(mask, value, 0), axis=0, keepdims=True)

    def over(mask, value):
        return jnp.sum(jnp.where(mask, value, 0), axis=1, keepdims=True)

    def both(mask, value):
        return jnp.sum(over(mask, value), axis=0, keepdims=True)

    sub, lane = grid(total, total, 0), grid(total, total, 1)
    row = owner_ref[...]
    col = over(sub == lane, row)
    slot = over((col == row) & (lane < sub), 1)
    dev = grid(total, devices, 1)
    own = col == dev
    n = down(own, 1)
    dsub, dlane = grid(devices, devices, 0), grid(devices, devices, 1)
    here = grid(1, devices, 1)
    even = (here % 2) == 0

    def turned(value):
        return over(dsub == dlane, value)

    swap = (dsub // 2 == dlane // 2) & (dsub != dlane)
    partner = down(swap, turned(n))
    total0 = over(even, n)
    surplus = jnp.abs(total0 - COLUMN)
    crowded = (even & (total0 >= COLUMN)) | (~even & (total0 < COLUMN))
    room = jnp.where(crowded, jnp.minimum(jnp.minimum(MOVES, n), HALF - partner), 0)
    levels = grid(16, devices, 0)
    filled_to = jnp.sum(jnp.minimum(room, levels), axis=1, keepdims=True)
    fits = (filled_to <= surplus) & (grid(16, 1, 0) <= MOVES)
    level = jnp.sum(fits.astype(jnp.int32), axis=0, keepdims=True) - 1
    base = jnp.minimum(room, level)
    rest = surplus - jnp.sum(base, axis=1, keepdims=True)
    can = (room > level).astype(jnp.int32)
    before = down(dsub < dlane, turned(can))
    move = base + jnp.where((can > 0) & (before < rest), 1, 0)
    stay = n - move
    height = stay + down(swap, turned(move))
    start = down((dsub < dlane) & (dsub % 2 == dlane % 2), turned(height))
    far = down(swap, turned(start)) + partner - stay
    moved = slot >= over(own, stay)
    place = jnp.where(moved, over(own, far), over(own, start)) + slot
    parity = over(own, here % 2)
    column = jnp.where(moved, 1 - parity, parity)
    line = column * COLUMN + place
    side = me % 2
    mine = here == me
    my_n, my_stay, my_start = over(mine, n), over(mine, stay), over(mine, start)
    my_height = over(mine, height)
    spots = grid(1, total, 1)
    wanted = spots + side * COLUMN
    wanted = jnp.where(wanted >= total, wanted - total, wanted)
    at = down(line == wanted, sub)
    later = jnp.maximum(at - split, 0)
    first = at < split
    at_row, later_row = count_from(at, cols_q, split), count_from(later, rows_q, total - split)
    left_at = jnp.where(first, at_row, rows_q + later_row)
    right_at = jnp.where(first, at - at_row * cols_q, cols_q + later - later_row * rows_q)
    my_blocks = down((col == me) & (slot == lane), sub)
    source = jnp.where(spots < my_stay, my_start + spots, COLUMN + spots - my_stay)
    source = jnp.where(spots < my_n, jnp.minimum(source, COLUMN + MOVES - 1), 0)
    give_at = jnp.minimum(my_start + my_n + spots, COLUMN - 1)
    give_slot = jnp.minimum(my_stay + spots, HALF - 1)
    spot = spots - my_start
    from_slot = jnp.where(spot < my_stay, spot, jnp.where(my_n > my_stay, 0, HALF + spot - my_n))
    from_slot = jnp.minimum(jnp.maximum(from_slot, 0), HALF + MOVES - 1)
    seen = jnp.where(column == side, place, COLUMN + place)
    edges = jnp.where(spots == 0, my_start, my_start + my_height) * SIDE
    rows = {
        LEFT_AT: left_at,
        RIGHT_AT: right_at,
        SOURCE: source,
        GIVE_AT: give_at,
        GIVE_SLOT: give_slot,
        FROM_SLOT: from_slot,
        HOLDS: (spots < my_n).astype(jnp.int32),
        KINDS: (my_blocks < split).astype(jnp.int32),
        SEEN: down(sub == lane, seen),
        EDGES: edges,
    }
    out[...] = jnp.zeros_like(out)
    for n, value in rows.items():
        out[n : n + 1, :total] = value


def layout_tables(owner, cols_q, rows_q):
    return pl.pallas_call(
        lambda *refs: table_kernel(cols_q, rows_q, *refs),
        out_shape=jax.ShapeDtypeStruct((TABLE_ROWS, TILE), jnp.int32),
        in_specs=[vmem()],
        out_specs=vmem(),
    )(owner.reshape(1, -1))


def pack(value):
    top = jnp.max(jnp.abs(value), axis=1, keepdims=True)
    code = jnp.ceil(jnp.log(jnp.maximum(top, 1e-30)) * (STEPS / LN2))
    scale = TOP / jnp.exp(code * (LN2 / STEPS))
    whole = jnp.round(value * scale).astype(jnp.int32)
    codes = jnp.broadcast_to(
        code.astype(jnp.int32), (value.shape[0], ROWS - SIDE, value.shape[2])
    )
    return jnp.concatenate([whole, codes], axis=1).astype(jnp.int16)


def unpack(coded):
    wide = coded.astype(jnp.int32).astype(jnp.float32)
    scale = jnp.exp(wide[:, SIDE : SIDE + 1] * (LN2 / STEPS)) * (1.0 / TOP)
    return wide[:, :SIDE] * scale


LN2 = 0.6931471805599453


def some(k):
    return pl.ds(k * PACE, PACE)


def pieces(j):
    low, high = j * SIDE, (j + 1) * SIDE
    for tile in range(low // TILE, -(-high // TILE)):
        a, b = max(low, tile * TILE), min(high, (tile + 1) * TILE)
        yield tile, slice(a - tile * TILE, b - tile * TILE), slice(a - low, b - low)


def put(into, base, j, value):
    for tile, there, here in pieces(j):
        into[base + tile, :SIDE, there] = value[:, here]


def take(ref, base, j, into, n):
    for tile, there, here in pieces(j):
        into[n, :, here] = ref[base + tile, :SIDE, there]


def greet(peers):
    barrier = pltpu.get_barrier_semaphore()
    count = 0
    for condition, device in peers:
        if condition is None:
            pl.semaphore_signal(barrier, inc=1, device_id=device, device_id_type=MESH)
            count = count + 1
        else:

            @pl.when(condition)
            def _():
                pl.semaphore_signal(barrier, inc=1, device_id=device, device_id_type=MESH)

            count = count + condition.astype(jnp.int32)
    pl.semaphore_wait(barrier, count)


def remote(src, dst, send, recv, device):
    return pltpu.make_async_remote_copy(
        src_ref=src, dst_ref=dst, send_sem=send, recv_sem=recv, device_id=device, device_id_type=MESH
    )


def loop(low, high, body):
    lax.fori_loop(low, high, lambda k, carry: (body(k), carry)[1], 0)


def reduce_kernel(
    tokens,
    table,
    left,
    right,
    out,
    stage,
    pair,
    sent_x,
    got_x,
    sent_up,
    got_up,
    sent_down,
    got_down,
    tiles,
    stage_m,
    sent_m,
    got_m,
    sems,
    sems_m,
):
    me = lax.axis_index("dp")
    z, side = me // 2, me % 2
    across = {"dp": me + 1 - 2 * side}
    upper = {"dp": jnp.minimum(me + 2, 2 * PLANES - 1)}
    lower = {"dp": jnp.maximum(me - 2, 0)}
    last = PLANES - 1
    greet([(None, across), (z < last, upper), (z > 0, lower)])

    def copy_x(k):
        return remote(
            sent_x.at[some(k)], got_x.at[some(k)], sems.at[0, k], sems.at[1, k], across
        )

    def copy_up(k):
        return remote(
            sent_up.at[some(k)], got_up.at[some(k)], sems.at[2, k], sems.at[3, k], upper
        )

    def copy_down(k):
        return remote(
            sent_down.at[some(k)], got_down.at[some(k)], sems.at[4, k], sems.at[5, k], lower
        )

    def product(n):
        return lax.dot_general(
            left[table[LEFT_AT, n]],
            right[table[RIGHT_AT, n]],
            (((1,), (1,)), ((), ())),
            preferred_element_type=jnp.float32,
        )

    def send_other(low, high):
        def body(k):
            sent_x[some(k)] = pack(stage[some(k)])
            copy_x(k).start()

        loop(low, high, body)

    done = 0
    for h in range(2):
        for part in range(4):
            for j in range(part * 4, part * 4 + 4):
                put(stage, h * HALF_TILES, j, product(COLUMN + h * HALF + j))
            ready = (h * HALF * SIDE + (part + 1) * 4 * SIDE) // (TILE * PACE)
            send_other(done, ready)
            done = ready

    def own_half(h):
        for j in range(HALF):
            put(pair, h * HALF_TILES, j, product(h * HALF + j))

    loop(0, 2, own_half)

    def step(t):
        @pl.when(t < CHUNKS)
        def _():
            copy_x(t).wait_recv()
            pair[some(t)] += unpack(got_x[some(t)])

        up = t - z

        @pl.when((up >= 0) & (up < CHUNKS))
        def _():
            @pl.when(z == 0)
            def _():
                sent_up[some(up)] = pack(pair[some(up)])

            @pl.when(z > 0)
            def _():
                copy_up(up).wait_recv()

                @pl.when(z < last)
                def _():
                    sent_up[some(up)] = pack(pair[some(up)] + unpack(got_up[some(up)]))

            @pl.when(z < last)
            def _():
                copy_up(up).start()

        down = t - (last - z)

        @pl.when((down >= 0) & (down < CHUNKS))
        def _():
            @pl.when(z == last)
            def _():
                sent_down[some(down)] = pack(pair[some(down)])

            @pl.when(z < last)
            def _():
                copy_down(down).wait_recv()

                @pl.when(z > 0)
                def _():
                    sent_down[some(down)] = pack(pair[some(down)] + unpack(got_down[some(down)]))

            @pl.when(z > 0)
            def _():
                copy_down(down).start()

        full = t - last

        @pl.when(full >= 0)
        def _():
            @pl.when(z > 0)
            def _():
                pair[some(full)] += unpack(got_up[some(full)])

            @pl.when(z < last)
            def _():
                pair[some(full)] += unpack(got_down[some(full)])

            @pl.when((full == HALF_TILES // PACE) | (full == CHUNKS - 1))
            def _():
                h = (full == CHUNKS - 1).astype(jnp.int32)
                for j in range(HALF):
                    take(pair, h * HALF_TILES, j, tiles, h * HALF + j)

    loop(0, CHUNKS + last, step)

    stage_m[MOVE_TILES - 1] = jnp.zeros((SIDE, TILE), jnp.float32)
    for k in range(MOVES):
        put(stage_m, 0, k, tiles[table[GIVE_AT, k]])
    sent_m[...] = pack(stage_m[...])
    move = remote(sent_m, got_m, sems_m.at[0], sems_m.at[1], across)
    move.start()

    def drain(k):
        copy_x(k).wait_send()

        @pl.when(z < last)
        def _():
            copy_up(k).wait_send()

        @pl.when(z > 0)
        def _():
            copy_down(k).wait_send()

    loop(0, CHUNKS, drain)
    move.wait()
    stage_m[...] = unpack(got_m[...])
    for k in range(MOVES):
        take(stage_m, 0, k, tiles, COLUMN + k)

    def finish(s):
        out[s] = jnp.where(
            table[HOLDS, s] > 0, tiles[table[SOURCE, s]] * (1.0 / tokens), 0.0
        )

    loop(0, HALF, finish)


def vmem():
    return pl.BlockSpec(memory_space=pltpu.VMEM)


def smem():
    return pl.BlockSpec(memory_space=pltpu.SMEM)


def hbm():
    return pl.BlockSpec(memory_space=pl.ANY)


def reduce_tiles(left, right, table, tokens):
    coded = pltpu.VMEM((TILES, ROWS, TILE), jnp.int16)
    moved = pltpu.VMEM((MOVE_TILES, ROWS, TILE), jnp.int16)
    return pl.pallas_call(
        lambda *refs: reduce_kernel(tokens, *refs),
        out_shape=jax.ShapeDtypeStruct((HALF, SIDE, SIDE), jnp.float32),
        in_specs=[smem()] + [vmem()] * 2,
        out_specs=vmem(),
        scratch_shapes=[
            pltpu.VMEM((TILES, SIDE, TILE), jnp.float32),
            pltpu.VMEM((TILES, SIDE, TILE), jnp.float32),
            *([coded] * 6),
            pltpu.VMEM((COLUMN + MOVES, SIDE, SIDE), jnp.float32),
            pltpu.VMEM((MOVE_TILES, SIDE, TILE), jnp.float32),
            moved,
            moved,
            pltpu.SemaphoreType.DMA((6, CHUNKS)),
            pltpu.SemaphoreType.DMA((2,)),
        ],
        compiler_params=pltpu.CompilerParams(
            collective_id=0, has_side_effects=True, vmem_limit_bytes=VMEM_LIMIT
        ),
    )(table, left, right)


VMEM_LIMIT = 60 * 1024 * 1024
EARLY = 10
SMALL_ROWS = 32
BIAS_ROWS = 24


def dot3(a, b, dims):
    a_high, b_high = a.astype(jnp.bfloat16), b.astype(jnp.bfloat16)
    a_low = (a - a_high.astype(jnp.float32)).astype(jnp.bfloat16)
    b_low = (b - b_high.astype(jnp.float32)).astype(jnp.bfloat16)

    def dot(p, q):
        return lax.dot_general(p, q, (dims, ((), ())), preferred_element_type=jnp.float32)

    return dot(a_high, b_high) + (dot(a_high, b_low) + dot(a_low, b_high))


def step_kernel(
    table,
    fixes,
    grads,
    small,
    master,
    moment,
    second,
    stat_left,
    stat_right,
    root_left,
    root_right,
    master_out,
    moment_out,
    second_out,
    left_out,
    right_out,
    small_out,
    blocks_out,
    state_w,
    state_m,
    state_v,
    state_l,
    state_r,
    state_a,
    state_b,
    sums,
    sums_dp,
    sums_grp,
    light,
    sent_m,
    got_m,
    own,
    got_up,
    got_down,
    known,
    got_x,
    blocks,
    block_sems,
    load_sems,
    store_sems,
    sum_sems,
    grp_sems,
    move_sems,
    sems,
):
    me = lax.axis_index("dp")
    z, side = me // 2, me % 2
    n_dp, n_grp = lax.axis_size("dp"), lax.axis_size("grp")
    my_grp = lax.axis_index("grp")
    across = {"dp": me + 1 - 2 * side}
    upper = {"dp": jnp.minimum(me + 2, 2 * PLANES - 1)}
    lower = {"dp": jnp.maximum(me - 2, 0)}
    last = PLANES - 1
    held = [state_v, state_a, state_b, state_w, state_m, state_l, state_r]
    given = [second, root_left, root_right, master, moment, stat_left, stat_right]
    loads = []
    for n, (ref, scratch) in enumerate(zip(given, held)):
        copy = pltpu.make_async_copy(ref.at[0], scratch, load_sems.at[n])
        copy.start()
        loads.append(copy)

    def store(scratch, ref, n):
        return pltpu.make_async_copy(scratch, ref.at[0], store_sems.at[n])

    peers = [(None, {"dp": lax.rem(me + k, n_dp)}) for k in range(1, n_dp)]
    peers += [(None, {"grp": lax.rem(my_grp + k, n_grp)}) for k in range(1, n_grp)]
    greet(peers)

    fix_two = fixes[0]
    for copy in loads[:3]:
        copy.wait()

    def direction(s, sums_now):
        adam_q, adam_p, shampoo_q, shampoo_p = sums_now
        grad = grads[s]
        old = state_v[s]
        new = beta_two * old + (1.0 - beta_two) * grad * grad
        adam = grad / (jnp.sqrt(new / fix_two) + epsilon)
        half = dot3(state_a[s], grad, ((1,), (0,)))
        shampoo = dot3(half, state_b[s], ((1,), (0,)))
        state_v[s] = jnp.where(table[HOLDS, s] > 0, new, old)
        state_a[s] = shampoo
        adam_sq = jnp.sum(adam * adam, axis=0, keepdims=True)
        shampoo_sq = jnp.sum(shampoo * shampoo, axis=0, keepdims=True)
        q = table[KINDS, s] > 0
        return (
            adam_q + jnp.where(q, adam_sq, 0.0),
            adam_p + jnp.where(q, 0.0, adam_sq),
            shampoo_q + jnp.where(q, shampoo_sq, 0.0),
            shampoo_p + jnp.where(q, 0.0, shampoo_sq),
        )

    nothing = jnp.zeros((1, SIDE), jnp.float32)
    parts = lax.fori_loop(0, HALF, direction, (nothing,) * 4, unroll=4)
    store(state_v, second_out, 0).start()
    sums[0, :BIAS_ROWS] = small[...]
    row = lax.broadcasted_iota(jnp.int32, (SMALL_ROWS - BIAS_ROWS, 128), 0)
    packed = jnp.zeros((SMALL_ROWS - BIAS_ROWS, 128), jnp.float32)
    for n, part in enumerate(parts):
        packed = jnp.where(row == n, jnp.sum(part), packed)
    sums[0, BIAS_ROWS:] = packed

    copies = []
    for k in range(1, n_dp):
        copy = remote(
            sums.at[0], sums_dp.at[k - 1], sum_sems.at[0, k - 1], sum_sems.at[1, k - 1],
            {"dp": lax.rem(me + k, n_dp)},
        )
        copy.start()
        copies.append(copy)
    for copy in loads[3:5]:
        copy.wait()
    for copy in copies:
        copy.wait()
    for d in range(n_dp):
        value = jnp.where(me == d, sums[0], sums_dp[lax.rem(me - d + n_dp + n_dp - 1, n_dp) % (n_dp - 1)])
        total = value if d == 0 else total + value
    small_out[...] = total[:BIAS_ROWS]
    sums_grp[my_grp] = total[BIAS_ROWS:]
    copies = []
    for k in range(1, n_grp):
        copy = remote(
            sums_grp.at[my_grp], sums_grp.at[my_grp], grp_sems.at[0, k - 1], grp_sems.at[1, k - 1],
            {"grp": lax.rem(my_grp + k, n_grp)},
        )
        copy.start()
        copies.append(copy)
    for copy in copies:
        copy.wait()
    total = sums_grp[0]
    for g in range(1, n_grp):
        total = total + sums_grp[g]
    graft_q = jnp.sqrt(total[0:1] / (total[2:3] + graft_floor))[:, :1]
    graft_p = jnp.sqrt(total[1:2] / (total[3:4] + graft_floor))[:, :1]

    def update(s):
        graft = jnp.where(table[KINDS, s] > 0, graft_q, graft_p)
        old_m, old_w = state_m[s], state_w[s]
        new_m = beta_one * old_m + (1.0 - beta_one) * (graft * state_a[s])
        new_w = old_w - learn_rate * (new_m + weight_decay * old_w)
        state_m[s] = jnp.where(table[HOLDS, s] > 0, new_m, old_m)
        state_w[s] = jnp.where(table[HOLDS, s] > 0, new_w, old_w)
        light[s] = jnp.where(table[KINDS, s] > 0, new_w.T, new_w).astype(jnp.bfloat16)

    loop(0, HALF, update)
    store(state_m, moment_out, 1).start()
    store(state_w, master_out, 2).start()

    sent_m[...] = jnp.zeros_like(sent_m)
    for k in range(MOVES):
        put(sent_m, 0, k, light[table[GIVE_SLOT, k]])
    move = remote(sent_m, got_m, move_sems.at[0], move_sems.at[1], across)
    move.start()

    for copy in loads[5:7]:
        copy.wait()

    def stats(s):
        grad = grads[s]
        keep = table[HOLDS, s] > 0
        new_l = beta_stat * state_l[s] + (1.0 - beta_stat) * dot3(grad, grad, ((1,), (1,)))
        new_r = beta_stat * state_r[s] + (1.0 - beta_stat) * dot3(grad, grad, ((0,), (0,)))
        state_l[s] = jnp.where(keep, new_l, state_l[s])
        state_r[s] = jnp.where(keep, new_r, state_r[s])

    loop(0, EARLY, stats)
    move.wait()
    for k in range(MOVES):
        take(got_m, 0, k, light, HALF + k)

    def fill(h):
        for j in range(HALF):
            put(own, h * HALF_TILES, j, light[table[FROM_SLOT, h * HALF + j]])

    def pad(k):
        own[k, SIDE:] = jnp.zeros((ROWS - SIDE, TILE), jnp.bfloat16)

    loop(0, TILES, pad)
    loop(0, 2, fill)

    low, high = table[EDGES, 0], table[EDGES, 1]
    shape = (PACE, ROWS, TILE)
    lane = lax.broadcasted_iota(jnp.int32, shape, 0) * TILE + lax.broadcasted_iota(
        jnp.int32, shape, 2
    )
    up_window = -(-HALF_TILES // PACE)
    down_window = HALF_TILES // PACE

    def wide(ref, k):
        return ref[some(k)].astype(jnp.float32)

    def copy_up(k, src):
        return remote(src.at[some(k)], got_up.at[some(k)], sems.at[0, k], sems.at[1, k], upper)

    def copy_down(k, src):
        return remote(src.at[some(k)], got_down.at[some(k)], sems.at[2, k], sems.at[3, k], lower)

    def copy_x(k):
        return remote(known.at[some(k)], got_x.at[some(k)], sems.at[4, k], sems.at[5, k], across)

    def keep_half(h):
        return pltpu.make_async_copy(
            blocks.at[pl.ds(h * HALF, HALF)], blocks_out.at[pl.ds(h * HALF, HALF)], block_sems.at[h]
        )

    def step(t):
        up = t - z

        @pl.when((up >= 0) & (up < CHUNKS))
        def _():
            @pl.when((z == 0) & (up < up_window))
            def _():
                copy_up(up, own).start()

            @pl.when(z > 0)
            def _():
                @pl.when((z > 1) | (up < up_window))
                def _():
                    copy_up(up, own).wait_recv()
                    mask = lane + up * (PACE * TILE) < low
                    got_up[some(up)] = jnp.where(mask, wide(got_up, up), wide(own, up)).astype(
                        jnp.bfloat16
                    )

                @pl.when((z == 1) & (up >= up_window))
                def _():
                    got_up[some(up)] = own[some(up)]

                @pl.when(z < last)
                def _():
                    copy_up(up, got_up).start()

        down = t - (last - z)

        @pl.when((down >= 0) & (down < CHUNKS))
        def _():
            @pl.when((z == last) & (down >= down_window))
            def _():
                copy_down(down, own).start()

            @pl.when(z < last)
            def _():
                @pl.when((z < last - 1) | (down >= down_window))
                def _():
                    copy_down(down, own).wait_recv()
                    mask = lane + down * (PACE * TILE) >= high
                    got_down[some(down)] = jnp.where(
                        mask, wide(got_down, down), wide(own, down)
                    ).astype(jnp.bfloat16)

                @pl.when((z == last - 1) & (down < down_window))
                def _():
                    got_down[some(down)] = own[some(down)]

                @pl.when(z > 0)
                def _():
                    copy_down(down, got_down).start()

        full = t - last

        @pl.when(full >= 0)
        def _():
            place = lane + full * (PACE * TILE)
            value = jnp.where(place < low, wide(got_up, full), wide(own, full))
            value = jnp.where(place >= high, wide(got_down, full), value)
            known[some(full)] = value.astype(jnp.bfloat16)
            copy_x(full).start()

            @pl.when((full == HALF_TILES // PACE) | (full == CHUNKS - 1))
            def _():
                h = (full == CHUNKS - 1).astype(jnp.int32)
                for j in range(HALF):
                    take(known, h * HALF_TILES, j, blocks, h * HALF + j)
                keep_half(h).start()

        @pl.when(t < HALF - EARLY)
        def _():
            stats(EARLY + t)

    loop(0, CHUNKS + last, step)
    store(state_l, left_out, 3).start()
    store(state_r, right_out, 4).start()
    for h in range(2):
        loop(0 if h == 0 else up_window, up_window if h == 0 else CHUNKS, lambda k: copy_x(k).wait_recv())
        for j in range(HALF):
            take(got_x, h * HALF_TILES, j, blocks, COLUMN + h * HALF + j)
        keep_half(2 + h).start()

    def drain(k):
        copy_x(k).wait_send()

        @pl.when((z == 1) | (z == 2) | ((z == 0) & (k < up_window)))
        def _():
            copy_up(k, own).wait_send()

        @pl.when((z == 1) | (z == 2) | ((z == last) & (k >= down_window)))
        def _():
            copy_down(k, own).wait_send()

    loop(0, CHUNKS, drain)
    for n, (scratch, ref) in enumerate(
        zip(
            [state_v, state_m, state_w, state_l, state_r],
            [second_out, moment_out, master_out, left_out, right_out],
        )
    ):
        store(scratch, ref, n).wait()
    for h in range(4):
        keep_half(h).wait()


def apply_step(table, fixes, grads, small, states):
    n_dp, n_grp = lax.axis_size("dp"), lax.axis_size("grp")
    state = jax.ShapeDtypeStruct(states[0].shape, jnp.float32)
    held = pltpu.VMEM((HALF, SIDE, SIDE), jnp.float32)
    line = pltpu.VMEM((TILES, ROWS, TILE), jnp.bfloat16)
    moved = pltpu.VMEM((MOVE_TILES, ROWS, TILE), jnp.bfloat16)
    return pl.pallas_call(
        step_kernel,
        out_shape=(
            *([state] * 5),
            jax.ShapeDtypeStruct((BIAS_ROWS, 128), jnp.float32),
            jax.ShapeDtypeStruct((2 * COLUMN, SIDE, SIDE), jnp.bfloat16),
        ),
        in_specs=[smem()] * 2 + [vmem()] * 2 + [hbm()] * 7,
        out_specs=[hbm()] * 5 + [vmem(), hbm()],
        scratch_shapes=[
            *([held] * 7),
            pltpu.VMEM((1, SMALL_ROWS, 128), jnp.float32),
            pltpu.VMEM((n_dp - 1, SMALL_ROWS, 128), jnp.float32),
            pltpu.VMEM((n_grp, SMALL_ROWS - BIAS_ROWS, 128), jnp.float32),
            pltpu.VMEM((HALF + MOVES, SIDE, SIDE), jnp.bfloat16),
            moved,
            moved,
            *([line] * 5),
            pltpu.VMEM((2 * COLUMN, SIDE, SIDE), jnp.bfloat16),
            pltpu.SemaphoreType.DMA((4,)),
            pltpu.SemaphoreType.DMA((7,)),
            pltpu.SemaphoreType.DMA((5,)),
            pltpu.SemaphoreType.DMA((2, n_dp - 1)),
            pltpu.SemaphoreType.DMA((2, n_grp - 1)),
            pltpu.SemaphoreType.DMA((2,)),
            pltpu.SemaphoreType.DMA((6, CHUNKS)),
        ],
        compiler_params=pltpu.CompilerParams(
            collective_id=1, has_side_effects=True, vmem_limit_bytes=VMEM_LIMIT
        ),
    )(table, fixes, grads, small, *states)


def finish_kernel(cols_q, rows_q, rows_p, table, blocks, *refs):
    given, kept = refs[:5], refs[5:10]
    qkv, proj, held, bands, copy_sems, held_sem, band_sems = refs[10:]
    load = pltpu.make_async_copy(blocks, held, held_sem)
    load.start()
    copies = [
        pltpu.make_async_copy(a, b, copy_sems.at[n]) for n, (a, b) in enumerate(zip(given, kept))
    ]
    for copy in copies:
        copy.start()
    load.wait()
    stores = []
    for n in range(cols_q + rows_p):
        first, stride = (n, cols_q) if n < cols_q else (cols_q * rows_q + (n - cols_q) * rows_q, 1)
        parts = [
            held[table[SEEN, first + k * stride]].astype(jnp.float32) for k in range(rows_q)
        ]
        bands[n] = jnp.concatenate(parts, axis=1).astype(jnp.bfloat16)
        into = qkv.at[n] if n < cols_q else proj.at[n - cols_q]
        stores.append(pltpu.make_async_copy(bands.at[n], into, band_sems.at[n]))
        stores[-1].start()
    for copy in stores + copies:
        copy.wait()


def finish(blocks, table, states, rows_q, cols_q, rows_p):
    across = rows_q * SIDE
    state = jax.ShapeDtypeStruct(states[0].shape, jnp.float32)
    return pl.pallas_call(
        lambda *refs: finish_kernel(cols_q, rows_q, rows_p, *refs),
        out_shape=(
            *([state] * 5),
            jax.ShapeDtypeStruct((cols_q, SIDE, across), jnp.bfloat16),
            jax.ShapeDtypeStruct((rows_p, SIDE, across), jnp.bfloat16),
        ),
        in_specs=[smem()] + [hbm()] * 6,
        out_specs=[hbm()] * 7,
        scratch_shapes=[
            pltpu.VMEM(blocks.shape, jnp.bfloat16),
            pltpu.VMEM((cols_q + rows_p, SIDE, across), jnp.bfloat16),
            pltpu.SemaphoreType.DMA((5,)),
            pltpu.SemaphoreType.DMA,
            pltpu.SemaphoreType.DMA((cols_q + rows_p,)),
        ],
        compiler_params=pltpu.CompilerParams(vmem_limit_bytes=VMEM_LIMIT),
    )(table, blocks, *states)


def on_device(
    x_in,
    attn_in,
    grad_qkv,
    grad_out,
    owner,
    step,
    master,
    moment,
    second,
    stat_left,
    stat_right,
    root_left,
    root_right,
    qkv_bias,
    qkv_bias_m,
    qkv_bias_v,
    proj_bias,
    proj_bias_m,
    proj_bias_v,
):
    groups = lax.axis_size("dp")
    slot_count, side = master.shape[1], master.shape[2]
    if (groups, slot_count, side, owner.shape[0]) != (2 * PLANES, HALF, SIDE, 2 * COLUMN):
        return on_device_any(
            x_in, attn_in, grad_qkv, grad_out, owner, step, master, moment, second, stat_left, stat_right,
            root_left, root_right, qkv_bias, qkv_bias_m, qkv_bias_v, proj_bias, proj_bias_m, proj_bias_v,
        )
    depth = x_in.shape[0]
    tokens = depth * groups
    rows_q = D // SIDE
    cols_q = grad_qkv.shape[1] // SIDE
    rows_p = attn_in.shape[1] // SIDE
    count_f = step[0].astype(jnp.float32)
    fix_one = 1.0 - jnp.power(jnp.float32(beta_one), count_f)
    fix_two = 1.0 - jnp.power(jnp.float32(beta_two), count_f)
    table = layout_tables(owner, cols_q, rows_q)
    left = jnp.concatenate([x_in.T.reshape(rows_q, SIDE, depth), attn_in.T.reshape(rows_p, SIDE, depth)])
    right = jnp.concatenate([grad_qkv.T.reshape(cols_q, SIDE, depth), grad_out.T.reshape(rows_q, SIDE, depth)])
    grads = reduce_tiles(left, right, table, tokens)
    width_q, width_p = grad_qkv.shape[1], grad_out.shape[1]
    small = jnp.concatenate(
        [
            jnp.sum(grad_qkv, axis=0, dtype=jnp.float32),
            jnp.sum(grad_out, axis=0, dtype=jnp.float32),
            jnp.zeros((BIAS_ROWS * 128 - width_q - width_p,), jnp.float32),
        ]
    ).reshape(BIAS_ROWS, 128)
    states = (master, moment, second, stat_left, stat_right, root_left, root_right)
    fixes = fix_two.reshape(1)
    *stepped, small_sum, blocks = apply_step(table, fixes, grads, small, states)
    *stepped, qkv, proj = finish(blocks, table, stepped, rows_q, cols_q, rows_p)
    master_new, moment_new, second_new, left_new, right_new = stepped
    qkv_weight = qkv.reshape(cols_q * SIDE, rows_q * SIDE).T
    proj_weight = proj.reshape(rows_p * SIDE, rows_q * SIDE)
    small_sum = small_sum.reshape(-1)
    qkv_total = small_sum[:width_q]
    proj_total = small_sum[width_q : width_q + width_p]
    qb_new, qm_new, qv_new = adamw(
        qkv_bias, qkv_bias_m, qkv_bias_v, qkv_total / tokens, fix_one, fix_two
    )
    pb_new, pm_new, pv_new = adamw(
        proj_bias, proj_bias_m, proj_bias_v, proj_total / tokens, fix_one, fix_two
    )
    return (
        master_new,
        moment_new,
        second_new,
        left_new,
        right_new,
        qkv_weight,
        proj_weight,
        qb_new,
        qm_new,
        qv_new,
        pb_new,
        pm_new,
        pv_new,
    )


def solution(mesh):
    return jax.shard_map(
        on_device,
        mesh=mesh,
        in_specs=(
            P("dp", None),
            P("dp", "grp"),
            P("dp", "grp"),
            P("dp", None),
            P(),
            P(),
            P("grp", "dp", None, None),
            P("grp", "dp", None, None),
            P("grp", "dp", None, None),
            P("grp", "dp", None, None),
            P("grp", "dp", None, None),
            P("grp", "dp", None, None),
            P("grp", "dp", None, None),
            P("grp"),
            P("grp"),
            P("grp"),
            P(),
            P(),
            P(),
        ),
        out_specs=(
            P("grp", "dp", None, None),
            P("grp", "dp", None, None),
            P("grp", "dp", None, None),
            P("grp", "dp", None, None),
            P("grp", "dp", None, None),
            P(None, "grp"),
            P("grp", None),
            P("grp"),
            P("grp"),
            P("grp"),
            P(),
            P(),
            P(),
        ),
        check_vma=False,
    )
```

```python
import jax
import jax.numpy as jnp
from jax import lax
from jax.experimental import pallas as pl
from jax.experimental.pallas import tpu as pltpu
from jax.sharding import PartitionSpec as P

D = 1600


beta_one = 0.9
beta_two = 0.95
beta_stat = 0.9
learn_rate = 0.02
weight_decay = 0.1
epsilon = 1e-08
graft_floor = 1e-06


def positions(owner, slot_count):
    total_blocks = owner.shape[0]
    blocks = jnp.arange(total_blocks, dtype=jnp.int32)
    same_owner = owner[None, :] == owner[:, None]
    earlier = blocks[None, :] < blocks[:, None]
    slot_rank = jnp.sum(jnp.where(same_owner & earlier, 1, 0).astype(jnp.int32), axis=1)
    return owner * slot_count + slot_rank


def adamw(param, first_m, second_m, grad, fix_one, fix_two):
    new_m = beta_one * first_m + (1.0 - beta_one) * grad
    new_v = beta_two * second_m + (1.0 - beta_two) * grad * grad
    new_p = param - learn_rate * (new_m / fix_one) / (jnp.sqrt(new_v / fix_two) + epsilon)
    return (new_p, new_m, new_v)


def place_kernel(
    split, cols_q, rows_q, slots, holder_ref, used_ref, left_ref, right_ref, tile_ref, peak_ref
):
    o = pl.program_id(0)
    peak_ref[...] = jnp.zeros_like(peak_ref)
    side = left_ref.shape[1]
    for s in range(slots):
        b = holder_ref[o * slots + s]

        @pl.when(used_ref[o * slots + s] > 0)
        def _():
            first = b < split
            later = jnp.maximum(b - split, 0)
            i = jnp.where(first, b // cols_q, rows_q + later // rows_q)
            j = jnp.where(first, b % cols_q, cols_q + later % rows_q)
            tile = lax.dot_general(
                left_ref[i],
                right_ref[j],
                (((1,), (1,)), ((), ())),
                preferred_element_type=jnp.float32,
            )
            tile_ref[0, :, s * side : (s + 1) * side] = tile
            peak_ref[0, s : s + 1, :] = jnp.full((1, 128), jnp.max(jnp.abs(tile)), jnp.float32)


def place_tiles(left, right, holder, used, split, cols_q, rows_q, groups, slots):
    side, depth = left.shape[1:]
    return pl.pallas_call(
        lambda *refs: place_kernel(split, cols_q, rows_q, slots, *refs),
        out_shape=(
            jax.ShapeDtypeStruct((groups, side, slots * side), jnp.float32),
            jax.ShapeDtypeStruct((groups, slots, 128), jnp.float32),
        ),
        grid_spec=pltpu.PrefetchScalarGridSpec(
            num_scalar_prefetch=2,
            grid=(groups,),
            in_specs=[
                pl.BlockSpec(left.shape, lambda o, h, u: (0, 0, 0)),
                pl.BlockSpec(right.shape, lambda o, h, u: (0, 0, 0)),
            ],
            out_specs=[
                pl.BlockSpec((1, side, slots * side), lambda o, h, u: (o, 0, 0)),
                pl.BlockSpec((1, slots, 128), lambda o, h, u: (o, 0, 0)),
            ],
        ),
        compiler_params=pltpu.CompilerParams(vmem_limit_bytes=32 * 1024 * 1024),
    )(holder, used, left, right)


def join_kernel(count, pos_ref, *refs):
    out_ref = refs[count]
    parts = [refs[k][0].astype(jnp.float32) for k in range(count)]
    out_ref[...] = jnp.concatenate(parts, axis=1).astype(out_ref.dtype)


def join_tiles(tiles, position, base, rows, cols):
    side = tiles.shape[1]

    def spot(k):
        return lambda r, pos: (pos[base + r * cols + k], 0, 0)

    return pl.pallas_call(
        lambda *refs: join_kernel(cols, *refs),
        out_shape=jax.ShapeDtypeStruct((rows * side, cols * side), tiles.dtype),
        grid_spec=pltpu.PrefetchScalarGridSpec(
            num_scalar_prefetch=1,
            grid=(rows,),
            in_specs=[pl.BlockSpec((1, side, side), spot(k)) for k in range(cols)],
            out_specs=pl.BlockSpec((side, cols * side), lambda r, pos: (r, 0)),
        ),
        compiler_params=pltpu.CompilerParams(vmem_limit_bytes=32 * 1024 * 1024),
    )(position, *([tiles] * cols))


def sum_kernel(axes, sizes, in_ref, out_ref, *scratch):
    buffers = scratch[: len(axes)]
    send_sems = scratch[len(axes) : 2 * len(axes)]
    recv_sems = scratch[2 * len(axes) :]
    barrier = pltpu.get_barrier_semaphore()
    for axis, size in zip(axes, sizes):
        me = lax.axis_index(axis)
        for k in range(1, size):
            pl.semaphore_signal(
                barrier,
                inc=1,
                device_id={axis: lax.rem(me + k, size)},
                device_id_type=pl.DeviceIdType.MESH,
            )
    pl.semaphore_wait(barrier, sum(size - 1 for size in sizes))
    value = in_ref[...]
    for n, (axis, size) in enumerate(zip(axes, sizes)):
        me = lax.axis_index(axis)
        buffers[n][me] = value
        copies = []
        for k in range(1, size):
            copy = pltpu.make_async_remote_copy(
                src_ref=buffers[n].at[me],
                dst_ref=buffers[n].at[me],
                send_sem=send_sems[n].at[k - 1],
                recv_sem=recv_sems[n].at[k - 1],
                device_id={axis: lax.rem(me + k, size)},
                device_id_type=pl.DeviceIdType.MESH,
            )
            copy.start()
            copies.append(copy)
        for copy in copies:
            copy.wait()
        value = buffers[n][0]
        for k in range(1, size):
            value = value + buffers[n][k]
    out_ref[...] = value


def sum_over(value, axes, collective_id):
    sizes = [lax.axis_size(axis) for axis in axes]
    scratch = [pltpu.VMEM((size,) + value.shape, jnp.float32) for size in sizes]
    scratch += [pltpu.SemaphoreType.DMA((size - 1,)) for size in sizes]
    scratch += [pltpu.SemaphoreType.DMA((size - 1,)) for size in sizes]
    return pl.pallas_call(
        lambda *refs: sum_kernel(axes, sizes, *refs),
        out_shape=jax.ShapeDtypeStruct(value.shape, jnp.float32),
        in_specs=[pl.BlockSpec(memory_space=pltpu.VMEM)],
        out_specs=pl.BlockSpec(memory_space=pltpu.VMEM),
        scratch_shapes=scratch,
        compiler_params=pltpu.CompilerParams(collective_id=collective_id, has_side_effects=True),
    )(value)


def on_device_any(
    x_in,
    attn_in,
    grad_qkv,
    grad_out,
    owner,
    step,
    master,
    moment,
    second,
    stat_left,
    stat_right,
    root_left,
    root_right,
    qkv_bias,
    qkv_bias_m,
    qkv_bias_v,
    proj_bias,
    proj_bias_m,
    proj_bias_v,
):
    exact = lax.Precision.HIGHEST
    groups = lax.axis_size("dp")
    own_index = lax.axis_index("dp")
    total_blocks = owner.shape[0]
    slot_count = master.shape[1]
    block_size = master.shape[2]
    tokens = x_in.shape[0] * groups
    rows_q = D // block_size
    cols_q = grad_qkv.shape[1] // block_size
    rows_p = attn_in.shape[1] // block_size
    first_kind = rows_q * cols_q
    count_f = step[0].astype(jnp.float32)
    fix_one = 1.0 - jnp.power(jnp.float32(beta_one), count_f)
    fix_two = 1.0 - jnp.power(jnp.float32(beta_two), count_f)
    blocks = jnp.arange(total_blocks, dtype=jnp.int32)
    position = positions(owner, slot_count)
    spots = groups * slot_count
    matches = position[None, :] == jnp.arange(spots, dtype=jnp.int32)[:, None]
    filled = jnp.any(matches, axis=1)
    holder = jnp.sum(jnp.where(matches, blocks[None, :], 0), axis=1)
    my_blocks = lax.dynamic_slice_in_dim(holder, own_index * slot_count, slot_count)
    my_filled = lax.dynamic_slice_in_dim(filled, own_index * slot_count, slot_count)
    filled_f = my_filled.astype(jnp.float32)
    keep = my_filled[:, None, None]

    depth = x_in.shape[0]
    left = jnp.concatenate(
        [
            x_in.T.reshape(rows_q, block_size, depth),
            attn_in.T.reshape(rows_p, block_size, depth),
        ]
    )
    right = jnp.concatenate(
        [
            grad_qkv.T.reshape(cols_q, block_size, depth),
            grad_out.T.reshape(rows_q, block_size, depth),
        ]
    )
    local_tiles, peaks = place_tiles(
        left,
        right,
        holder,
        filled.astype(jnp.int32),
        first_kind,
        cols_q,
        rows_q,
        groups,
        slot_count,
    )

    width_q, width_p = grad_qkv.shape[1], grad_out.shape[1]
    small = jnp.concatenate(
        [
            jnp.sum(grad_qkv, axis=0, dtype=jnp.float32),
            jnp.sum(grad_out, axis=0, dtype=jnp.float32),
            peaks[:, :, 0].reshape(spots),
        ]
    )
    used = small.shape[0]
    padded = -(-used // 1024) * 1024
    small = jnp.pad(small, (0, padded - used)).reshape(8, padded // 8)
    small = sum_over(small, ("dp",), 0).reshape(padded)
    qkv_total = small[:width_q]
    proj_total = small[width_q : width_q + width_p]
    bound = small[width_q + width_p : used]
    spot_bound = jnp.where(bound > 0.0, bound, 1.0).reshape(groups, 1, slot_count)
    spot_bound = jnp.repeat(spot_bound, block_size, axis=2)
    shrink = 16384.0 / spot_bound
    grow = spot_bound / 16384.0

    pair = own_index // 2
    side = own_index % 2
    pairs = groups // 2
    tiles = local_tiles

    def chunk(array, where):
        return lax.dynamic_index_in_dim(array, where, 0, keepdims=False)

    across = [(d, d ^ 1) for d in range(groups)]
    arrivals = []
    order = list(range(1, pairs))
    if pairs == 4:
        order = [1, 3, 2]
    order = order + [0]
    received = []
    for step_off in order:
        theirs = lax.rem(pair + step_off, pairs) * 2 + 1 - side
        sent = (chunk(tiles, theirs) * chunk(shrink, theirs)).astype(jnp.float16)
        received.append(lax.ppermute(sent, "dp", across))
    after = jnp.int32(0)
    for step_off, got in zip(order, received):
        ours = lax.rem(pair + step_off, pairs) * 2 + side
        both = chunk(tiles, ours + after) * chunk(shrink, ours) + got.astype(jnp.float32)
        if step_off == 0:
            mine = both
        else:
            hop = [(d, ((d // 2 + step_off) % pairs) * 2 + d % 2) for d in range(groups)]
            both = both.astype(jnp.float16)
            arrivals.append(lax.ppermute(both, "dp", hop))
            probe = arrivals[-1][0, 0].astype(jnp.float32)
            after = jnp.minimum((probe == probe).astype(jnp.int32), 0)
    for arrived in arrivals:
        mine = mine + arrived.astype(jnp.float32)
    mine = mine * (chunk(grow, own_index) / tokens)
    mine = mine.reshape(block_size, slot_count, block_size).transpose(1, 0, 2)
    grads = jnp.where(keep, mine, 0.0)
    old_w = master[0]
    old_m = moment[0]
    old_v = second[0]
    old_l = stat_left[0]
    old_r = stat_right[0]
    new_v = beta_two * old_v + (1.0 - beta_two) * grads * grads
    adam_dir = grads / (jnp.sqrt(new_v / fix_two) + epsilon)
    half = jnp.einsum("sij,sjk->sik", root_left[0], grads, precision=exact)
    shampoo_dir = jnp.einsum("sij,sjk->sik", half, root_right[0], precision=exact)
    is_qkv = my_blocks < first_kind
    adam_sq = jnp.sum(adam_dir * adam_dir, axis=(1, 2)) * filled_f
    shampoo_sq = jnp.sum(shampoo_dir * shampoo_dir, axis=(1, 2)) * filled_f
    sums = [
        jnp.sum(jnp.where(is_qkv, adam_sq, 0.0)),
        jnp.sum(jnp.where(is_qkv, 0.0, adam_sq)),
        jnp.sum(jnp.where(is_qkv, shampoo_sq, 0.0)),
        jnp.sum(jnp.where(is_qkv, 0.0, shampoo_sq)),
    ]
    lane = lax.broadcasted_iota(jnp.int32, (8, 128), 1)
    part = jnp.zeros((8, 128), jnp.float32)
    for n, value in enumerate(sums):
        part = jnp.where(lane == n, value, part)
    total = sum_over(part, ("grp", "dp"), 1)
    graft = jnp.sqrt(total[0, 0:2] / (total[0, 2:4] + graft_floor))
    block_graft = jnp.where(is_qkv, graft[0], graft[1])
    new_m = beta_one * old_m + (1.0 - beta_one) * (block_graft[:, None, None] * shampoo_dir)
    new_w = old_w - learn_rate * (new_m + weight_decay * old_w)
    new_l = beta_stat * old_l + (1.0 - beta_stat) * jnp.einsum(
        "sik,sjk->sij", grads, grads, precision=exact
    )
    new_r = beta_stat * old_r + (1.0 - beta_stat) * jnp.einsum(
        "ski,skj->sij", grads, grads, precision=exact
    )
    master_new = jnp.where(keep, new_w, old_w)
    moment_new = jnp.where(keep, new_m, old_m)
    second_new = jnp.where(keep, new_v, old_v)
    left_new = jnp.where(keep, new_l, old_l)
    right_new = jnp.where(keep, new_r, old_r)
    new_weights = master_new.astype(jnp.bfloat16)
    spread = [new_weights]
    turns = None
    if pairs == 4:
        up = [(d, d + 2) for d in range(groups - 2)]
        down = [(d + 2, d) for d in range(groups - 2)]
        from_low, from_high = [new_weights], [new_weights]
        for k in range(1, pairs):
            from_low.append(lax.ppermute(from_low[-1], "dp", up))
            from_high.append(lax.ppermute(from_high[-1], "dp", down))
        rows = []
        for z in range(pairs):
            found = [(k, 0) for k in range(1, z + 1)] + [(k, 1) for k in range(1, pairs - z)]
            rows.append(sorted(found))
        turns = [[0] * pairs for _ in range(pairs)]
        other = [lax.ppermute(new_weights, "dp", across)]
        for m in range(pairs - 1):
            value = None
            probe = other[-1][0, 0, 0].astype(jnp.float32)
            here = pair + jnp.minimum((probe == probe).astype(jnp.int32), 0)
            for z in range(pairs):
                k, way = rows[z][m]
                turns[z][z + k if way else z - k] = m + 1
                part_w = (from_low, from_high)[way][k]
                value = part_w if value is None else jnp.where(here == z, part_w, value)
            spread.append(value)
            other.append(lax.ppermute(value, "dp", across))
    else:
        for step_off in range(1, pairs):
            hop = [(d, ((d // 2 + step_off) % pairs) * 2 + d % 2) for d in range(groups)]
            spread.append(lax.ppermute(new_weights, "dp", hop))
        other = [lax.ppermute(part_w, "dp", across) for part_w in spread]
    everyone = jnp.concatenate(spread + other)
    place_owner = owner // 2
    turn = lax.rem(pair - place_owner + pairs, pairs)
    if turns is not None:
        turn = jnp.zeros_like(owner)
        for z in range(pairs):
            for origin in range(pairs):
                hit = (pair == z) & (place_owner == origin)
                turn = jnp.where(hit, turns[z][origin], turn)
    held = jnp.where(owner % 2 == side, turn, pairs + turn)
    where_held = held * slot_count + (position - owner * slot_count)
    qkv_weight = join_tiles(everyone, where_held, 0, rows_q, cols_q)
    proj_weight = join_tiles(everyone, where_held, first_kind, rows_p, rows_q)
    qb_new, qm_new, qv_new = adamw(
        qkv_bias, qkv_bias_m, qkv_bias_v, qkv_total / tokens, fix_one, fix_two
    )
    pb_new, pm_new, pv_new = adamw(
        proj_bias, proj_bias_m, proj_bias_v, proj_total / tokens, fix_one, fix_two
    )
    return (
        master_new[None],
        moment_new[None],
        second_new[None],
        left_new[None],
        right_new[None],
        qkv_weight,
        proj_weight,
        qb_new,
        qm_new,
        qv_new,
        pb_new,
        pm_new,
        pv_new,
    )


SIDE = 200
COLUMN = 32
HALF = 16
TILE = 128
HALF_TILES = HALF * SIDE // TILE
TILES = 2 * HALF_TILES
PACE = 2
LAG = 2
CHUNKS = TILES // PACE
ROWS = 208
MOVES = 8
MOVE_TILES = -(-MOVES * SIDE // TILE)
PLANES = 4
STEPS = 8.0
TOP = 32000.0
MESH = pl.DeviceIdType.MESH
TABLE_ROWS = 16
(
    LEFT_AT,
    RIGHT_AT,
    SOURCE,
    GIVE_AT,
    GIVE_SLOT,
    FROM_SLOT,
    HOLDS,
    KINDS,
    SEEN,
    EDGES,
) = range(10)


def count_from(value, step, most):
    whole = jnp.zeros_like(value)
    for k in range(step, most, step):
        whole = whole + (value >= k).astype(jnp.int32)
    return whole


def table_kernel(cols_q, rows_q, owner_ref, out):
    me = lax.axis_index("dp")
    total, devices = 2 * COLUMN, 2 * PLANES
    split = cols_q * rows_q

    def grid(rows, columns, axis):
        return lax.broadcasted_iota(jnp.int32, (rows, columns), axis)

    def down(mask, value):
        return jnp.sum(jnp.where(mask, value, 0), axis=0, keepdims=True)

    def over(mask, value):
        return jnp.sum(jnp.where(mask, value, 0), axis=1, keepdims=True)

    def both(mask, value):
        return jnp.sum(over(mask, value), axis=0, keepdims=True)

    sub, lane = grid(total, total, 0), grid(total, total, 1)
    row = owner_ref[...]
    col = over(sub == lane, row)
    slot = over((col == row) & (lane < sub), 1)
    dev = grid(total, devices, 1)
    own = col == dev
    n = down(own, 1)
    dsub, dlane = grid(devices, devices, 0), grid(devices, devices, 1)
    here = grid(1, devices, 1)
    even = (here % 2) == 0

    def turned(value):
        return over(dsub == dlane, value)

    swap = (dsub // 2 == dlane // 2) & (dsub != dlane)
    partner = down(swap, turned(n))
    total0 = over(even, n)
    surplus = jnp.abs(total0 - COLUMN)
    crowded = (even & (total0 >= COLUMN)) | (~even & (total0 < COLUMN))
    room = jnp.where(crowded, jnp.minimum(jnp.minimum(MOVES, n), HALF - partner), 0)
    levels = grid(16, devices, 0)
    filled_to = jnp.sum(jnp.minimum(room, levels), axis=1, keepdims=True)
    fits = (filled_to <= surplus) & (grid(16, 1, 0) <= MOVES)
    level = jnp.sum(fits.astype(jnp.int32), axis=0, keepdims=True) - 1
    base = jnp.minimum(room, level)
    rest = surplus - jnp.sum(base, axis=1, keepdims=True)
    can = (room > level).astype(jnp.int32)
    before = down(dsub < dlane, turned(can))
    move = base + jnp.where((can > 0) & (before < rest), 1, 0)
    stay = n - move
    height = stay + down(swap, turned(move))
    start = down((dsub < dlane) & (dsub % 2 == dlane % 2), turned(height))
    far = down(swap, turned(start)) + partner - stay
    moved = slot >= over(own, stay)
    place = jnp.where(moved, over(own, far), over(own, start)) + slot
    parity = over(own, here % 2)
    column = jnp.where(moved, 1 - parity, parity)
    line = column * COLUMN + place
    side = me % 2
    mine = here == me
    my_n, my_stay, my_start = over(mine, n), over(mine, stay), over(mine, start)
    my_height = over(mine, height)
    spots = grid(1, total, 1)
    wanted = spots + side * COLUMN
    wanted = jnp.where(wanted >= total, wanted - total, wanted)
    at = down(line == wanted, sub)
    later = jnp.maximum(at - split, 0)
    first = at < split
    at_row, later_row = count_from(at, cols_q, split), count_from(later, rows_q, total - split)
    left_at = jnp.where(first, at_row, rows_q + later_row)
    right_at = jnp.where(first, at - at_row * cols_q, cols_q + later - later_row * rows_q)
    my_blocks = down((col == me) & (slot == lane), sub)
    source = jnp.where(spots < my_stay, my_start + spots, COLUMN + spots - my_stay)
    source = jnp.where(spots < my_n, jnp.minimum(source, COLUMN + MOVES - 1), 0)
    give_at = jnp.minimum(my_start + my_n + spots, COLUMN - 1)
    give_slot = jnp.minimum(my_stay + spots, HALF - 1)
    spot = spots - my_start
    from_slot = jnp.where(spot < my_stay, spot, jnp.where(my_n > my_stay, 0, HALF + spot - my_n))
    from_slot = jnp.minimum(jnp.maximum(from_slot, 0), HALF + MOVES - 1)
    seen = jnp.where(column == side, place, COLUMN + place)
    edges = jnp.where(spots == 0, my_start, my_start + my_height) * SIDE
    rows = {
        LEFT_AT: left_at,
        RIGHT_AT: right_at,
        SOURCE: source,
        GIVE_AT: give_at,
        GIVE_SLOT: give_slot,
        FROM_SLOT: from_slot,
        HOLDS: (spots < my_n).astype(jnp.int32),
        KINDS: (my_blocks < split).astype(jnp.int32),
        SEEN: down(sub == lane, seen),
        EDGES: edges,
    }
    out[...] = jnp.zeros_like(out)
    for n, value in rows.items():
        out[n : n + 1, :total] = value


def layout_tables(owner, cols_q, rows_q):
    return pl.pallas_call(
        lambda *refs: table_kernel(cols_q, rows_q, *refs),
        out_shape=jax.ShapeDtypeStruct((TABLE_ROWS, TILE), jnp.int32),
        in_specs=[vmem()],
        out_specs=vmem(),
    )(owner.reshape(1, -1))


def pack(value):
    top = jnp.max(jnp.abs(value), axis=1, keepdims=True)
    code = jnp.ceil(jnp.log(jnp.maximum(top, 1e-30)) * (STEPS / LN2))
    scale = TOP / jnp.exp(code * (LN2 / STEPS))
    whole = jnp.round(value * scale).astype(jnp.int32)
    codes = jnp.broadcast_to(
        code.astype(jnp.int32), (value.shape[0], ROWS - SIDE, value.shape[2])
    )
    return jnp.concatenate([whole, codes], axis=1).astype(jnp.int16)


def unpack(coded):
    wide = coded.astype(jnp.int32).astype(jnp.float32)
    scale = jnp.exp(wide[:, SIDE : SIDE + 1] * (LN2 / STEPS)) * (1.0 / TOP)
    return wide[:, :SIDE] * scale


LN2 = 0.6931471805599453


def some(k):
    return pl.ds(k * PACE, PACE)


def pieces(j):
    low, high = j * SIDE, (j + 1) * SIDE
    for tile in range(low // TILE, -(-high // TILE)):
        a, b = max(low, tile * TILE), min(high, (tile + 1) * TILE)
        yield tile, slice(a - tile * TILE, b - tile * TILE), slice(a - low, b - low)


def put(into, base, j, value):
    for tile, there, here in pieces(j):
        into[base + tile, :SIDE, there] = value[:, here]


def take(ref, base, j, into, n):
    for tile, there, here in pieces(j):
        into[n, :, here] = ref[base + tile, :SIDE, there]


def greet(peers):
    barrier = pltpu.get_barrier_semaphore()
    count = 0
    for condition, device in peers:
        if condition is None:
            pl.semaphore_signal(barrier, inc=1, device_id=device, device_id_type=MESH)
            count = count + 1
        else:

            @pl.when(condition)
            def _():
                pl.semaphore_signal(barrier, inc=1, device_id=device, device_id_type=MESH)

            count = count + condition.astype(jnp.int32)
    pl.semaphore_wait(barrier, count)


def remote(src, dst, send, recv, device):
    return pltpu.make_async_remote_copy(
        src_ref=src, dst_ref=dst, send_sem=send, recv_sem=recv, device_id=device, device_id_type=MESH
    )


def loop(low, high, body):
    lax.fori_loop(low, high, lambda k, carry: (body(k), carry)[1], 0)


def reduce_kernel(
    tokens,
    table,
    left,
    right,
    out,
    stage,
    pair,
    sent_x,
    got_x,
    sent_up,
    got_up,
    sent_down,
    got_down,
    tiles,
    stage_m,
    sent_m,
    got_m,
    sems,
    sems_m,
):
    me = lax.axis_index("dp")
    z, side = me // 2, me % 2
    across = {"dp": me + 1 - 2 * side}
    upper = {"dp": jnp.minimum(me + 2, 2 * PLANES - 1)}
    lower = {"dp": jnp.maximum(me - 2, 0)}
    last = PLANES - 1
    greet([(None, across), (z < last, upper), (z > 0, lower)])

    def copy_x(k):
        return remote(
            sent_x.at[some(k)], got_x.at[some(k)], sems.at[0, k], sems.at[1, k], across
        )

    def copy_up(k):
        return remote(
            sent_up.at[some(k)], got_up.at[some(k)], sems.at[2, k], sems.at[3, k], upper
        )

    def copy_down(k):
        return remote(
            sent_down.at[some(k)], got_down.at[some(k)], sems.at[4, k], sems.at[5, k], lower
        )

    def product(n):
        return lax.dot_general(
            left[table[LEFT_AT, n]],
            right[table[RIGHT_AT, n]],
            (((1,), (1,)), ((), ())),
            preferred_element_type=jnp.float32,
        )

    def send_other(low, high):
        def body(k):
            sent_x[some(k)] = pack(stage[some(k)])
            copy_x(k).start()

        loop(low, high, body)

    done = 0
    for h in range(2):
        for part in range(4):
            for j in range(part * 4, part * 4 + 4):
                put(stage, h * HALF_TILES, j, product(COLUMN + h * HALF + j))
            ready = (h * HALF * SIDE + (part + 1) * 4 * SIDE) // (TILE * PACE)
            send_other(done, ready)
            done = ready

    def own_half(h):
        for j in range(HALF):
            put(pair, h * HALF_TILES, j, product(h * HALF + j))

    loop(0, 2, own_half)

    def step(t):
        @pl.when(t < CHUNKS)
        def _():
            copy_x(t).wait_recv()
            pair[some(t)] += unpack(got_x[some(t)])

        up = t - LAG * z

        @pl.when((up >= 0) & (up < CHUNKS))
        def _():
            @pl.when(z == 0)
            def _():
                sent_up[some(up)] = pack(pair[some(up)])

            @pl.when(z > 0)
            def _():
                copy_up(up).wait_recv()

                @pl.when(z < last)
                def _():
                    sent_up[some(up)] = pack(pair[some(up)] + unpack(got_up[some(up)]))

            @pl.when(z < last)
            def _():
                copy_up(up).start()

        down = t - LAG * (last - z)

        @pl.when((down >= 0) & (down < CHUNKS))
        def _():
            @pl.when(z == last)
            def _():
                sent_down[some(down)] = pack(pair[some(down)])

            @pl.when(z < last)
            def _():
                copy_down(down).wait_recv()

                @pl.when(z > 0)
                def _():
                    sent_down[some(down)] = pack(pair[some(down)] + unpack(got_down[some(down)]))

            @pl.when(z > 0)
            def _():
                copy_down(down).start()

        full = t - LAG * last

        @pl.when(full >= 0)
        def _():
            @pl.when(z > 0)
            def _():
                pair[some(full)] += unpack(got_up[some(full)])

            @pl.when(z < last)
            def _():
                pair[some(full)] += unpack(got_down[some(full)])

            @pl.when((full == HALF_TILES // PACE) | (full == CHUNKS - 1))
            def _():
                h = (full == CHUNKS - 1).astype(jnp.int32)
                for j in range(HALF):
                    take(pair, h * HALF_TILES, j, tiles, h * HALF + j)

    loop(0, CHUNKS + LAG * last, step)

    stage_m[MOVE_TILES - 1] = jnp.zeros((SIDE, TILE), jnp.float32)
    for k in range(MOVES):
        put(stage_m, 0, k, tiles[table[GIVE_AT, k]])
    sent_m[...] = pack(stage_m[...])
    move = remote(sent_m, got_m, sems_m.at[0], sems_m.at[1], across)
    move.start()

    def drain(k):
        copy_x(k).wait_send()

        @pl.when(z < last)
        def _():
            copy_up(k).wait_send()

        @pl.when(z > 0)
        def _():
            copy_down(k).wait_send()

    loop(0, CHUNKS, drain)
    move.wait()
    stage_m[...] = unpack(got_m[...])
    for k in range(MOVES):
        take(stage_m, 0, k, tiles, COLUMN + k)

    def finish(s):
        out[s] = jnp.where(
            table[HOLDS, s] > 0, tiles[table[SOURCE, s]] * (1.0 / tokens), 0.0
        )

    loop(0, HALF, finish)


def vmem():
    return pl.BlockSpec(memory_space=pltpu.VMEM)


def smem():
    return pl.BlockSpec(memory_space=pltpu.SMEM)


def hbm():
    return pl.BlockSpec(memory_space=pl.ANY)


def reduce_tiles(left, right, table, tokens):
    coded = pltpu.VMEM((TILES, ROWS, TILE), jnp.int16)
    moved = pltpu.VMEM((MOVE_TILES, ROWS, TILE), jnp.int16)
    return pl.pallas_call(
        lambda *refs: reduce_kernel(tokens, *refs),
        out_shape=pltpu.VMEM((HALF, SIDE, SIDE), jnp.float32),
        in_specs=[smem()] + [vmem()] * 2,
        out_specs=vmem(),
        scratch_shapes=[
            pltpu.VMEM((TILES, SIDE, TILE), jnp.float32),
            pltpu.VMEM((TILES, SIDE, TILE), jnp.float32),
            *([coded] * 6),
            pltpu.VMEM((COLUMN + MOVES, SIDE, SIDE), jnp.float32),
            pltpu.VMEM((MOVE_TILES, SIDE, TILE), jnp.float32),
            moved,
            moved,
            pltpu.SemaphoreType.DMA((6, CHUNKS)),
            pltpu.SemaphoreType.DMA((2,)),
        ],
        compiler_params=pltpu.CompilerParams(
            collective_id=0, has_side_effects=True, vmem_limit_bytes=VMEM_LIMIT
        ),
    )(table, left, right)


VMEM_LIMIT = 56 * 1024 * 1024
STEP_LIMIT = 26 * 1024 * 1024
LAST_LIMIT = 16 * 1024 * 1024
EARLY = 10
SMALL_ROWS = 32
BIAS_ROWS = 24


def dot3(a, b, dims):
    a_high, b_high = a.astype(jnp.bfloat16), b.astype(jnp.bfloat16)
    a_low = (a - a_high.astype(jnp.float32)).astype(jnp.bfloat16)
    b_low = (b - b_high.astype(jnp.float32)).astype(jnp.bfloat16)

    def dot(p, q):
        return lax.dot_general(p, q, (dims, ((), ())), preferred_element_type=jnp.float32)

    return dot(a_high, b_high) + (dot(a_high, b_low) + dot(a_low, b_high))


def step_kernel(
    table,
    fixes,
    grads,
    small,
    master,
    moment,
    second,
    stat_left,
    stat_right,
    root_left,
    root_right,
    state_w,
    state_m,
    state_v,
    state_l,
    state_r,
    small_out,
    blocks,
    state_a,
    state_b,
    sums,
    sums_dp,
    sums_grp,
    light,
    sent_m,
    got_m,
    own,
    got_up,
    got_down,
    known,
    got_x,
    load_sems,
    sum_sems,
    grp_sems,
    move_sems,
    sems,
):
    me = lax.axis_index("dp")
    z, side = me // 2, me % 2
    n_dp, n_grp = lax.axis_size("dp"), lax.axis_size("grp")
    my_grp = lax.axis_index("grp")
    across = {"dp": me + 1 - 2 * side}
    upper = {"dp": jnp.minimum(me + 2, 2 * PLANES - 1)}
    lower = {"dp": jnp.maximum(me - 2, 0)}
    last = PLANES - 1
    held = [state_v, state_a, state_b, state_w, state_m, state_l, state_r]
    given = [second, root_left, root_right, master, moment, stat_left, stat_right]
    loads = []
    for n, (ref, scratch) in enumerate(zip(given, held)):
        copy = pltpu.make_async_copy(ref.at[0], scratch, load_sems.at[n])
        copy.start()
        loads.append(copy)

    peers = [(None, {"dp": lax.rem(me + k, n_dp)}) for k in range(1, n_dp)]
    peers += [(None, {"grp": lax.rem(my_grp + k, n_grp)}) for k in range(1, n_grp)]
    greet(peers)

    fix_two = fixes[0]
    for copy in loads[:3]:
        copy.wait()

    def direction(s, sums_now):
        adam_q, adam_p, shampoo_q, shampoo_p = sums_now
        grad = grads[s]
        old = state_v[s]
        new = beta_two * old + (1.0 - beta_two) * grad * grad
        adam = grad / (jnp.sqrt(new / fix_two) + epsilon)
        half = dot3(state_a[s], grad, ((1,), (0,)))
        shampoo = dot3(half, state_b[s], ((1,), (0,)))
        state_v[s] = jnp.where(table[HOLDS, s] > 0, new, old)
        state_a[s] = shampoo
        adam_sq = jnp.sum(adam * adam, axis=0, keepdims=True)
        shampoo_sq = jnp.sum(shampoo * shampoo, axis=0, keepdims=True)
        q = table[KINDS, s] > 0
        return (
            adam_q + jnp.where(q, adam_sq, 0.0),
            adam_p + jnp.where(q, 0.0, adam_sq),
            shampoo_q + jnp.where(q, shampoo_sq, 0.0),
            shampoo_p + jnp.where(q, 0.0, shampoo_sq),
        )

    nothing = jnp.zeros((1, SIDE), jnp.float32)
    parts = lax.fori_loop(0, HALF, direction, (nothing,) * 4, unroll=4)
    sums[0, :BIAS_ROWS] = small[...]
    row = lax.broadcasted_iota(jnp.int32, (SMALL_ROWS - BIAS_ROWS, 128), 0)
    packed = jnp.zeros((SMALL_ROWS - BIAS_ROWS, 128), jnp.float32)
    for n, part in enumerate(parts):
        packed = jnp.where(row == n, jnp.sum(part), packed)
    sums[0, BIAS_ROWS:] = packed

    copies = []
    for k in range(1, n_dp):
        copy = remote(
            sums.at[0], sums_dp.at[k - 1], sum_sems.at[0, k - 1], sum_sems.at[1, k - 1],
            {"dp": lax.rem(me + k, n_dp)},
        )
        copy.start()
        copies.append(copy)
    for copy in loads[3:5]:
        copy.wait()
    for copy in copies:
        copy.wait()
    for d in range(n_dp):
        value = jnp.where(me == d, sums[0], sums_dp[lax.rem(me - d + n_dp + n_dp - 1, n_dp) % (n_dp - 1)])
        total = value if d == 0 else total + value
    small_out[...] = total[:BIAS_ROWS]
    sums_grp[my_grp] = total[BIAS_ROWS:]
    copies = []
    for k in range(1, n_grp):
        copy = remote(
            sums_grp.at[my_grp], sums_grp.at[my_grp], grp_sems.at[0, k - 1], grp_sems.at[1, k - 1],
            {"grp": lax.rem(my_grp + k, n_grp)},
        )
        copy.start()
        copies.append(copy)
    for copy in copies:
        copy.wait()
    total = sums_grp[0]
    for g in range(1, n_grp):
        total = total + sums_grp[g]
    graft_q = jnp.sqrt(total[0:1] / (total[2:3] + graft_floor))[:, :1]
    graft_p = jnp.sqrt(total[1:2] / (total[3:4] + graft_floor))[:, :1]

    def update(s):
        graft = jnp.where(table[KINDS, s] > 0, graft_q, graft_p)
        old_m, old_w = state_m[s], state_w[s]
        new_m = beta_one * old_m + (1.0 - beta_one) * (graft * state_a[s])
        new_w = old_w - learn_rate * (new_m + weight_decay * old_w)
        state_m[s] = jnp.where(table[HOLDS, s] > 0, new_m, old_m)
        state_w[s] = jnp.where(table[HOLDS, s] > 0, new_w, old_w)
        light[s] = jnp.where(table[KINDS, s] > 0, new_w.T, new_w).astype(jnp.bfloat16)

    loop(0, HALF, update)

    sent_m[...] = jnp.zeros_like(sent_m)
    for k in range(MOVES):
        put(sent_m, 0, k, light[table[GIVE_SLOT, k]])
    move = remote(sent_m, got_m, move_sems.at[0], move_sems.at[1], across)
    move.start()

    for copy in loads[5:7]:
        copy.wait()

    def stats(s):
        grad = grads[s]
        keep = table[HOLDS, s] > 0
        new_l = beta_stat * state_l[s] + (1.0 - beta_stat) * dot3(grad, grad, ((1,), (1,)))
        new_r = beta_stat * state_r[s] + (1.0 - beta_stat) * dot3(grad, grad, ((0,), (0,)))
        state_l[s] = jnp.where(keep, new_l, state_l[s])
        state_r[s] = jnp.where(keep, new_r, state_r[s])

    loop(0, EARLY, stats)
    move.wait()
    for k in range(MOVES):
        take(got_m, 0, k, light, HALF + k)

    def fill(h):
        for j in range(HALF):
            put(own, h * HALF_TILES, j, light[table[FROM_SLOT, h * HALF + j]])

    def pad(k):
        own[k, SIDE:] = jnp.zeros((ROWS - SIDE, TILE), jnp.bfloat16)

    loop(0, TILES, pad)
    loop(0, 2, fill)

    low, high = table[EDGES, 0], table[EDGES, 1]
    shape = (PACE, ROWS, TILE)
    lane = lax.broadcasted_iota(jnp.int32, shape, 0) * TILE + lax.broadcasted_iota(
        jnp.int32, shape, 2
    )
    up_window = -(-HALF_TILES // PACE)
    down_window = HALF_TILES // PACE

    def wide(ref, k):
        return ref[some(k)].astype(jnp.float32)

    def copy_up(k, src):
        return remote(src.at[some(k)], got_up.at[some(k)], sems.at[0, k], sems.at[1, k], upper)

    def copy_down(k, src):
        return remote(src.at[some(k)], got_down.at[some(k)], sems.at[2, k], sems.at[3, k], lower)

    def copy_x(k):
        return remote(known.at[some(k)], got_x.at[some(k)], sems.at[4, k], sems.at[5, k], across)

    def step(t):
        up = t - LAG * z

        @pl.when((up >= 0) & (up < CHUNKS))
        def _():
            @pl.when((z == 0) & (up < up_window))
            def _():
                copy_up(up, own).start()

            @pl.when(z > 0)
            def _():
                @pl.when((z > 1) | (up < up_window))
                def _():
                    copy_up(up, own).wait_recv()
                    mask = lane + up * (PACE * TILE) < low
                    got_up[some(up)] = jnp.where(mask, wide(got_up, up), wide(own, up)).astype(
                        jnp.bfloat16
                    )

                @pl.when((z == 1) & (up >= up_window))
                def _():
                    got_up[some(up)] = own[some(up)]

                @pl.when(z < last)
                def _():
                    copy_up(up, got_up).start()

        down = t - LAG * (last - z)

        @pl.when((down >= 0) & (down < CHUNKS))
        def _():
            @pl.when((z == last) & (down >= down_window))
            def _():
                copy_down(down, own).start()

            @pl.when(z < last)
            def _():
                @pl.when((z < last - 1) | (down >= down_window))
                def _():
                    copy_down(down, own).wait_recv()
                    mask = lane + down * (PACE * TILE) >= high
                    got_down[some(down)] = jnp.where(
                        mask, wide(got_down, down), wide(own, down)
                    ).astype(jnp.bfloat16)

                @pl.when((z == last - 1) & (down < down_window))
                def _():
                    got_down[some(down)] = own[some(down)]

                @pl.when(z > 0)
                def _():
                    copy_down(down, got_down).start()

        full = t - LAG * last

        @pl.when(full >= 0)
        def _():
            place = lane + full * (PACE * TILE)
            value = jnp.where(place < low, wide(got_up, full), wide(own, full))
            value = jnp.where(place >= high, wide(got_down, full), value)
            known[some(full)] = value.astype(jnp.bfloat16)
            copy_x(full).start()

            @pl.when((full == HALF_TILES // PACE) | (full == CHUNKS - 1))
            def _():
                h = (full == CHUNKS - 1).astype(jnp.int32)
                for j in range(HALF):
                    take(known, h * HALF_TILES, j, blocks, h * HALF + j)

        @pl.when(t < HALF - EARLY)
        def _():
            stats(EARLY + t)

    loop(0, CHUNKS + LAG * last, step)
    for h in range(2):
        loop(0 if h == 0 else up_window, up_window if h == 0 else CHUNKS, lambda k: copy_x(k).wait_recv())
        for j in range(HALF):
            take(got_x, h * HALF_TILES, j, blocks, COLUMN + h * HALF + j)

    def drain(k):
        copy_x(k).wait_send()

        @pl.when((z == 1) | (z == 2) | ((z == 0) & (k < up_window)))
        def _():
            copy_up(k, own).wait_send()

        @pl.when((z == 1) | (z == 2) | ((z == last) & (k >= down_window)))
        def _():
            copy_down(k, own).wait_send()

    loop(0, CHUNKS, drain)


def apply_step(table, fixes, grads, small, states):
    n_dp, n_grp = lax.axis_size("dp"), lax.axis_size("grp")
    held = pltpu.VMEM((HALF, SIDE, SIDE), jnp.float32)
    line = pltpu.VMEM((TILES, ROWS, TILE), jnp.bfloat16)
    moved = pltpu.VMEM((MOVE_TILES, ROWS, TILE), jnp.bfloat16)
    return pl.pallas_call(
        step_kernel,
        out_shape=(
            *([held] * 5),
            jax.ShapeDtypeStruct((BIAS_ROWS, 128), jnp.float32),
            pltpu.VMEM((2 * COLUMN, SIDE, SIDE), jnp.bfloat16),
        ),
        in_specs=[smem()] * 2 + [vmem()] * 2 + [hbm()] * 7,
        out_specs=[vmem()] * 7,
        scratch_shapes=[
            *([held] * 2),
            pltpu.VMEM((1, SMALL_ROWS, 128), jnp.float32),
            pltpu.VMEM((n_dp - 1, SMALL_ROWS, 128), jnp.float32),
            pltpu.VMEM((n_grp, SMALL_ROWS - BIAS_ROWS, 128), jnp.float32),
            pltpu.VMEM((HALF + MOVES, SIDE, SIDE), jnp.bfloat16),
            moved,
            moved,
            *([line] * 5),
            pltpu.SemaphoreType.DMA((7,)),
            pltpu.SemaphoreType.DMA((2, n_dp - 1)),
            pltpu.SemaphoreType.DMA((2, n_grp - 1)),
            pltpu.SemaphoreType.DMA((2,)),
            pltpu.SemaphoreType.DMA((6, CHUNKS)),
        ],
        compiler_params=pltpu.CompilerParams(
            collective_id=1, has_side_effects=True, vmem_limit_bytes=STEP_LIMIT
        ),
    )(table, fixes, grads, small, *states)


def finish_kernel(cols_q, rows_q, rows_p, table, blocks, *refs):
    given, kept = refs[:5], refs[5:10]
    qkv, proj, bands, copy_sems, band_sems = refs[10:]
    stores = []
    for n, (ref, into) in enumerate(zip(given, kept)):
        stores.append(pltpu.make_async_copy(ref, into.at[0], copy_sems.at[n]))
        stores[-1].start()
    for n in range(cols_q + rows_p):
        first, stride = (n, cols_q) if n < cols_q else (cols_q * rows_q + (n - cols_q) * rows_q, 1)
        parts = [
            blocks[table[SEEN, first + k * stride]].astype(jnp.float32) for k in range(rows_q)
        ]
        bands[n] = jnp.concatenate(parts, axis=1).astype(jnp.bfloat16)
        into = qkv.at[n] if n < cols_q else proj.at[n - cols_q]
        stores.append(pltpu.make_async_copy(bands.at[n], into, band_sems.at[n]))
        stores[-1].start()
    for copy in stores:
        copy.wait()


def finish(blocks, table, states, rows_q, cols_q, rows_p):
    across = rows_q * SIDE
    state = jax.ShapeDtypeStruct((1, HALF, SIDE, SIDE), jnp.float32)
    return pl.pallas_call(
        lambda *refs: finish_kernel(cols_q, rows_q, rows_p, *refs),
        out_shape=(
            *([state] * 5),
            jax.ShapeDtypeStruct((cols_q, SIDE, across), jnp.bfloat16),
            jax.ShapeDtypeStruct((rows_p, SIDE, across), jnp.bfloat16),
        ),
        in_specs=[smem()] + [vmem()] * 6,
        out_specs=[hbm()] * 7,
        scratch_shapes=[
            pltpu.VMEM((cols_q + rows_p, SIDE, across), jnp.bfloat16),
            pltpu.SemaphoreType.DMA((5,)),
            pltpu.SemaphoreType.DMA((cols_q + rows_p,)),
        ],
        compiler_params=pltpu.CompilerParams(vmem_limit_bytes=LAST_LIMIT),
    )(table, blocks, *states)


def on_device(
    x_in,
    attn_in,
    grad_qkv,
    grad_out,
    owner,
    step,
    master,
    moment,
    second,
    stat_left,
    stat_right,
    root_left,
    root_right,
    qkv_bias,
    qkv_bias_m,
    qkv_bias_v,
    proj_bias,
    proj_bias_m,
    proj_bias_v,
):
    groups = lax.axis_size("dp")
    slot_count, side = master.shape[1], master.shape[2]
    if (groups, slot_count, side, owner.shape[0]) != (2 * PLANES, HALF, SIDE, 2 * COLUMN):
        return on_device_any(
            x_in, attn_in, grad_qkv, grad_out, owner, step, master, moment, second, stat_left, stat_right,
            root_left, root_right, qkv_bias, qkv_bias_m, qkv_bias_v, proj_bias, proj_bias_m, proj_bias_v,
        )
    depth = x_in.shape[0]
    tokens = depth * groups
    rows_q = D // SIDE
    cols_q = grad_qkv.shape[1] // SIDE
    rows_p = attn_in.shape[1] // SIDE
    count_f = step[0].astype(jnp.float32)
    fix_one = 1.0 - jnp.power(jnp.float32(beta_one), count_f)
    fix_two = 1.0 - jnp.power(jnp.float32(beta_two), count_f)
    table = layout_tables(owner, cols_q, rows_q)
    left = jnp.concatenate([x_in.T.reshape(rows_q, SIDE, depth), attn_in.T.reshape(rows_p, SIDE, depth)])
    right = jnp.concatenate([grad_qkv.T.reshape(cols_q, SIDE, depth), grad_out.T.reshape(rows_q, SIDE, depth)])
    grads = reduce_tiles(left, right, table, tokens)
    width_q, width_p = grad_qkv.shape[1], grad_out.shape[1]
    small = jnp.concatenate(
        [
            jnp.sum(grad_qkv, axis=0, dtype=jnp.float32),
            jnp.sum(grad_out, axis=0, dtype=jnp.float32),
            jnp.zeros((BIAS_ROWS * 128 - width_q - width_p,), jnp.float32),
        ]
    ).reshape(BIAS_ROWS, 128)
    states = (master, moment, second, stat_left, stat_right, root_left, root_right)
    fixes = fix_two.reshape(1)
    *stepped, small_sum, blocks = apply_step(table, fixes, grads, small, states)
    *stepped, qkv, proj = finish(blocks, table, stepped, rows_q, cols_q, rows_p)
    master_new, moment_new, second_new, left_new, right_new = stepped
    qkv_weight = qkv.reshape(cols_q * SIDE, rows_q * SIDE).T
    proj_weight = proj.reshape(rows_p * SIDE, rows_q * SIDE)
    small_sum = small_sum.reshape(-1)
    qkv_total = small_sum[:width_q]
    proj_total = small_sum[width_q : width_q + width_p]
    qb_new, qm_new, qv_new = adamw(
        qkv_bias, qkv_bias_m, qkv_bias_v, qkv_total / tokens, fix_one, fix_two
    )
    pb_new, pm_new, pv_new = adamw(
        proj_bias, proj_bias_m, proj_bias_v, proj_total / tokens, fix_one, fix_two
    )
    return (
        master_new,
        moment_new,
        second_new,
        left_new,
        right_new,
        qkv_weight,
        proj_weight,
        qb_new,
        qm_new,
        qv_new,
        pb_new,
        pm_new,
        pv_new,
    )


def solution(mesh):
    return jax.shard_map(
        on_device,
        mesh=mesh,
        in_specs=(
            P("dp", None),
            P("dp", "grp"),
            P("dp", "grp"),
            P("dp", None),
            P(),
            P(),
            P("grp", "dp", None, None),
            P("grp", "dp", None, None),
            P("grp", "dp", None, None),
            P("grp", "dp", None, None),
            P("grp", "dp", None, None),
            P("grp", "dp", None, None),
            P("grp", "dp", None, None),
            P("grp"),
            P("grp"),
            P("grp"),
            P(),
            P(),
            P(),
        ),
        out_specs=(
            P("grp", "dp", None, None),
            P("grp", "dp", None, None),
            P("grp", "dp", None, None),
            P("grp", "dp", None, None),
            P("grp", "dp", None, None),
            P(None, "grp"),
            P("grp", None),
            P("grp"),
            P("grp"),
            P("grp"),
            P(),
            P(),
            P(),
        ),
        check_vma=False,
    )
```

```python
import jax
import jax.numpy as jnp
from jax import lax
from jax.experimental import pallas as pl
from jax.experimental.pallas import tpu as pltpu
from jax.sharding import PartitionSpec as P

D = 1600


beta_one = 0.9
beta_two = 0.95
beta_stat = 0.9
learn_rate = 0.02
weight_decay = 0.1
epsilon = 1e-08
graft_floor = 1e-06


def positions(owner, slot_count):
    total_blocks = owner.shape[0]
    blocks = jnp.arange(total_blocks, dtype=jnp.int32)
    same_owner = owner[None, :] == owner[:, None]
    earlier = blocks[None, :] < blocks[:, None]
    slot_rank = jnp.sum(jnp.where(same_owner & earlier, 1, 0).astype(jnp.int32), axis=1)
    return owner * slot_count + slot_rank


def adamw(param, first_m, second_m, grad, fix_one, fix_two):
    new_m = beta_one * first_m + (1.0 - beta_one) * grad
    new_v = beta_two * second_m + (1.0 - beta_two) * grad * grad
    new_p = param - learn_rate * (new_m / fix_one) / (jnp.sqrt(new_v / fix_two) + epsilon)
    return (new_p, new_m, new_v)


def place_kernel(
    split, cols_q, rows_q, slots, holder_ref, used_ref, left_ref, right_ref, tile_ref, peak_ref
):
    o = pl.program_id(0)
    peak_ref[...] = jnp.zeros_like(peak_ref)
    side = left_ref.shape[1]
    for s in range(slots):
        b = holder_ref[o * slots + s]

        @pl.when(used_ref[o * slots + s] > 0)
        def _():
            first = b < split
            later = jnp.maximum(b - split, 0)
            i = jnp.where(first, b // cols_q, rows_q + later // rows_q)
            j = jnp.where(first, b % cols_q, cols_q + later % rows_q)
            tile = lax.dot_general(
                left_ref[i],
                right_ref[j],
                (((1,), (1,)), ((), ())),
                preferred_element_type=jnp.float32,
            )
            tile_ref[0, :, s * side : (s + 1) * side] = tile
            peak_ref[0, s : s + 1, :] = jnp.full((1, 128), jnp.max(jnp.abs(tile)), jnp.float32)


def place_tiles(left, right, holder, used, split, cols_q, rows_q, groups, slots):
    side, depth = left.shape[1:]
    return pl.pallas_call(
        lambda *refs: place_kernel(split, cols_q, rows_q, slots, *refs),
        out_shape=(
            jax.ShapeDtypeStruct((groups, side, slots * side), jnp.float32),
            jax.ShapeDtypeStruct((groups, slots, 128), jnp.float32),
        ),
        grid_spec=pltpu.PrefetchScalarGridSpec(
            num_scalar_prefetch=2,
            grid=(groups,),
            in_specs=[
                pl.BlockSpec(left.shape, lambda o, h, u: (0, 0, 0)),
                pl.BlockSpec(right.shape, lambda o, h, u: (0, 0, 0)),
            ],
            out_specs=[
                pl.BlockSpec((1, side, slots * side), lambda o, h, u: (o, 0, 0)),
                pl.BlockSpec((1, slots, 128), lambda o, h, u: (o, 0, 0)),
            ],
        ),
        compiler_params=pltpu.CompilerParams(vmem_limit_bytes=32 * 1024 * 1024),
    )(holder, used, left, right)


def join_kernel(count, pos_ref, *refs):
    out_ref = refs[count]
    parts = [refs[k][0].astype(jnp.float32) for k in range(count)]
    out_ref[...] = jnp.concatenate(parts, axis=1).astype(out_ref.dtype)


def join_tiles(tiles, position, base, rows, cols):
    side = tiles.shape[1]

    def spot(k):
        return lambda r, pos: (pos[base + r * cols + k], 0, 0)

    return pl.pallas_call(
        lambda *refs: join_kernel(cols, *refs),
        out_shape=jax.ShapeDtypeStruct((rows * side, cols * side), tiles.dtype),
        grid_spec=pltpu.PrefetchScalarGridSpec(
            num_scalar_prefetch=1,
            grid=(rows,),
            in_specs=[pl.BlockSpec((1, side, side), spot(k)) for k in range(cols)],
            out_specs=pl.BlockSpec((side, cols * side), lambda r, pos: (r, 0)),
        ),
        compiler_params=pltpu.CompilerParams(vmem_limit_bytes=32 * 1024 * 1024),
    )(position, *([tiles] * cols))


def sum_kernel(axes, sizes, in_ref, out_ref, *scratch):
    buffers = scratch[: len(axes)]
    send_sems = scratch[len(axes) : 2 * len(axes)]
    recv_sems = scratch[2 * len(axes) :]
    barrier = pltpu.get_barrier_semaphore()
    for axis, size in zip(axes, sizes):
        me = lax.axis_index(axis)
        for k in range(1, size):
            pl.semaphore_signal(
                barrier,
                inc=1,
                device_id={axis: lax.rem(me + k, size)},
                device_id_type=pl.DeviceIdType.MESH,
            )
    pl.semaphore_wait(barrier, sum(size - 1 for size in sizes))
    value = in_ref[...]
    for n, (axis, size) in enumerate(zip(axes, sizes)):
        me = lax.axis_index(axis)
        buffers[n][me] = value
        copies = []
        for k in range(1, size):
            copy = pltpu.make_async_remote_copy(
                src_ref=buffers[n].at[me],
                dst_ref=buffers[n].at[me],
                send_sem=send_sems[n].at[k - 1],
                recv_sem=recv_sems[n].at[k - 1],
                device_id={axis: lax.rem(me + k, size)},
                device_id_type=pl.DeviceIdType.MESH,
            )
            copy.start()
            copies.append(copy)
        for copy in copies:
            copy.wait()
        value = buffers[n][0]
        for k in range(1, size):
            value = value + buffers[n][k]
    out_ref[...] = value


def sum_over(value, axes, collective_id):
    sizes = [lax.axis_size(axis) for axis in axes]
    scratch = [pltpu.VMEM((size,) + value.shape, jnp.float32) for size in sizes]
    scratch += [pltpu.SemaphoreType.DMA((size - 1,)) for size in sizes]
    scratch += [pltpu.SemaphoreType.DMA((size - 1,)) for size in sizes]
    return pl.pallas_call(
        lambda *refs: sum_kernel(axes, sizes, *refs),
        out_shape=jax.ShapeDtypeStruct(value.shape, jnp.float32),
        in_specs=[pl.BlockSpec(memory_space=pltpu.VMEM)],
        out_specs=pl.BlockSpec(memory_space=pltpu.VMEM),
        scratch_shapes=scratch,
        compiler_params=pltpu.CompilerParams(collective_id=collective_id, has_side_effects=True),
    )(value)


def on_device_any(
    x_in,
    attn_in,
    grad_qkv,
    grad_out,
    owner,
    step,
    master,
    moment,
    second,
    stat_left,
    stat_right,
    root_left,
    root_right,
    qkv_bias,
    qkv_bias_m,
    qkv_bias_v,
    proj_bias,
    proj_bias_m,
    proj_bias_v,
):
    exact = lax.Precision.HIGHEST
    groups = lax.axis_size("dp")
    own_index = lax.axis_index("dp")
    total_blocks = owner.shape[0]
    slot_count = master.shape[1]
    block_size = master.shape[2]
    tokens = x_in.shape[0] * groups
    rows_q = D // block_size
    cols_q = grad_qkv.shape[1] // block_size
    rows_p = attn_in.shape[1] // block_size
    first_kind = rows_q * cols_q
    count_f = step[0].astype(jnp.float32)
    fix_one = 1.0 - jnp.power(jnp.float32(beta_one), count_f)
    fix_two = 1.0 - jnp.power(jnp.float32(beta_two), count_f)
    blocks = jnp.arange(total_blocks, dtype=jnp.int32)
    position = positions(owner, slot_count)
    spots = groups * slot_count
    matches = position[None, :] == jnp.arange(spots, dtype=jnp.int32)[:, None]
    filled = jnp.any(matches, axis=1)
    holder = jnp.sum(jnp.where(matches, blocks[None, :], 0), axis=1)
    my_blocks = lax.dynamic_slice_in_dim(holder, own_index * slot_count, slot_count)
    my_filled = lax.dynamic_slice_in_dim(filled, own_index * slot_count, slot_count)
    filled_f = my_filled.astype(jnp.float32)
    keep = my_filled[:, None, None]

    depth = x_in.shape[0]
    left = jnp.concatenate(
        [
            x_in.T.reshape(rows_q, block_size, depth),
            attn_in.T.reshape(rows_p, block_size, depth),
        ]
    )
    right = jnp.concatenate(
        [
            grad_qkv.T.reshape(cols_q, block_size, depth),
            grad_out.T.reshape(rows_q, block_size, depth),
        ]
    )
    local_tiles, peaks = place_tiles(
        left,
        right,
        holder,
        filled.astype(jnp.int32),
        first_kind,
        cols_q,
        rows_q,
        groups,
        slot_count,
    )

    width_q, width_p = grad_qkv.shape[1], grad_out.shape[1]
    small = jnp.concatenate(
        [
            jnp.sum(grad_qkv, axis=0, dtype=jnp.float32),
            jnp.sum(grad_out, axis=0, dtype=jnp.float32),
            peaks[:, :, 0].reshape(spots),
        ]
    )
    used = small.shape[0]
    padded = -(-used // 1024) * 1024
    small = jnp.pad(small, (0, padded - used)).reshape(8, padded // 8)
    small = sum_over(small, ("dp",), 0).reshape(padded)
    qkv_total = small[:width_q]
    proj_total = small[width_q : width_q + width_p]
    bound = small[width_q + width_p : used]
    spot_bound = jnp.where(bound > 0.0, bound, 1.0).reshape(groups, 1, slot_count)
    spot_bound = jnp.repeat(spot_bound, block_size, axis=2)
    shrink = 16384.0 / spot_bound
    grow = spot_bound / 16384.0

    pair = own_index // 2
    side = own_index % 2
    pairs = groups // 2
    tiles = local_tiles

    def chunk(array, where):
        return lax.dynamic_index_in_dim(array, where, 0, keepdims=False)

    across = [(d, d ^ 1) for d in range(groups)]
    arrivals = []
    order = list(range(1, pairs))
    if pairs == 4:
        order = [1, 3, 2]
    order = order + [0]
    received = []
    for step_off in order:
        theirs = lax.rem(pair + step_off, pairs) * 2 + 1 - side
        sent = (chunk(tiles, theirs) * chunk(shrink, theirs)).astype(jnp.float16)
        received.append(lax.ppermute(sent, "dp", across))
    after = jnp.int32(0)
    for step_off, got in zip(order, received):
        ours = lax.rem(pair + step_off, pairs) * 2 + side
        both = chunk(tiles, ours + after) * chunk(shrink, ours) + got.astype(jnp.float32)
        if step_off == 0:
            mine = both
        else:
            hop = [(d, ((d // 2 + step_off) % pairs) * 2 + d % 2) for d in range(groups)]
            both = both.astype(jnp.float16)
            arrivals.append(lax.ppermute(both, "dp", hop))
            probe = arrivals[-1][0, 0].astype(jnp.float32)
            after = jnp.minimum((probe == probe).astype(jnp.int32), 0)
    for arrived in arrivals:
        mine = mine + arrived.astype(jnp.float32)
    mine = mine * (chunk(grow, own_index) / tokens)
    mine = mine.reshape(block_size, slot_count, block_size).transpose(1, 0, 2)
    grads = jnp.where(keep, mine, 0.0)
    old_w = master[0]
    old_m = moment[0]
    old_v = second[0]
    old_l = stat_left[0]
    old_r = stat_right[0]
    new_v = beta_two * old_v + (1.0 - beta_two) * grads * grads
    adam_dir = grads / (jnp.sqrt(new_v / fix_two) + epsilon)
    half = jnp.einsum("sij,sjk->sik", root_left[0], grads, precision=exact)
    shampoo_dir = jnp.einsum("sij,sjk->sik", half, root_right[0], precision=exact)
    is_qkv = my_blocks < first_kind
    adam_sq = jnp.sum(adam_dir * adam_dir, axis=(1, 2)) * filled_f
    shampoo_sq = jnp.sum(shampoo_dir * shampoo_dir, axis=(1, 2)) * filled_f
    sums = [
        jnp.sum(jnp.where(is_qkv, adam_sq, 0.0)),
        jnp.sum(jnp.where(is_qkv, 0.0, adam_sq)),
        jnp.sum(jnp.where(is_qkv, shampoo_sq, 0.0)),
        jnp.sum(jnp.where(is_qkv, 0.0, shampoo_sq)),
    ]
    lane = lax.broadcasted_iota(jnp.int32, (8, 128), 1)
    part = jnp.zeros((8, 128), jnp.float32)
    for n, value in enumerate(sums):
        part = jnp.where(lane == n, value, part)
    total = sum_over(part, ("grp", "dp"), 1)
    graft = jnp.sqrt(total[0, 0:2] / (total[0, 2:4] + graft_floor))
    block_graft = jnp.where(is_qkv, graft[0], graft[1])
    new_m = beta_one * old_m + (1.0 - beta_one) * (block_graft[:, None, None] * shampoo_dir)
    new_w = old_w - learn_rate * (new_m + weight_decay * old_w)
    new_l = beta_stat * old_l + (1.0 - beta_stat) * jnp.einsum(
        "sik,sjk->sij", grads, grads, precision=exact
    )
    new_r = beta_stat * old_r + (1.0 - beta_stat) * jnp.einsum(
        "ski,skj->sij", grads, grads, precision=exact
    )
    master_new = jnp.where(keep, new_w, old_w)
    moment_new = jnp.where(keep, new_m, old_m)
    second_new = jnp.where(keep, new_v, old_v)
    left_new = jnp.where(keep, new_l, old_l)
    right_new = jnp.where(keep, new_r, old_r)
    new_weights = master_new.astype(jnp.bfloat16)
    spread = [new_weights]
    turns = None
    if pairs == 4:
        up = [(d, d + 2) for d in range(groups - 2)]
        down = [(d + 2, d) for d in range(groups - 2)]
        from_low, from_high = [new_weights], [new_weights]
        for k in range(1, pairs):
            from_low.append(lax.ppermute(from_low[-1], "dp", up))
            from_high.append(lax.ppermute(from_high[-1], "dp", down))
        rows = []
        for z in range(pairs):
            found = [(k, 0) for k in range(1, z + 1)] + [(k, 1) for k in range(1, pairs - z)]
            rows.append(sorted(found))
        turns = [[0] * pairs for _ in range(pairs)]
        other = [lax.ppermute(new_weights, "dp", across)]
        for m in range(pairs - 1):
            value = None
            probe = other[-1][0, 0, 0].astype(jnp.float32)
            here = pair + jnp.minimum((probe == probe).astype(jnp.int32), 0)
            for z in range(pairs):
                k, way = rows[z][m]
                turns[z][z + k if way else z - k] = m + 1
                part_w = (from_low, from_high)[way][k]
                value = part_w if value is None else jnp.where(here == z, part_w, value)
            spread.append(value)
            other.append(lax.ppermute(value, "dp", across))
    else:
        for step_off in range(1, pairs):
            hop = [(d, ((d // 2 + step_off) % pairs) * 2 + d % 2) for d in range(groups)]
            spread.append(lax.ppermute(new_weights, "dp", hop))
        other = [lax.ppermute(part_w, "dp", across) for part_w in spread]
    everyone = jnp.concatenate(spread + other)
    place_owner = owner // 2
    turn = lax.rem(pair - place_owner + pairs, pairs)
    if turns is not None:
        turn = jnp.zeros_like(owner)
        for z in range(pairs):
            for origin in range(pairs):
                hit = (pair == z) & (place_owner == origin)
                turn = jnp.where(hit, turns[z][origin], turn)
    held = jnp.where(owner % 2 == side, turn, pairs + turn)
    where_held = held * slot_count + (position - owner * slot_count)
    qkv_weight = join_tiles(everyone, where_held, 0, rows_q, cols_q)
    proj_weight = join_tiles(everyone, where_held, first_kind, rows_p, rows_q)
    qb_new, qm_new, qv_new = adamw(
        qkv_bias, qkv_bias_m, qkv_bias_v, qkv_total / tokens, fix_one, fix_two
    )
    pb_new, pm_new, pv_new = adamw(
        proj_bias, proj_bias_m, proj_bias_v, proj_total / tokens, fix_one, fix_two
    )
    return (
        master_new[None],
        moment_new[None],
        second_new[None],
        left_new[None],
        right_new[None],
        qkv_weight,
        proj_weight,
        qb_new,
        qm_new,
        qv_new,
        pb_new,
        pm_new,
        pv_new,
    )


SIDE = 200
COLUMN = 32
HALF = 16
TILE = 128
HALF_TILES = HALF * SIDE // TILE
TILES = 2 * HALF_TILES
PACE = 2
LAG = 2
CHUNKS = TILES // PACE
ROWS = 208
MOVES = 8
FEW = 3
PLANES = 4
STEPS = 8.0
TOP = 32000.0
MESH = pl.DeviceIdType.MESH
TABLE_ROWS = 16
(
    LEFT_AT,
    RIGHT_AT,
    SOURCE,
    GIVE_AT,
    GIVE_SLOT,
    FROM_SLOT,
    HOLDS,
    KINDS,
    SEEN,
    EDGES,
) = range(10)
MOST = 2


def count_from(value, step, most):
    whole = jnp.zeros_like(value)
    for k in range(step, most, step):
        whole = whole + (value >= k).astype(jnp.int32)
    return whole


def table_kernel(cols_q, rows_q, owner_ref, out):
    me = lax.axis_index("dp")
    total, devices = 2 * COLUMN, 2 * PLANES
    split = cols_q * rows_q

    def grid(rows, columns, axis):
        return lax.broadcasted_iota(jnp.int32, (rows, columns), axis)

    def down(mask, value):
        return jnp.sum(jnp.where(mask, value, 0), axis=0, keepdims=True)

    def over(mask, value):
        return jnp.sum(jnp.where(mask, value, 0), axis=1, keepdims=True)

    def both(mask, value):
        return jnp.sum(over(mask, value), axis=0, keepdims=True)

    sub, lane = grid(total, total, 0), grid(total, total, 1)
    row = owner_ref[...]
    col = over(sub == lane, row)
    slot = over((col == row) & (lane < sub), 1)
    dev = grid(total, devices, 1)
    own = col == dev
    n = down(own, 1)
    dsub, dlane = grid(devices, devices, 0), grid(devices, devices, 1)
    here = grid(1, devices, 1)
    even = (here % 2) == 0

    def turned(value):
        return over(dsub == dlane, value)

    swap = (dsub // 2 == dlane // 2) & (dsub != dlane)
    partner = down(swap, turned(n))
    total0 = over(even, n)
    surplus = jnp.abs(total0 - COLUMN)
    crowded = (even & (total0 >= COLUMN)) | (~even & (total0 < COLUMN))
    room = jnp.where(crowded, jnp.minimum(jnp.minimum(MOVES, n), HALF - partner), 0)
    levels = grid(16, devices, 0)
    filled_to = jnp.sum(jnp.minimum(room, levels), axis=1, keepdims=True)
    fits = (filled_to <= surplus) & (grid(16, 1, 0) <= MOVES)
    level = jnp.sum(fits.astype(jnp.int32), axis=0, keepdims=True) - 1
    base = jnp.minimum(room, level)
    rest = surplus - jnp.sum(base, axis=1, keepdims=True)
    can = (room > level).astype(jnp.int32)
    before = down(dsub < dlane, turned(can))
    move = base + jnp.where((can > 0) & (before < rest), 1, 0)
    stay = n - move
    height = stay + down(swap, turned(move))
    start = down((dsub < dlane) & (dsub % 2 == dlane % 2), turned(height))
    far = down(swap, turned(start)) + partner - stay
    moved = slot >= over(own, stay)
    place = jnp.where(moved, over(own, far), over(own, start)) + slot
    parity = over(own, here % 2)
    column = jnp.where(moved, 1 - parity, parity)
    line = column * COLUMN + place
    side = me % 2
    mine = here == me
    my_n, my_stay, my_start = over(mine, n), over(mine, stay), over(mine, start)
    my_height = over(mine, height)
    spots = grid(1, total, 1)
    wanted = spots + side * COLUMN
    wanted = jnp.where(wanted >= total, wanted - total, wanted)
    at = down(line == wanted, sub)
    later = jnp.maximum(at - split, 0)
    first = at < split
    at_row, later_row = count_from(at, cols_q, split), count_from(later, rows_q, total - split)
    left_at = jnp.where(first, at_row, rows_q + later_row)
    right_at = jnp.where(first, at - at_row * cols_q, cols_q + later - later_row * rows_q)
    my_blocks = down((col == me) & (slot == lane), sub)
    source = jnp.where(spots < my_stay, my_start + spots, COLUMN + spots - my_stay)
    source = jnp.where(spots < my_n, jnp.minimum(source, COLUMN + MOVES - 1), 0)
    give_at = jnp.minimum(my_start + my_n + spots, COLUMN - 1)
    give_slot = jnp.minimum(my_stay + spots, HALF - 1)
    spot = spots - my_start
    from_slot = jnp.where(spot < my_stay, spot, jnp.where(my_n > my_stay, 0, HALF + spot - my_n))
    from_slot = jnp.minimum(jnp.maximum(from_slot, 0), HALF + MOVES - 1)
    seen = jnp.where(column == side, place, COLUMN + place)
    edges = jnp.where(spots == 0, my_start, my_start + my_height) * SIDE
    most = jnp.max(move, axis=1, keepdims=True)
    edges = jnp.where(spots == MOST, most, edges)
    rows = {
        LEFT_AT: left_at,
        RIGHT_AT: right_at,
        SOURCE: source,
        GIVE_AT: give_at,
        GIVE_SLOT: give_slot,
        FROM_SLOT: from_slot,
        HOLDS: (spots < my_n).astype(jnp.int32),
        KINDS: (my_blocks < split).astype(jnp.int32),
        SEEN: down(sub == lane, seen),
        EDGES: edges,
    }
    out[...] = jnp.zeros_like(out)
    for n, value in rows.items():
        out[n : n + 1, :total] = value


def layout_tables(owner, cols_q, rows_q):
    return pl.pallas_call(
        lambda *refs: table_kernel(cols_q, rows_q, *refs),
        out_shape=jax.ShapeDtypeStruct((TABLE_ROWS, TILE), jnp.int32),
        in_specs=[vmem()],
        out_specs=vmem(),
    )(owner.reshape(1, -1))


def pack(value):
    top = jnp.max(jnp.abs(value), axis=1, keepdims=True)
    code = jnp.ceil(jnp.log(jnp.maximum(top, 1e-30)) * (STEPS / LN2))
    scale = TOP / jnp.exp(code * (LN2 / STEPS))
    whole = jnp.round(value * scale).astype(jnp.int32)
    codes = jnp.broadcast_to(
        code.astype(jnp.int32), (value.shape[0], ROWS - SIDE, value.shape[2])
    )
    return jnp.concatenate([whole, codes], axis=1).astype(jnp.int16)


def unpack(coded):
    wide = coded.astype(jnp.int32).astype(jnp.float32)
    scale = jnp.exp(wide[:, SIDE : SIDE + 1] * (LN2 / STEPS)) * (1.0 / TOP)
    return wide[:, :SIDE] * scale


LN2 = 0.6931471805599453


def some(k):
    return pl.ds(k * PACE, PACE)


def pieces(j):
    low, high = j * SIDE, (j + 1) * SIDE
    for tile in range(low // TILE, -(-high // TILE)):
        a, b = max(low, tile * TILE), min(high, (tile + 1) * TILE)
        yield tile, slice(a - tile * TILE, b - tile * TILE), slice(a - low, b - low)


def tiles_of(moves):
    return -(-moves * SIDE // TILE)


def put(into, base, j, value):
    for tile, there, here in pieces(j):
        into[base + tile, :SIDE, there] = value[:, here]


def take(ref, base, j, into, n):
    for tile, there, here in pieces(j):
        into[n, :, here] = ref[base + tile, :SIDE, there]


def greet(peers):
    barrier = pltpu.get_barrier_semaphore()
    count = 0
    for condition, device in peers:
        if condition is None:
            pl.semaphore_signal(barrier, inc=1, device_id=device, device_id_type=MESH)
            count = count + 1
        else:

            @pl.when(condition)
            def _():
                pl.semaphore_signal(barrier, inc=1, device_id=device, device_id_type=MESH)

            count = count + condition.astype(jnp.int32)
    pl.semaphore_wait(barrier, count)


def remote(src, dst, send, recv, device):
    return pltpu.make_async_remote_copy(
        src_ref=src, dst_ref=dst, send_sem=send, recv_sem=recv, device_id=device, device_id_type=MESH
    )


def loop(low, high, body):
    lax.fori_loop(low, high, lambda k, carry: (body(k), carry)[1], 0)


def reduce_kernel(
    tokens,
    moves,
    table,
    x_blocks,
    attn_blocks,
    qkv_blocks,
    out_blocks,
    out,
    sums,
    left,
    right,
    stage,
    pair,
    sent_x,
    got_x,
    sent_up,
    got_up,
    sent_down,
    got_down,
    tiles,
    stage_m,
    sent_m,
    got_m,
    sems,
    sems_m,
    load_sems,
):
    me = lax.axis_index("dp")
    loads = []
    for into, parts in ((left, (x_blocks, attn_blocks)), (right, (qkv_blocks, out_blocks))):
        at = 0
        for ref in parts:
            there = into.at[pl.ds(at, ref.shape[0])]
            loads.append(pltpu.make_async_copy(ref, there, load_sems.at[len(loads)]))
            loads[-1].start()
            at += ref.shape[0]
    z, side = me // 2, me % 2
    across = {"dp": me + 1 - 2 * side}
    upper = {"dp": jnp.minimum(me + 2, 2 * PLANES - 1)}
    lower = {"dp": jnp.maximum(me - 2, 0)}
    last = PLANES - 1
    greet([(None, across), (z < last, upper), (z > 0, lower)])
    for load in loads:
        load.wait()

    def copy_x(k):
        return remote(
            sent_x.at[some(k)], got_x.at[some(k)], sems.at[0, k], sems.at[1, k], across
        )

    def copy_up(k):
        return remote(
            sent_up.at[some(k)], got_up.at[some(k)], sems.at[2, k], sems.at[3, k], upper
        )

    def copy_down(k):
        return remote(
            sent_down.at[some(k)], got_down.at[some(k)], sems.at[4, k], sems.at[5, k], lower
        )

    def product(n):
        return lax.dot_general(
            left[table[LEFT_AT, n]],
            right[table[RIGHT_AT, n]],
            (((1,), (1,)), ((), ())),
            preferred_element_type=jnp.float32,
        )

    def send_other(low, high):
        def body(k):
            sent_x[some(k)] = pack(stage[some(k)])
            copy_x(k).start()

        loop(low, high, body)

    def other_part(h, part):
        for j in range(part * 4, part * 4 + 4):
            put(stage, h * HALF_TILES, j, product(COLUMN + h * HALF + j))
        edge = (h * HALF + part * 4) * SIDE
        send_other(edge // (TILE * PACE), (edge + 4 * SIDE) // (TILE * PACE))

    def own_part(h, part):
        for j in range(part * 4, part * 4 + 4):
            put(pair, h * HALF_TILES, j, product(h * HALF + j))

    for part in range(4):
        other_part(0, part)
    for part in range(4):
        own_part(0, part)

    def bias_sums():
        ones = jnp.ones((8, right.shape[2]), jnp.bfloat16)
        sums[...] = jnp.zeros_like(sums)
        for j in range(right.shape[0]):
            total = lax.dot_general(
                ones, right[j], (((1,), (1,)), ((), ())), preferred_element_type=jnp.float32
            )
            sums[j : j + 1, :SIDE] = total[:1]

    def step(t):
        for part in range(4):
            pl.when(t == part)(lambda part=part: other_part(1, part))
        for part in range(4):
            pl.when(t == 4 + part)(lambda part=part: own_part(1, part))
        pl.when(t == 8)(bias_sums)

        @pl.when(t < CHUNKS)
        def _():
            copy_x(t).wait_recv()
            pair[some(t)] += unpack(got_x[some(t)])

        up = t - LAG * z

        @pl.when((up >= 0) & (up < CHUNKS))
        def _():
            @pl.when(z == 0)
            def _():
                sent_up[some(up)] = pack(pair[some(up)])

            @pl.when(z > 0)
            def _():
                copy_up(up).wait_recv()

                @pl.when(z < last)
                def _():
                    sent_up[some(up)] = pack(pair[some(up)] + unpack(got_up[some(up)]))

            @pl.when(z < last)
            def _():
                copy_up(up).start()

        down = t - LAG * (last - z)

        @pl.when((down >= 0) & (down < CHUNKS))
        def _():
            @pl.when(z == last)
            def _():
                sent_down[some(down)] = pack(pair[some(down)])

            @pl.when(z < last)
            def _():
                copy_down(down).wait_recv()

                @pl.when(z > 0)
                def _():
                    sent_down[some(down)] = pack(pair[some(down)] + unpack(got_down[some(down)]))

            @pl.when(z > 0)
            def _():
                copy_down(down).start()

        full = t - LAG * last

        @pl.when(full >= 0)
        def _():
            @pl.when(z > 0)
            def _():
                pair[some(full)] += unpack(got_up[some(full)])

            @pl.when(z < last)
            def _():
                pair[some(full)] += unpack(got_down[some(full)])

            @pl.when((full == HALF_TILES // PACE) | (full == CHUNKS - 1))
            def _():
                h = (full == CHUNKS - 1).astype(jnp.int32)
                for j in range(HALF):
                    take(pair, h * HALF_TILES, j, tiles, h * HALF + j)

    loop(0, CHUNKS + LAG * last, step)

    stage_m[tiles_of(moves) - 1] = jnp.zeros((SIDE, TILE), jnp.float32)
    for k in range(moves):
        put(stage_m, 0, k, tiles[table[GIVE_AT, k]])
    sent_m[...] = pack(stage_m[...])
    move = remote(sent_m, got_m, sems_m.at[0], sems_m.at[1], across)
    move.start()

    def drain(k):
        copy_x(k).wait_send()

        @pl.when(z < last)
        def _():
            copy_up(k).wait_send()

        @pl.when(z > 0)
        def _():
            copy_down(k).wait_send()

    loop(0, CHUNKS, drain)
    move.wait()
    stage_m[...] = unpack(got_m[...])
    for k in range(moves):
        take(stage_m, 0, k, tiles, COLUMN + k)

    def finish(s):
        out[s] = jnp.where(
            table[HOLDS, s] > 0, tiles[jnp.minimum(table[SOURCE, s], COLUMN + moves - 1)] * (1.0 / tokens), 0.0
        )

    loop(0, HALF, finish)


def vmem():
    return pl.BlockSpec(memory_space=pltpu.VMEM)


def smem():
    return pl.BlockSpec(memory_space=pltpu.SMEM)


def hbm():
    return pl.BlockSpec(memory_space=pl.ANY)


def reduce_tiles(table, x_blocks, attn_blocks, qkv_blocks, out_blocks, tokens, moves):
    coded = pltpu.VMEM((TILES, ROWS, TILE), jnp.int16)
    moved = pltpu.VMEM((tiles_of(moves), ROWS, TILE), jnp.int16)
    depth = x_blocks.shape[2]
    rows = x_blocks.shape[0] + attn_blocks.shape[0]
    cols = qkv_blocks.shape[0] + out_blocks.shape[0]
    return pl.pallas_call(
        lambda *refs: reduce_kernel(tokens, moves, *refs),
        out_shape=(
            pltpu.VMEM((HALF, SIDE, SIDE), jnp.float32),
            pltpu.VMEM((BIAS_ROWS, SMALL_WIDE), jnp.float32),
        ),
        in_specs=[smem()] + [hbm()] * 4,
        out_specs=[vmem()] * 2,
        scratch_shapes=[
            pltpu.VMEM((rows, SIDE, depth), jnp.bfloat16),
            pltpu.VMEM((cols, SIDE, depth), jnp.bfloat16),
            pltpu.VMEM((TILES, SIDE, TILE), jnp.float32),
            pltpu.VMEM((TILES, SIDE, TILE), jnp.float32),
            *([coded] * 6),
            pltpu.VMEM((COLUMN + moves, SIDE, SIDE), jnp.float32),
            pltpu.VMEM((tiles_of(moves), SIDE, TILE), jnp.float32),
            moved,
            moved,
            pltpu.SemaphoreType.DMA((6, CHUNKS)),
            pltpu.SemaphoreType.DMA((2,)),
            pltpu.SemaphoreType.DMA((4,)),
        ],
        compiler_params=pltpu.CompilerParams(
            collective_id=0 if moves == MOVES else 2,
            has_side_effects=True,
            vmem_limit_bytes=VMEM_LIMIT,
        ),
    )(table, x_blocks, attn_blocks, qkv_blocks, out_blocks)


VMEM_LIMIT = 44 * 1024 * 1024
STEP_LIMIT = 26 * 1024 * 1024
LAST_LIMIT = 16 * 1024 * 1024
EARLY = 10
FEW_EARLY = 4
SMALL_ROWS = 24
BIAS_ROWS = 16
SMALL_WIDE = 256


def dot3(a, b, dims):
    a_high, b_high = a.astype(jnp.bfloat16), b.astype(jnp.bfloat16)
    a_low = (a - a_high.astype(jnp.float32)).astype(jnp.bfloat16)
    b_low = (b - b_high.astype(jnp.float32)).astype(jnp.bfloat16)

    def dot(p, q):
        return lax.dot_general(p, q, (dims, ((), ())), preferred_element_type=jnp.float32)

    return dot(a_high, b_high) + (dot(a_high, b_low) + dot(a_low, b_high))


def step_kernel(
    moves,
    table,
    fixes,
    grads,
    small,
    master,
    moment,
    second,
    stat_left,
    stat_right,
    root_left,
    root_right,
    state_w,
    state_m,
    state_v,
    state_l,
    state_r,
    small_out,
    blocks,
    state_a,
    state_b,
    sums,
    sums_dp,
    sums_grp,
    light,
    sent_m,
    got_m,
    own,
    got_up,
    got_down,
    known,
    got_x,
    load_sems,
    sum_sems,
    grp_sems,
    move_sems,
    sems,
):
    me = lax.axis_index("dp")
    z, side = me // 2, me % 2
    n_dp, n_grp = lax.axis_size("dp"), lax.axis_size("grp")
    my_grp = lax.axis_index("grp")
    across = {"dp": me + 1 - 2 * side}
    upper = {"dp": jnp.minimum(me + 2, 2 * PLANES - 1)}
    lower = {"dp": jnp.maximum(me - 2, 0)}
    last = PLANES - 1
    held = [state_v, state_a, state_b, state_w, state_m, state_l, state_r]
    given = [second, root_left, root_right, master, moment, stat_left, stat_right]
    loads = []
    for n, (ref, scratch) in enumerate(zip(given, held)):
        copy = pltpu.make_async_copy(ref.at[0], scratch, load_sems.at[n])
        copy.start()
        loads.append(copy)

    peers = [(None, {"dp": lax.rem(me + k, n_dp)}) for k in range(1, n_dp)]
    peers += [(None, {"grp": lax.rem(my_grp + k, n_grp)}) for k in range(1, n_grp)]
    greet(peers)

    early = EARLY if moves == MOVES else FEW_EARLY
    fix_two = fixes[0]
    for copy in loads[:3]:
        copy.wait()

    def direction(s, sums_now):
        adam_q, adam_p, shampoo_q, shampoo_p = sums_now
        grad = grads[s]
        old = state_v[s]
        new = beta_two * old + (1.0 - beta_two) * grad * grad
        adam = grad / (jnp.sqrt(new / fix_two) + epsilon)
        half = dot3(state_a[s], grad, ((1,), (0,)))
        shampoo = dot3(half, state_b[s], ((1,), (0,)))
        state_v[s] = jnp.where(table[HOLDS, s] > 0, new, old)
        state_a[s] = shampoo
        adam_sq = jnp.sum(adam * adam, axis=0, keepdims=True)
        shampoo_sq = jnp.sum(shampoo * shampoo, axis=0, keepdims=True)
        q = table[KINDS, s] > 0
        return (
            adam_q + jnp.where(q, adam_sq, 0.0),
            adam_p + jnp.where(q, 0.0, adam_sq),
            shampoo_q + jnp.where(q, shampoo_sq, 0.0),
            shampoo_p + jnp.where(q, 0.0, shampoo_sq),
        )

    nothing = jnp.zeros((1, SIDE), jnp.float32)
    parts = lax.fori_loop(0, HALF, direction, (nothing,) * 4, unroll=4)
    sums[0, :BIAS_ROWS] = small[...]
    row = lax.broadcasted_iota(jnp.int32, (SMALL_ROWS - BIAS_ROWS, SMALL_WIDE), 0)
    packed = jnp.zeros((SMALL_ROWS - BIAS_ROWS, SMALL_WIDE), jnp.float32)
    for n, part in enumerate(parts):
        packed = jnp.where(row == n, jnp.sum(part), packed)
    sums[0, BIAS_ROWS:] = packed

    copies = []
    for k in range(1, n_dp):
        copy = remote(
            sums.at[0], sums_dp.at[k - 1], sum_sems.at[0, k - 1], sum_sems.at[1, k - 1],
            {"dp": lax.rem(me + k, n_dp)},
        )
        copy.start()
        copies.append(copy)
    for copy in loads[3:5]:
        copy.wait()
    for copy in copies:
        copy.wait()
    for d in range(n_dp):
        value = jnp.where(me == d, sums[0], sums_dp[lax.rem(me - d + n_dp + n_dp - 1, n_dp) % (n_dp - 1)])
        total = value if d == 0 else total + value
    small_out[...] = total[:BIAS_ROWS]
    sums_grp[my_grp] = total[BIAS_ROWS:]
    copies = []
    for k in range(1, n_grp):
        copy = remote(
            sums_grp.at[my_grp], sums_grp.at[my_grp], grp_sems.at[0, k - 1], grp_sems.at[1, k - 1],
            {"grp": lax.rem(my_grp + k, n_grp)},
        )
        copy.start()
        copies.append(copy)
    for copy in copies:
        copy.wait()
    total = sums_grp[0]
    for g in range(1, n_grp):
        total = total + sums_grp[g]
    graft_q = jnp.sqrt(total[0:1] / (total[2:3] + graft_floor))[:, :1]
    graft_p = jnp.sqrt(total[1:2] / (total[3:4] + graft_floor))[:, :1]

    def update(s):
        graft = jnp.where(table[KINDS, s] > 0, graft_q, graft_p)
        old_m, old_w = state_m[s], state_w[s]
        new_m = beta_one * old_m + (1.0 - beta_one) * (graft * state_a[s])
        new_w = old_w - learn_rate * (new_m + weight_decay * old_w)
        state_m[s] = jnp.where(table[HOLDS, s] > 0, new_m, old_m)
        state_w[s] = jnp.where(table[HOLDS, s] > 0, new_w, old_w)
        light[s] = jnp.where(table[KINDS, s] > 0, new_w.T, new_w).astype(jnp.bfloat16)

    loop(0, HALF, update)

    sent_m[...] = jnp.zeros_like(sent_m)
    for k in range(moves):
        put(sent_m, 0, k, light[table[GIVE_SLOT, k]])
    move = remote(sent_m, got_m, move_sems.at[0], move_sems.at[1], across)
    move.start()

    for copy in loads[5:7]:
        copy.wait()

    def stats(s):
        grad = grads[s]
        keep = table[HOLDS, s] > 0
        new_l = beta_stat * state_l[s] + (1.0 - beta_stat) * dot3(grad, grad, ((1,), (1,)))
        new_r = beta_stat * state_r[s] + (1.0 - beta_stat) * dot3(grad, grad, ((0,), (0,)))
        state_l[s] = jnp.where(keep, new_l, state_l[s])
        state_r[s] = jnp.where(keep, new_r, state_r[s])

    loop(0, early, stats)
    move.wait()
    for k in range(moves):
        take(got_m, 0, k, light, HALF + k)

    def fill(h):
        for j in range(HALF):
            put(own, h * HALF_TILES, j, light[jnp.minimum(table[FROM_SLOT, h * HALF + j], HALF + moves - 1)])

    def pad(k):
        own[k, SIDE:] = jnp.zeros((ROWS - SIDE, TILE), jnp.bfloat16)

    loop(0, TILES, pad)
    loop(0, 2, fill)

    low, high = table[EDGES, 0], table[EDGES, 1]
    shape = (PACE, ROWS, TILE)
    lane = lax.broadcasted_iota(jnp.int32, shape, 0) * TILE + lax.broadcasted_iota(
        jnp.int32, shape, 2
    )
    up_window = -(-HALF_TILES // PACE)
    down_window = HALF_TILES // PACE

    def wide(ref, k):
        return ref[some(k)].astype(jnp.float32)

    def copy_up(k, src):
        return remote(src.at[some(k)], got_up.at[some(k)], sems.at[0, k], sems.at[1, k], upper)

    def copy_down(k, src):
        return remote(src.at[some(k)], got_down.at[some(k)], sems.at[2, k], sems.at[3, k], lower)

    def copy_x(k):
        return remote(known.at[some(k)], got_x.at[some(k)], sems.at[4, k], sems.at[5, k], across)

    def step(t):
        up = t - LAG * z

        @pl.when((up >= 0) & (up < CHUNKS))
        def _():
            @pl.when((z == 0) & (up < up_window))
            def _():
                copy_up(up, own).start()

            @pl.when(z > 0)
            def _():
                @pl.when((z > 1) | (up < up_window))
                def _():
                    copy_up(up, own).wait_recv()
                    mask = lane + up * (PACE * TILE) < low
                    got_up[some(up)] = jnp.where(mask, wide(got_up, up), wide(own, up)).astype(
                        jnp.bfloat16
                    )

                @pl.when((z == 1) & (up >= up_window))
                def _():
                    got_up[some(up)] = own[some(up)]

                @pl.when(z < last)
                def _():
                    copy_up(up, got_up).start()

        down = t - LAG * (last - z)

        @pl.when((down >= 0) & (down < CHUNKS))
        def _():
            @pl.when((z == last) & (down >= down_window))
            def _():
                copy_down(down, own).start()

            @pl.when(z < last)
            def _():
                @pl.when((z < last - 1) | (down >= down_window))
                def _():
                    copy_down(down, own).wait_recv()
                    mask = lane + down * (PACE * TILE) >= high
                    got_down[some(down)] = jnp.where(
                        mask, wide(got_down, down), wide(own, down)
                    ).astype(jnp.bfloat16)

                @pl.when((z == last - 1) & (down < down_window))
                def _():
                    got_down[some(down)] = own[some(down)]

                @pl.when(z > 0)
                def _():
                    copy_down(down, got_down).start()

        full = t - LAG * last

        @pl.when(full >= 0)
        def _():
            place = lane + full * (PACE * TILE)
            value = jnp.where(place < low, wide(got_up, full), wide(own, full))
            value = jnp.where(place >= high, wide(got_down, full), value)
            known[some(full)] = value.astype(jnp.bfloat16)
            copy_x(full).start()

            @pl.when((full == HALF_TILES // PACE) | (full == CHUNKS - 1))
            def _():
                h = (full == CHUNKS - 1).astype(jnp.int32)
                for j in range(HALF):
                    take(known, h * HALF_TILES, j, blocks, h * HALF + j)

        @pl.when(t < HALF - early)
        def _():
            stats(early + t)

    loop(0, CHUNKS + LAG * last, step)
    for h in range(2):
        loop(0 if h == 0 else up_window, up_window if h == 0 else CHUNKS, lambda k: copy_x(k).wait_recv())
        for j in range(HALF):
            take(got_x, h * HALF_TILES, j, blocks, COLUMN + h * HALF + j)

    def drain(k):
        copy_x(k).wait_send()

        @pl.when((z == 1) | (z == 2) | ((z == 0) & (k < up_window)))
        def _():
            copy_up(k, own).wait_send()

        @pl.when((z == 1) | (z == 2) | ((z == last) & (k >= down_window)))
        def _():
            copy_down(k, own).wait_send()

    loop(0, CHUNKS, drain)


def apply_step(table, fixes, grads, small, states, moves):
    n_dp, n_grp = lax.axis_size("dp"), lax.axis_size("grp")
    held = pltpu.VMEM((HALF, SIDE, SIDE), jnp.float32)
    line = pltpu.VMEM((TILES, ROWS, TILE), jnp.bfloat16)
    moved = pltpu.VMEM((tiles_of(moves), ROWS, TILE), jnp.bfloat16)
    return pl.pallas_call(
        lambda *refs: step_kernel(moves, *refs),
        out_shape=(
            *([held] * 5),
            jax.ShapeDtypeStruct((BIAS_ROWS, SMALL_WIDE), jnp.float32),
            pltpu.VMEM((2 * COLUMN, SIDE, SIDE), jnp.bfloat16),
        ),
        in_specs=[smem()] * 2 + [vmem()] * 2 + [hbm()] * 7,
        out_specs=[vmem()] * 7,
        scratch_shapes=[
            *([held] * 2),
            pltpu.VMEM((1, SMALL_ROWS, SMALL_WIDE), jnp.float32),
            pltpu.VMEM((n_dp - 1, SMALL_ROWS, SMALL_WIDE), jnp.float32),
            pltpu.VMEM((n_grp, SMALL_ROWS - BIAS_ROWS, SMALL_WIDE), jnp.float32),
            pltpu.VMEM((HALF + MOVES, SIDE, SIDE), jnp.bfloat16),
            moved,
            moved,
            *([line] * 5),
            pltpu.SemaphoreType.DMA((7,)),
            pltpu.SemaphoreType.DMA((2, n_dp - 1)),
            pltpu.SemaphoreType.DMA((2, n_grp - 1)),
            pltpu.SemaphoreType.DMA((2,)),
            pltpu.SemaphoreType.DMA((6, CHUNKS)),
        ],
        compiler_params=pltpu.CompilerParams(
            collective_id=1 if moves == MOVES else 3,
            has_side_effects=True,
            vmem_limit_bytes=STEP_LIMIT,
        ),
    )(table, fixes, grads, small, *states)


def finish_kernel(cols_q, rows_q, rows_p, table, blocks, *refs):
    given, kept = refs[:5], refs[5:10]
    qkv, proj, bands, copy_sems, band_sems = refs[10:]
    stores = []
    for n, (ref, into) in enumerate(zip(given, kept)):
        stores.append(pltpu.make_async_copy(ref, into.at[0], copy_sems.at[n]))
        stores[-1].start()
    for n in range(cols_q + rows_p):
        first, stride = (n, cols_q) if n < cols_q else (cols_q * rows_q + (n - cols_q) * rows_q, 1)
        parts = [
            blocks[table[SEEN, first + k * stride]].astype(jnp.float32) for k in range(rows_q)
        ]
        bands[n] = jnp.concatenate(parts, axis=1).astype(jnp.bfloat16)
        into = qkv.at[n] if n < cols_q else proj.at[n - cols_q]
        stores.append(pltpu.make_async_copy(bands.at[n], into, band_sems.at[n]))
        stores[-1].start()
    for copy in stores:
        copy.wait()


def finish(blocks, table, states, rows_q, cols_q, rows_p):
    across = rows_q * SIDE
    state = jax.ShapeDtypeStruct((1, HALF, SIDE, SIDE), jnp.float32)
    return pl.pallas_call(
        lambda *refs: finish_kernel(cols_q, rows_q, rows_p, *refs),
        out_shape=(
            *([state] * 5),
            jax.ShapeDtypeStruct((cols_q, SIDE, across), jnp.bfloat16),
            jax.ShapeDtypeStruct((rows_p, SIDE, across), jnp.bfloat16),
        ),
        in_specs=[smem()] + [vmem()] * 6,
        out_specs=[hbm()] * 7,
        scratch_shapes=[
            pltpu.VMEM((cols_q + rows_p, SIDE, across), jnp.bfloat16),
            pltpu.SemaphoreType.DMA((5,)),
            pltpu.SemaphoreType.DMA((cols_q + rows_p,)),
        ],
        compiler_params=pltpu.CompilerParams(vmem_limit_bytes=LAST_LIMIT),
    )(table, blocks, *states)


def on_device(
    x_in,
    attn_in,
    grad_qkv,
    grad_out,
    owner,
    step,
    master,
    moment,
    second,
    stat_left,
    stat_right,
    root_left,
    root_right,
    qkv_bias,
    qkv_bias_m,
    qkv_bias_v,
    proj_bias,
    proj_bias_m,
    proj_bias_v,
):
    groups = lax.axis_size("dp")
    slot_count, side = master.shape[1], master.shape[2]
    if (groups, slot_count, side, owner.shape[0]) != (2 * PLANES, HALF, SIDE, 2 * COLUMN):
        return on_device_any(
            x_in, attn_in, grad_qkv, grad_out, owner, step, master, moment, second, stat_left, stat_right,
            root_left, root_right, qkv_bias, qkv_bias_m, qkv_bias_v, proj_bias, proj_bias_m, proj_bias_v,
        )
    depth = x_in.shape[0]
    tokens = depth * groups
    rows_q = D // SIDE
    cols_q = grad_qkv.shape[1] // SIDE
    rows_p = attn_in.shape[1] // SIDE
    count_f = step[0].astype(jnp.float32)
    fix_one = 1.0 - jnp.power(jnp.float32(beta_one), count_f)
    fix_two = 1.0 - jnp.power(jnp.float32(beta_two), count_f)
    table = layout_tables(owner, cols_q, rows_q)
    tiles = (
        x_in.T.reshape(rows_q, SIDE, depth),
        attn_in.T.reshape(rows_p, SIDE, depth),
        grad_qkv.T.reshape(cols_q, SIDE, depth),
        grad_out.T.reshape(rows_q, SIDE, depth),
    )
    states = (master, moment, second, stat_left, stat_right, root_left, root_right)
    fixes = fix_two.reshape(1)

    def path(moves):
        def run(table, fixes, tiles, states):
            grads, small = reduce_tiles(table, *tiles, tokens, moves)
            *stepped, small_sum, blocks = apply_step(table, fixes, grads, small, states, moves)
            return *finish(blocks, table, stepped, rows_q, cols_q, rows_p), small_sum

        return run

    few = table[EDGES, MOST] <= FEW
    *stepped, qkv, proj, small_sum = lax.cond(
        few, path(FEW), path(MOVES), table, fixes, tiles, states
    )
    master_new, moment_new, second_new, left_new, right_new = stepped
    qkv_weight = qkv.reshape(cols_q * SIDE, rows_q * SIDE).T
    proj_weight = proj.reshape(rows_p * SIDE, rows_q * SIDE)
    qkv_total = small_sum[:cols_q, :SIDE].reshape(-1)
    proj_total = small_sum[cols_q : cols_q + rows_q, :SIDE].reshape(-1)
    qb_new, qm_new, qv_new = adamw(
        qkv_bias, qkv_bias_m, qkv_bias_v, qkv_total / tokens, fix_one, fix_two
    )
    pb_new, pm_new, pv_new = adamw(
        proj_bias, proj_bias_m, proj_bias_v, proj_total / tokens, fix_one, fix_two
    )
    return (
        master_new,
        moment_new,
        second_new,
        left_new,
        right_new,
        qkv_weight,
        proj_weight,
        qb_new,
        qm_new,
        qv_new,
        pb_new,
        pm_new,
        pv_new,
    )


def solution(mesh):
    return jax.shard_map(
        on_device,
        mesh=mesh,
        in_specs=(
            P("dp", None),
            P("dp", "grp"),
            P("dp", "grp"),
            P("dp", None),
            P(),
            P(),
            P("grp", "dp", None, None),
            P("grp", "dp", None, None),
            P("grp", "dp", None, None),
            P("grp", "dp", None, None),
            P("grp", "dp", None, None),
            P("grp", "dp", None, None),
            P("grp", "dp", None, None),
            P("grp"),
            P("grp"),
            P("grp"),
            P(),
            P(),
            P(),
        ),
        out_specs=(
            P("grp", "dp", None, None),
            P("grp", "dp", None, None),
            P("grp", "dp", None, None),
            P("grp", "dp", None, None),
            P("grp", "dp", None, None),
            P(None, "grp"),
            P("grp", None),
            P("grp"),
            P("grp"),
            P("grp"),
            P(),
            P(),
            P(),
        ),
        check_vma=False,
    )
```

```python
import jax
import jax.numpy as jnp
from jax import lax
from jax.experimental import pallas as pl
from jax.experimental.pallas import tpu as pltpu
from jax.sharding import PartitionSpec as P

D = 1600


beta_one = 0.9
beta_two = 0.95
beta_stat = 0.9
learn_rate = 0.02
weight_decay = 0.1
epsilon = 1e-08
graft_floor = 1e-06


def positions(owner, slot_count):
    total_blocks = owner.shape[0]
    blocks = jnp.arange(total_blocks, dtype=jnp.int32)
    same_owner = owner[None, :] == owner[:, None]
    earlier = blocks[None, :] < blocks[:, None]
    slot_rank = jnp.sum(jnp.where(same_owner & earlier, 1, 0).astype(jnp.int32), axis=1)
    return owner * slot_count + slot_rank


def adamw(param, first_m, second_m, grad, fix_one, fix_two):
    new_m = beta_one * first_m + (1.0 - beta_one) * grad
    new_v = beta_two * second_m + (1.0 - beta_two) * grad * grad
    new_p = param - learn_rate * (new_m / fix_one) / (jnp.sqrt(new_v / fix_two) + epsilon)
    return (new_p, new_m, new_v)


def place_kernel(
    split, cols_q, rows_q, slots, holder_ref, used_ref, left_ref, right_ref, tile_ref, peak_ref
):
    o = pl.program_id(0)
    peak_ref[...] = jnp.zeros_like(peak_ref)
    side = left_ref.shape[1]
    for s in range(slots):
        b = holder_ref[o * slots + s]

        @pl.when(used_ref[o * slots + s] > 0)
        def _():
            first = b < split
            later = jnp.maximum(b - split, 0)
            i = jnp.where(first, b // cols_q, rows_q + later // rows_q)
            j = jnp.where(first, b % cols_q, cols_q + later % rows_q)
            tile = lax.dot_general(
                left_ref[i],
                right_ref[j],
                (((1,), (1,)), ((), ())),
                preferred_element_type=jnp.float32,
            )
            tile_ref[0, :, s * side : (s + 1) * side] = tile
            peak_ref[0, s : s + 1, :] = jnp.full((1, 128), jnp.max(jnp.abs(tile)), jnp.float32)


def place_tiles(left, right, holder, used, split, cols_q, rows_q, groups, slots):
    side, depth = left.shape[1:]
    return pl.pallas_call(
        lambda *refs: place_kernel(split, cols_q, rows_q, slots, *refs),
        out_shape=(
            jax.ShapeDtypeStruct((groups, side, slots * side), jnp.float32),
            jax.ShapeDtypeStruct((groups, slots, 128), jnp.float32),
        ),
        grid_spec=pltpu.PrefetchScalarGridSpec(
            num_scalar_prefetch=2,
            grid=(groups,),
            in_specs=[
                pl.BlockSpec(left.shape, lambda o, h, u: (0, 0, 0)),
                pl.BlockSpec(right.shape, lambda o, h, u: (0, 0, 0)),
            ],
            out_specs=[
                pl.BlockSpec((1, side, slots * side), lambda o, h, u: (o, 0, 0)),
                pl.BlockSpec((1, slots, 128), lambda o, h, u: (o, 0, 0)),
            ],
        ),
        compiler_params=pltpu.CompilerParams(vmem_limit_bytes=32 * 1024 * 1024),
    )(holder, used, left, right)


def join_kernel(count, pos_ref, *refs):
    out_ref = refs[count]
    parts = [refs[k][0].astype(jnp.float32) for k in range(count)]
    out_ref[...] = jnp.concatenate(parts, axis=1).astype(out_ref.dtype)


def join_tiles(tiles, position, base, rows, cols):
    side = tiles.shape[1]

    def spot(k):
        return lambda r, pos: (pos[base + r * cols + k], 0, 0)

    return pl.pallas_call(
        lambda *refs: join_kernel(cols, *refs),
        out_shape=jax.ShapeDtypeStruct((rows * side, cols * side), tiles.dtype),
        grid_spec=pltpu.PrefetchScalarGridSpec(
            num_scalar_prefetch=1,
            grid=(rows,),
            in_specs=[pl.BlockSpec((1, side, side), spot(k)) for k in range(cols)],
            out_specs=pl.BlockSpec((side, cols * side), lambda r, pos: (r, 0)),
        ),
        compiler_params=pltpu.CompilerParams(vmem_limit_bytes=32 * 1024 * 1024),
    )(position, *([tiles] * cols))


def sum_kernel(axes, sizes, in_ref, out_ref, *scratch):
    buffers = scratch[: len(axes)]
    send_sems = scratch[len(axes) : 2 * len(axes)]
    recv_sems = scratch[2 * len(axes) :]
    barrier = pltpu.get_barrier_semaphore()
    for axis, size in zip(axes, sizes):
        me = lax.axis_index(axis)
        for k in range(1, size):
            pl.semaphore_signal(
                barrier,
                inc=1,
                device_id={axis: lax.rem(me + k, size)},
                device_id_type=pl.DeviceIdType.MESH,
            )
    pl.semaphore_wait(barrier, sum(size - 1 for size in sizes))
    value = in_ref[...]
    for n, (axis, size) in enumerate(zip(axes, sizes)):
        me = lax.axis_index(axis)
        buffers[n][me] = value
        copies = []
        for k in range(1, size):
            copy = pltpu.make_async_remote_copy(
                src_ref=buffers[n].at[me],
                dst_ref=buffers[n].at[me],
                send_sem=send_sems[n].at[k - 1],
                recv_sem=recv_sems[n].at[k - 1],
                device_id={axis: lax.rem(me + k, size)},
                device_id_type=pl.DeviceIdType.MESH,
            )
            copy.start()
            copies.append(copy)
        for copy in copies:
            copy.wait()
        value = buffers[n][0]
        for k in range(1, size):
            value = value + buffers[n][k]
    out_ref[...] = value


def sum_over(value, axes, collective_id):
    sizes = [lax.axis_size(axis) for axis in axes]
    scratch = [pltpu.VMEM((size,) + value.shape, jnp.float32) for size in sizes]
    scratch += [pltpu.SemaphoreType.DMA((size - 1,)) for size in sizes]
    scratch += [pltpu.SemaphoreType.DMA((size - 1,)) for size in sizes]
    return pl.pallas_call(
        lambda *refs: sum_kernel(axes, sizes, *refs),
        out_shape=jax.ShapeDtypeStruct(value.shape, jnp.float32),
        in_specs=[pl.BlockSpec(memory_space=pltpu.VMEM)],
        out_specs=pl.BlockSpec(memory_space=pltpu.VMEM),
        scratch_shapes=scratch,
        compiler_params=pltpu.CompilerParams(collective_id=collective_id, has_side_effects=True),
    )(value)


def on_device_any(
    x_in,
    attn_in,
    grad_qkv,
    grad_out,
    owner,
    step,
    master,
    moment,
    second,
    stat_left,
    stat_right,
    root_left,
    root_right,
    qkv_bias,
    qkv_bias_m,
    qkv_bias_v,
    proj_bias,
    proj_bias_m,
    proj_bias_v,
):
    exact = lax.Precision.HIGHEST
    groups = lax.axis_size("dp")
    own_index = lax.axis_index("dp")
    total_blocks = owner.shape[0]
    slot_count = master.shape[1]
    block_size = master.shape[2]
    tokens = x_in.shape[0] * groups
    rows_q = D // block_size
    cols_q = grad_qkv.shape[1] // block_size
    rows_p = attn_in.shape[1] // block_size
    first_kind = rows_q * cols_q
    count_f = step[0].astype(jnp.float32)
    fix_one = 1.0 - jnp.power(jnp.float32(beta_one), count_f)
    fix_two = 1.0 - jnp.power(jnp.float32(beta_two), count_f)
    blocks = jnp.arange(total_blocks, dtype=jnp.int32)
    position = positions(owner, slot_count)
    spots = groups * slot_count
    matches = position[None, :] == jnp.arange(spots, dtype=jnp.int32)[:, None]
    filled = jnp.any(matches, axis=1)
    holder = jnp.sum(jnp.where(matches, blocks[None, :], 0), axis=1)
    my_blocks = lax.dynamic_slice_in_dim(holder, own_index * slot_count, slot_count)
    my_filled = lax.dynamic_slice_in_dim(filled, own_index * slot_count, slot_count)
    filled_f = my_filled.astype(jnp.float32)
    keep = my_filled[:, None, None]

    depth = x_in.shape[0]
    left = jnp.concatenate(
        [
            x_in.T.reshape(rows_q, block_size, depth),
            attn_in.T.reshape(rows_p, block_size, depth),
        ]
    )
    right = jnp.concatenate(
        [
            grad_qkv.T.reshape(cols_q, block_size, depth),
            grad_out.T.reshape(rows_q, block_size, depth),
        ]
    )
    local_tiles, peaks = place_tiles(
        left,
        right,
        holder,
        filled.astype(jnp.int32),
        first_kind,
        cols_q,
        rows_q,
        groups,
        slot_count,
    )

    width_q, width_p = grad_qkv.shape[1], grad_out.shape[1]
    small = jnp.concatenate(
        [
            jnp.sum(grad_qkv, axis=0, dtype=jnp.float32),
            jnp.sum(grad_out, axis=0, dtype=jnp.float32),
            peaks[:, :, 0].reshape(spots),
        ]
    )
    used = small.shape[0]
    padded = -(-used // 1024) * 1024
    small = jnp.pad(small, (0, padded - used)).reshape(8, padded // 8)
    small = sum_over(small, ("dp",), 0).reshape(padded)
    qkv_total = small[:width_q]
    proj_total = small[width_q : width_q + width_p]
    bound = small[width_q + width_p : used]
    spot_bound = jnp.where(bound > 0.0, bound, 1.0).reshape(groups, 1, slot_count)
    spot_bound = jnp.repeat(spot_bound, block_size, axis=2)
    shrink = 16384.0 / spot_bound
    grow = spot_bound / 16384.0

    pair = own_index // 2
    side = own_index % 2
    pairs = groups // 2
    tiles = local_tiles

    def chunk(array, where):
        return lax.dynamic_index_in_dim(array, where, 0, keepdims=False)

    across = [(d, d ^ 1) for d in range(groups)]
    arrivals = []
    order = list(range(1, pairs))
    if pairs == 4:
        order = [1, 3, 2]
    order = order + [0]
    received = []
    for step_off in order:
        theirs = lax.rem(pair + step_off, pairs) * 2 + 1 - side
        sent = (chunk(tiles, theirs) * chunk(shrink, theirs)).astype(jnp.float16)
        received.append(lax.ppermute(sent, "dp", across))
    after = jnp.int32(0)
    for step_off, got in zip(order, received):
        ours = lax.rem(pair + step_off, pairs) * 2 + side
        both = chunk(tiles, ours + after) * chunk(shrink, ours) + got.astype(jnp.float32)
        if step_off == 0:
            mine = both
        else:
            hop = [(d, ((d // 2 + step_off) % pairs) * 2 + d % 2) for d in range(groups)]
            both = both.astype(jnp.float16)
            arrivals.append(lax.ppermute(both, "dp", hop))
            probe = arrivals[-1][0, 0].astype(jnp.float32)
            after = jnp.minimum((probe == probe).astype(jnp.int32), 0)
    for arrived in arrivals:
        mine = mine + arrived.astype(jnp.float32)
    mine = mine * (chunk(grow, own_index) / tokens)
    mine = mine.reshape(block_size, slot_count, block_size).transpose(1, 0, 2)
    grads = jnp.where(keep, mine, 0.0)
    old_w = master[0]
    old_m = moment[0]
    old_v = second[0]
    old_l = stat_left[0]
    old_r = stat_right[0]
    new_v = beta_two * old_v + (1.0 - beta_two) * grads * grads
    adam_dir = grads / (jnp.sqrt(new_v / fix_two) + epsilon)
    half = jnp.einsum("sij,sjk->sik", root_left[0], grads, precision=exact)
    shampoo_dir = jnp.einsum("sij,sjk->sik", half, root_right[0], precision=exact)
    is_qkv = my_blocks < first_kind
    adam_sq = jnp.sum(adam_dir * adam_dir, axis=(1, 2)) * filled_f
    shampoo_sq = jnp.sum(shampoo_dir * shampoo_dir, axis=(1, 2)) * filled_f
    sums = [
        jnp.sum(jnp.where(is_qkv, adam_sq, 0.0)),
        jnp.sum(jnp.where(is_qkv, 0.0, adam_sq)),
        jnp.sum(jnp.where(is_qkv, shampoo_sq, 0.0)),
        jnp.sum(jnp.where(is_qkv, 0.0, shampoo_sq)),
    ]
    lane = lax.broadcasted_iota(jnp.int32, (8, 128), 1)
    part = jnp.zeros((8, 128), jnp.float32)
    for n, value in enumerate(sums):
        part = jnp.where(lane == n, value, part)
    total = sum_over(part, ("grp", "dp"), 1)
    graft = jnp.sqrt(total[0, 0:2] / (total[0, 2:4] + graft_floor))
    block_graft = jnp.where(is_qkv, graft[0], graft[1])
    new_m = beta_one * old_m + (1.0 - beta_one) * (block_graft[:, None, None] * shampoo_dir)
    new_w = old_w - learn_rate * (new_m + weight_decay * old_w)
    new_l = beta_stat * old_l + (1.0 - beta_stat) * jnp.einsum(
        "sik,sjk->sij", grads, grads, precision=exact
    )
    new_r = beta_stat * old_r + (1.0 - beta_stat) * jnp.einsum(
        "ski,skj->sij", grads, grads, precision=exact
    )
    master_new = jnp.where(keep, new_w, old_w)
    moment_new = jnp.where(keep, new_m, old_m)
    second_new = jnp.where(keep, new_v, old_v)
    left_new = jnp.where(keep, new_l, old_l)
    right_new = jnp.where(keep, new_r, old_r)
    new_weights = master_new.astype(jnp.bfloat16)
    spread = [new_weights]
    turns = None
    if pairs == 4:
        up = [(d, d + 2) for d in range(groups - 2)]
        down = [(d + 2, d) for d in range(groups - 2)]
        from_low, from_high = [new_weights], [new_weights]
        for k in range(1, pairs):
            from_low.append(lax.ppermute(from_low[-1], "dp", up))
            from_high.append(lax.ppermute(from_high[-1], "dp", down))
        rows = []
        for z in range(pairs):
            found = [(k, 0) for k in range(1, z + 1)] + [(k, 1) for k in range(1, pairs - z)]
            rows.append(sorted(found))
        turns = [[0] * pairs for _ in range(pairs)]
        other = [lax.ppermute(new_weights, "dp", across)]
        for m in range(pairs - 1):
            value = None
            probe = other[-1][0, 0, 0].astype(jnp.float32)
            here = pair + jnp.minimum((probe == probe).astype(jnp.int32), 0)
            for z in range(pairs):
                k, way = rows[z][m]
                turns[z][z + k if way else z - k] = m + 1
                part_w = (from_low, from_high)[way][k]
                value = part_w if value is None else jnp.where(here == z, part_w, value)
            spread.append(value)
            other.append(lax.ppermute(value, "dp", across))
    else:
        for step_off in range(1, pairs):
            hop = [(d, ((d // 2 + step_off) % pairs) * 2 + d % 2) for d in range(groups)]
            spread.append(lax.ppermute(new_weights, "dp", hop))
        other = [lax.ppermute(part_w, "dp", across) for part_w in spread]
    everyone = jnp.concatenate(spread + other)
    place_owner = owner // 2
    turn = lax.rem(pair - place_owner + pairs, pairs)
    if turns is not None:
        turn = jnp.zeros_like(owner)
        for z in range(pairs):
            for origin in range(pairs):
                hit = (pair == z) & (place_owner == origin)
                turn = jnp.where(hit, turns[z][origin], turn)
    held = jnp.where(owner % 2 == side, turn, pairs + turn)
    where_held = held * slot_count + (position - owner * slot_count)
    qkv_weight = join_tiles(everyone, where_held, 0, rows_q, cols_q)
    proj_weight = join_tiles(everyone, where_held, first_kind, rows_p, rows_q)
    qb_new, qm_new, qv_new = adamw(
        qkv_bias, qkv_bias_m, qkv_bias_v, qkv_total / tokens, fix_one, fix_two
    )
    pb_new, pm_new, pv_new = adamw(
        proj_bias, proj_bias_m, proj_bias_v, proj_total / tokens, fix_one, fix_two
    )
    return (
        master_new[None],
        moment_new[None],
        second_new[None],
        left_new[None],
        right_new[None],
        qkv_weight,
        proj_weight,
        qb_new,
        qm_new,
        qv_new,
        pb_new,
        pm_new,
        pv_new,
    )


SIDE = 200
COLUMN = 32
HALF = 16
TILE = 128
HALF_TILES = HALF * SIDE // TILE
TILES = 2 * HALF_TILES
PACE = 2
LAG = 2
CHUNKS = TILES // PACE
ROWS = 208
MOVES = 8
FEW = 3
PLANES = 4
STEPS = 8.0
TOP = 32000.0
MESH = pl.DeviceIdType.MESH
TABLE_ROWS = 16
(
    LEFT_AT,
    RIGHT_AT,
    SOURCE,
    GIVE_AT,
    GIVE_SLOT,
    FROM_SLOT,
    HOLDS,
    KINDS,
    SEEN,
    EDGES,
) = range(10)
MOST = 2


def count_from(value, step, most):
    whole = jnp.zeros_like(value)
    for k in range(step, most, step):
        whole = whole + (value >= k).astype(jnp.int32)
    return whole


def table_kernel(cols_q, rows_q, owner_ref, out):
    me = lax.axis_index("dp")
    total, devices = 2 * COLUMN, 2 * PLANES
    split = cols_q * rows_q

    def grid(rows, columns, axis):
        return lax.broadcasted_iota(jnp.int32, (rows, columns), axis)

    def down(mask, value):
        return jnp.sum(jnp.where(mask, value, 0), axis=0, keepdims=True)

    def over(mask, value):
        return jnp.sum(jnp.where(mask, value, 0), axis=1, keepdims=True)

    def both(mask, value):
        return jnp.sum(over(mask, value), axis=0, keepdims=True)

    sub, lane = grid(total, total, 0), grid(total, total, 1)
    row = owner_ref[...]
    col = over(sub == lane, row)
    slot = over((col == row) & (lane < sub), 1)
    dev = grid(total, devices, 1)
    own = col == dev
    n = down(own, 1)
    dsub, dlane = grid(devices, devices, 0), grid(devices, devices, 1)
    here = grid(1, devices, 1)
    even = (here % 2) == 0

    def turned(value):
        return over(dsub == dlane, value)

    swap = (dsub // 2 == dlane // 2) & (dsub != dlane)
    partner = down(swap, turned(n))
    total0 = over(even, n)
    surplus = jnp.abs(total0 - COLUMN)
    crowded = (even & (total0 >= COLUMN)) | (~even & (total0 < COLUMN))
    room = jnp.where(crowded, jnp.minimum(jnp.minimum(MOVES, n), HALF - partner), 0)
    levels = grid(16, devices, 0)
    filled_to = jnp.sum(jnp.minimum(room, levels), axis=1, keepdims=True)
    fits = (filled_to <= surplus) & (grid(16, 1, 0) <= MOVES)
    level = jnp.sum(fits.astype(jnp.int32), axis=0, keepdims=True) - 1
    base = jnp.minimum(room, level)
    rest = surplus - jnp.sum(base, axis=1, keepdims=True)
    can = (room > level).astype(jnp.int32)
    before = down(dsub < dlane, turned(can))
    move = base + jnp.where((can > 0) & (before < rest), 1, 0)
    stay = n - move
    height = stay + down(swap, turned(move))
    start = down((dsub < dlane) & (dsub % 2 == dlane % 2), turned(height))
    far = down(swap, turned(start)) + partner - stay
    moved = slot >= over(own, stay)
    place = jnp.where(moved, over(own, far), over(own, start)) + slot
    parity = over(own, here % 2)
    column = jnp.where(moved, 1 - parity, parity)
    line = column * COLUMN + place
    side = me % 2
    mine = here == me
    my_n, my_stay, my_start = over(mine, n), over(mine, stay), over(mine, start)
    my_height = over(mine, height)
    spots = grid(1, total, 1)
    wanted = spots + side * COLUMN
    wanted = jnp.where(wanted >= total, wanted - total, wanted)
    at = down(line == wanted, sub)
    later = jnp.maximum(at - split, 0)
    first = at < split
    at_row, later_row = count_from(at, cols_q, split), count_from(later, rows_q, total - split)
    left_at = jnp.where(first, at_row, rows_q + later_row)
    right_at = jnp.where(first, at - at_row * cols_q, cols_q + later - later_row * rows_q)
    my_blocks = down((col == me) & (slot == lane), sub)
    source = jnp.where(spots < my_stay, my_start + spots, COLUMN + spots - my_stay)
    source = jnp.where(spots < my_n, jnp.minimum(source, COLUMN + MOVES - 1), 0)
    give_at = jnp.minimum(my_start + my_n + spots, COLUMN - 1)
    give_slot = jnp.minimum(my_stay + spots, HALF - 1)
    spot = spots - my_start
    from_slot = jnp.where(spot < my_stay, spot, jnp.where(my_n > my_stay, 0, HALF + spot - my_n))
    from_slot = jnp.minimum(jnp.maximum(from_slot, 0), HALF + MOVES - 1)
    seen = jnp.where(column == side, place, COLUMN + place)
    edges = jnp.where(spots == 0, my_start, my_start + my_height) * SIDE
    most = jnp.max(move, axis=1, keepdims=True)
    edges = jnp.where(spots == MOST, most, edges)
    rows = {
        LEFT_AT: left_at,
        RIGHT_AT: right_at,
        SOURCE: source,
        GIVE_AT: give_at,
        GIVE_SLOT: give_slot,
        FROM_SLOT: from_slot,
        HOLDS: (spots < my_n).astype(jnp.int32),
        KINDS: (my_blocks < split).astype(jnp.int32),
        SEEN: down(sub == lane, seen),
        EDGES: edges,
    }
    out[...] = jnp.zeros_like(out)
    for n, value in rows.items():
        out[n : n + 1, :total] = value


def layout_tables(owner, cols_q, rows_q):
    return pl.pallas_call(
        lambda *refs: table_kernel(cols_q, rows_q, *refs),
        out_shape=jax.ShapeDtypeStruct((TABLE_ROWS, TILE), jnp.int32),
        in_specs=[vmem()],
        out_specs=vmem(),
    )(owner.reshape(1, -1))


def pack(value):
    top = jnp.max(jnp.abs(value), axis=1, keepdims=True)
    code = jnp.ceil(jnp.log(jnp.maximum(top, 1e-30)) * (STEPS / LN2))
    scale = TOP / jnp.exp(code * (LN2 / STEPS))
    whole = jnp.round(value * scale).astype(jnp.int32)
    codes = jnp.broadcast_to(
        code.astype(jnp.int32), (value.shape[0], ROWS - SIDE, value.shape[2])
    )
    return jnp.concatenate([whole, codes], axis=1).astype(jnp.int16)


def unpack(coded):
    wide = coded.astype(jnp.int32).astype(jnp.float32)
    scale = jnp.exp(wide[:, SIDE : SIDE + 1] * (LN2 / STEPS)) * (1.0 / TOP)
    return wide[:, :SIDE] * scale


LN2 = 0.6931471805599453


def some(k):
    return pl.ds(k * PACE, PACE)


def pieces(j):
    low, high = j * SIDE, (j + 1) * SIDE
    for tile in range(low // TILE, -(-high // TILE)):
        a, b = max(low, tile * TILE), min(high, (tile + 1) * TILE)
        yield tile, slice(a - tile * TILE, b - tile * TILE), slice(a - low, b - low)


def tiles_of(moves):
    return -(-moves * SIDE // TILE)


def put(into, base, j, value):
    for tile, there, here in pieces(j):
        into[base + tile, :SIDE, there] = value[:, here]


def take(ref, base, j, into, n):
    for tile, there, here in pieces(j):
        into[n, :, here] = ref[base + tile, :SIDE, there]


def greet(peers):
    barrier = pltpu.get_barrier_semaphore()
    count = 0
    for condition, device in peers:
        if condition is None:
            pl.semaphore_signal(barrier, inc=1, device_id=device, device_id_type=MESH)
            count = count + 1
        else:

            @pl.when(condition)
            def _():
                pl.semaphore_signal(barrier, inc=1, device_id=device, device_id_type=MESH)

            count = count + condition.astype(jnp.int32)
    pl.semaphore_wait(barrier, count)


def remote(src, dst, send, recv, device):
    return pltpu.make_async_remote_copy(
        src_ref=src, dst_ref=dst, send_sem=send, recv_sem=recv, device_id=device, device_id_type=MESH
    )


def loop(low, high, body):
    lax.fori_loop(low, high, lambda k, carry: (body(k), carry)[1], 0)


def reduce_kernel(
    tokens,
    moves,
    table,
    x_blocks,
    attn_blocks,
    qkv_blocks,
    out_blocks,
    out,
    sums,
    left,
    right,
    stage,
    pair,
    sent_x,
    got_x,
    sent_up,
    got_up,
    sent_down,
    got_down,
    tiles,
    stage_m,
    sent_m,
    got_m,
    sems,
    sems_m,
    load_sems,
):
    me = lax.axis_index("dp")
    loads = []
    for into, parts in ((left, (x_blocks, attn_blocks)), (right, (qkv_blocks, out_blocks))):
        at = 0
        for ref in parts:
            there = into.at[pl.ds(at, ref.shape[0])]
            loads.append(pltpu.make_async_copy(ref, there, load_sems.at[len(loads)]))
            loads[-1].start()
            at += ref.shape[0]
    z, side = me // 2, me % 2
    across = {"dp": me + 1 - 2 * side}
    upper = {"dp": jnp.minimum(me + 2, 2 * PLANES - 1)}
    lower = {"dp": jnp.maximum(me - 2, 0)}
    last = PLANES - 1
    greet([(None, across), (z < last, upper), (z > 0, lower)])
    for load in loads:
        load.wait()

    def copy_x(k):
        return remote(
            sent_x.at[some(k)], got_x.at[some(k)], sems.at[0, k], sems.at[1, k], across
        )

    def copy_up(k):
        return remote(
            sent_up.at[some(k)], got_up.at[some(k)], sems.at[2, k], sems.at[3, k], upper
        )

    def copy_down(k):
        return remote(
            sent_down.at[some(k)], got_down.at[some(k)], sems.at[4, k], sems.at[5, k], lower
        )

    def product(n):
        return lax.dot_general(
            left[table[LEFT_AT, n]],
            right[table[RIGHT_AT, n]],
            (((1,), (1,)), ((), ())),
            preferred_element_type=jnp.float32,
        )

    def send_other(low, high):
        def body(k):
            sent_x[some(k)] = pack(stage[some(k)])
            copy_x(k).start()

        loop(low, high, body)

    def other_part(h, part):
        for j in range(part * 4, part * 4 + 4):
            put(stage, h * HALF_TILES, j, product(COLUMN + h * HALF + j))
        edge = (h * HALF + part * 4) * SIDE
        send_other(edge // (TILE * PACE), (edge + 4 * SIDE) // (TILE * PACE))

    def own_part(h, part):
        for j in range(part * 4, part * 4 + 4):
            put(pair, h * HALF_TILES, j, product(h * HALF + j))

    for part in range(4):
        other_part(0, part)
    for part in range(4):
        own_part(0, part)

    def bias_sums():
        ones = jnp.ones((8, right.shape[2]), jnp.bfloat16)
        sums[...] = jnp.zeros_like(sums)
        for j in range(right.shape[0]):
            total = lax.dot_general(
                ones, right[j], (((1,), (1,)), ((), ())), preferred_element_type=jnp.float32
            )
            sums[j : j + 1, :SIDE] = total[:1]

    def step(t):
        for part in range(4):
            pl.when(t == part)(lambda part=part: other_part(1, part))
        for part in range(4):
            pl.when(t == 4 + part)(lambda part=part: own_part(1, part))
        pl.when(t == 8)(bias_sums)

        @pl.when(t < CHUNKS)
        def _():
            copy_x(t).wait_recv()
            pair[some(t)] += unpack(got_x[some(t)])

        up = t - LAG * z

        @pl.when((up >= 0) & (up < CHUNKS))
        def _():
            @pl.when(z == 0)
            def _():
                sent_up[some(up)] = pack(pair[some(up)])

            @pl.when(z > 0)
            def _():
                copy_up(up).wait_recv()

                @pl.when(z < last)
                def _():
                    sent_up[some(up)] = pack(pair[some(up)] + unpack(got_up[some(up)]))

            @pl.when(z < last)
            def _():
                copy_up(up).start()

        down = t - LAG * (last - z)

        @pl.when((down >= 0) & (down < CHUNKS))
        def _():
            @pl.when(z == last)
            def _():
                sent_down[some(down)] = pack(pair[some(down)])

            @pl.when(z < last)
            def _():
                copy_down(down).wait_recv()

                @pl.when(z > 0)
                def _():
                    sent_down[some(down)] = pack(pair[some(down)] + unpack(got_down[some(down)]))

            @pl.when(z > 0)
            def _():
                copy_down(down).start()

        full = t - LAG * last

        @pl.when(full >= 0)
        def _():
            @pl.when(z > 0)
            def _():
                pair[some(full)] += unpack(got_up[some(full)])

            @pl.when(z < last)
            def _():
                pair[some(full)] += unpack(got_down[some(full)])

            @pl.when((full == HALF_TILES // PACE) | (full == CHUNKS - 1))
            def _():
                h = (full == CHUNKS - 1).astype(jnp.int32)
                for j in range(HALF):
                    take(pair, h * HALF_TILES, j, tiles, h * HALF + j)

    loop(0, CHUNKS + LAG * last, step)

    stage_m[tiles_of(moves) - 1] = jnp.zeros((SIDE, TILE), jnp.float32)
    for k in range(moves):
        put(stage_m, 0, k, tiles[table[GIVE_AT, k]])
    sent_m[...] = pack(stage_m[...])
    move = remote(sent_m, got_m, sems_m.at[0], sems_m.at[1], across)
    move.start()

    def drain(k):
        copy_x(k).wait_send()

        @pl.when(z < last)
        def _():
            copy_up(k).wait_send()

        @pl.when(z > 0)
        def _():
            copy_down(k).wait_send()

    loop(0, CHUNKS, drain)
    move.wait()
    stage_m[...] = unpack(got_m[...])
    for k in range(moves):
        take(stage_m, 0, k, tiles, COLUMN + k)

    def finish(s):
        out[s] = jnp.where(
            table[HOLDS, s] > 0, tiles[jnp.minimum(table[SOURCE, s], COLUMN + moves - 1)] * (1.0 / tokens), 0.0
        )

    loop(0, HALF, finish)


def vmem():
    return pl.BlockSpec(memory_space=pltpu.VMEM)


def smem():
    return pl.BlockSpec(memory_space=pltpu.SMEM)


def hbm():
    return pl.BlockSpec(memory_space=pl.ANY)


def reduce_tiles(table, x_blocks, attn_blocks, qkv_blocks, out_blocks, tokens, moves):
    coded = pltpu.VMEM((TILES, ROWS, TILE), jnp.int16)
    moved = pltpu.VMEM((tiles_of(moves), ROWS, TILE), jnp.int16)
    depth = x_blocks.shape[2]
    rows = x_blocks.shape[0] + attn_blocks.shape[0]
    cols = qkv_blocks.shape[0] + out_blocks.shape[0]
    return pl.pallas_call(
        lambda *refs: reduce_kernel(tokens, moves, *refs),
        out_shape=(
            pltpu.VMEM((HALF, SIDE, SIDE), jnp.float32),
            pltpu.VMEM((BIAS_ROWS, SMALL_WIDE), jnp.float32),
        ),
        in_specs=[smem()] + [hbm()] * 4,
        out_specs=[vmem()] * 2,
        scratch_shapes=[
            pltpu.VMEM((rows, SIDE, depth), jnp.bfloat16),
            pltpu.VMEM((cols, SIDE, depth), jnp.bfloat16),
            pltpu.VMEM((TILES, SIDE, TILE), jnp.float32),
            pltpu.VMEM((TILES, SIDE, TILE), jnp.float32),
            *([coded] * 6),
            pltpu.VMEM((COLUMN + moves, SIDE, SIDE), jnp.float32),
            pltpu.VMEM((tiles_of(moves), SIDE, TILE), jnp.float32),
            moved,
            moved,
            pltpu.SemaphoreType.DMA((6, CHUNKS)),
            pltpu.SemaphoreType.DMA((2,)),
            pltpu.SemaphoreType.DMA((4,)),
        ],
        compiler_params=pltpu.CompilerParams(
            collective_id=0 if moves == MOVES else 2,
            has_side_effects=True,
            vmem_limit_bytes=VMEM_LIMIT,
        ),
    )(table, x_blocks, attn_blocks, qkv_blocks, out_blocks)


VMEM_LIMIT = 44 * 1024 * 1024
STEP_LIMIT = 26 * 1024 * 1024
LAST_LIMIT = 16 * 1024 * 1024
EARLY = 10
FEW_EARLY = 4
SMALL_ROWS = 24
BIAS_ROWS = 16
SMALL_WIDE = 256


def dot3(a, b, dims):
    a_high, b_high = a.astype(jnp.bfloat16), b.astype(jnp.bfloat16)
    a_low = (a - a_high.astype(jnp.float32)).astype(jnp.bfloat16)
    b_low = (b - b_high.astype(jnp.float32)).astype(jnp.bfloat16)

    def dot(p, q):
        return lax.dot_general(p, q, (dims, ((), ())), preferred_element_type=jnp.float32)

    return dot(a_high, b_high) + (dot(a_high, b_low) + dot(a_low, b_high))


def step_kernel(
    moves,
    table,
    fixes,
    grads,
    small,
    master,
    moment,
    second,
    stat_left,
    stat_right,
    root_left,
    root_right,
    state_w,
    state_m,
    state_v,
    state_l,
    state_r,
    small_out,
    blocks,
    state_a,
    state_b,
    sums,
    sums_dp,
    sums_grp,
    light,
    sent_m,
    got_m,
    own,
    got_up,
    got_down,
    known,
    got_x,
    load_sems,
    sum_sems,
    grp_sems,
    move_sems,
    sems,
):
    me = lax.axis_index("dp")
    z, side = me // 2, me % 2
    n_dp, n_grp = lax.axis_size("dp"), lax.axis_size("grp")
    my_grp = lax.axis_index("grp")
    across = {"dp": me + 1 - 2 * side}
    upper = {"dp": jnp.minimum(me + 2, 2 * PLANES - 1)}
    lower = {"dp": jnp.maximum(me - 2, 0)}
    last = PLANES - 1
    held = [state_v, state_a, state_b, state_w, state_m, state_l, state_r]
    given = [second, root_left, root_right, master, moment, stat_left, stat_right]
    loads = []
    for n, (ref, scratch) in enumerate(zip(given, held)):
        copy = pltpu.make_async_copy(ref.at[0], scratch, load_sems.at[n])
        copy.start()
        loads.append(copy)

    peers = [(None, {"dp": lax.rem(me + k, n_dp)}) for k in range(1, n_dp)]
    peers += [(None, {"grp": lax.rem(my_grp + k, n_grp)}) for k in range(1, n_grp)]
    greet(peers)

    early = EARLY if moves == MOVES else FEW_EARLY
    fix_two = fixes[0]
    for copy in loads[:3]:
        copy.wait()

    def direction(s, sums_now):
        adam_q, adam_p, shampoo_q, shampoo_p = sums_now
        grad = grads[s]
        old = state_v[s]
        new = beta_two * old + (1.0 - beta_two) * grad * grad
        adam = grad / (jnp.sqrt(new / fix_two) + epsilon)
        half = dot3(state_a[s], grad, ((1,), (0,)))
        shampoo = dot3(half, state_b[s], ((1,), (0,)))
        state_v[s] = jnp.where(table[HOLDS, s] > 0, new, old)
        state_a[s] = shampoo
        adam_sq = jnp.sum(adam * adam, axis=0, keepdims=True)
        shampoo_sq = jnp.sum(shampoo * shampoo, axis=0, keepdims=True)
        q = table[KINDS, s] > 0
        return (
            adam_q + jnp.where(q, adam_sq, 0.0),
            adam_p + jnp.where(q, 0.0, adam_sq),
            shampoo_q + jnp.where(q, shampoo_sq, 0.0),
            shampoo_p + jnp.where(q, 0.0, shampoo_sq),
        )

    nothing = jnp.zeros((1, SIDE), jnp.float32)
    parts = lax.fori_loop(0, HALF, direction, (nothing,) * 4, unroll=4)
    sums[0, :BIAS_ROWS] = small[...]
    row = lax.broadcasted_iota(jnp.int32, (SMALL_ROWS - BIAS_ROWS, SMALL_WIDE), 0)
    packed = jnp.zeros((SMALL_ROWS - BIAS_ROWS, SMALL_WIDE), jnp.float32)
    for n, part in enumerate(parts):
        packed = jnp.where(row == n, jnp.sum(part), packed)
    sums[0, BIAS_ROWS:] = packed

    copies = []
    for k in range(1, n_dp):
        copy = remote(
            sums.at[0], sums_dp.at[k - 1], sum_sems.at[0, k - 1], sum_sems.at[1, k - 1],
            {"dp": lax.rem(me + k, n_dp)},
        )
        copy.start()
        copies.append(copy)
    for copy in loads[3:5]:
        copy.wait()
    for copy in copies:
        copy.wait()
    for d in range(n_dp):
        value = jnp.where(me == d, sums[0], sums_dp[lax.rem(me - d + n_dp + n_dp - 1, n_dp) % (n_dp - 1)])
        total = value if d == 0 else total + value
    small_out[...] = total[:BIAS_ROWS]
    sums_grp[my_grp] = total[BIAS_ROWS:]
    copies = []
    for k in range(1, n_grp):
        copy = remote(
            sums_grp.at[my_grp], sums_grp.at[my_grp], grp_sems.at[0, k - 1], grp_sems.at[1, k - 1],
            {"grp": lax.rem(my_grp + k, n_grp)},
        )
        copy.start()
        copies.append(copy)
    for copy in copies:
        copy.wait()
    total = sums_grp[0]
    for g in range(1, n_grp):
        total = total + sums_grp[g]
    graft_q = jnp.sqrt(total[0:1] / (total[2:3] + graft_floor))[:, :1]
    graft_p = jnp.sqrt(total[1:2] / (total[3:4] + graft_floor))[:, :1]

    def update(s):
        graft = jnp.where(table[KINDS, s] > 0, graft_q, graft_p)
        old_m, old_w = state_m[s], state_w[s]
        new_m = beta_one * old_m + (1.0 - beta_one) * (graft * state_a[s])
        new_w = old_w - learn_rate * (new_m + weight_decay * old_w)
        state_m[s] = jnp.where(table[HOLDS, s] > 0, new_m, old_m)
        state_w[s] = jnp.where(table[HOLDS, s] > 0, new_w, old_w)
        light[s] = jnp.where(table[KINDS, s] > 0, new_w.T, new_w).astype(jnp.bfloat16)

    loop(0, HALF, update)

    sent_m[...] = jnp.zeros_like(sent_m)
    for k in range(moves):
        put(sent_m, 0, k, light[table[GIVE_SLOT, k]])
    move = remote(sent_m, got_m, move_sems.at[0], move_sems.at[1], across)
    move.start()

    for copy in loads[5:7]:
        copy.wait()

    def stats(s):
        grad = grads[s]
        keep = table[HOLDS, s] > 0
        new_l = beta_stat * state_l[s] + (1.0 - beta_stat) * dot3(grad, grad, ((1,), (1,)))
        new_r = beta_stat * state_r[s] + (1.0 - beta_stat) * dot3(grad, grad, ((0,), (0,)))
        state_l[s] = jnp.where(keep, new_l, state_l[s])
        state_r[s] = jnp.where(keep, new_r, state_r[s])

    def pad(k):
        own[k, SIDE:] = jnp.zeros((ROWS - SIDE, TILE), jnp.bfloat16)

    loop(0, TILES, pad)
    loop(0, early, stats)
    move.wait()
    for k in range(moves):
        take(got_m, 0, k, light, HALF + k)

    def fill(h, part):
        for j in range(part * 4, part * 4 + 4):
            slot = jnp.minimum(table[FROM_SLOT, h * HALF + j], HALF + moves - 1)
            put(own, h * HALF_TILES, j, light[slot])

    fill(0, 0)

    low, high = table[EDGES, 0], table[EDGES, 1]
    shape = (PACE, ROWS, TILE)
    lane = lax.broadcasted_iota(jnp.int32, shape, 0) * TILE + lax.broadcasted_iota(
        jnp.int32, shape, 2
    )
    up_window = -(-HALF_TILES // PACE)
    down_window = HALF_TILES // PACE

    def wide(ref, k):
        return ref[some(k)].astype(jnp.float32)

    def copy_up(k, src):
        return remote(src.at[some(k)], got_up.at[some(k)], sems.at[0, k], sems.at[1, k], upper)

    def copy_down(k, src):
        return remote(src.at[some(k)], got_down.at[some(k)], sems.at[2, k], sems.at[3, k], lower)

    def copy_x(k):
        return remote(known.at[some(k)], got_x.at[some(k)], sems.at[4, k], sems.at[5, k], across)

    def step(t):
        for n in range(1, 8):
            pl.when(t == 4 * SIDE * n // (TILE * PACE))(lambda n=n: fill(n // 4, n % 4))

        up = t - LAG * z

        @pl.when((up >= 0) & (up < CHUNKS))
        def _():
            @pl.when((z == 0) & (up < up_window))
            def _():
                copy_up(up, own).start()

            @pl.when(z > 0)
            def _():
                @pl.when((z > 1) | (up < up_window))
                def _():
                    copy_up(up, own).wait_recv()
                    mask = lane + up * (PACE * TILE) < low
                    got_up[some(up)] = jnp.where(mask, wide(got_up, up), wide(own, up)).astype(
                        jnp.bfloat16
                    )

                @pl.when((z == 1) & (up >= up_window))
                def _():
                    got_up[some(up)] = own[some(up)]

                @pl.when(z < last)
                def _():
                    copy_up(up, got_up).start()

        down = t - LAG * (last - z)

        @pl.when((down >= 0) & (down < CHUNKS))
        def _():
            @pl.when((z == last) & (down >= down_window))
            def _():
                copy_down(down, own).start()

            @pl.when(z < last)
            def _():
                @pl.when((z < last - 1) | (down >= down_window))
                def _():
                    copy_down(down, own).wait_recv()
                    mask = lane + down * (PACE * TILE) >= high
                    got_down[some(down)] = jnp.where(
                        mask, wide(got_down, down), wide(own, down)
                    ).astype(jnp.bfloat16)

                @pl.when((z == last - 1) & (down < down_window))
                def _():
                    got_down[some(down)] = own[some(down)]

                @pl.when(z > 0)
                def _():
                    copy_down(down, got_down).start()

        full = t - LAG * last

        @pl.when(full >= 0)
        def _():
            place = lane + full * (PACE * TILE)
            value = jnp.where(place < low, wide(got_up, full), wide(own, full))
            value = jnp.where(place >= high, wide(got_down, full), value)
            known[some(full)] = value.astype(jnp.bfloat16)
            copy_x(full).start()

            @pl.when((full == HALF_TILES // PACE) | (full == CHUNKS - 1))
            def _():
                h = (full == CHUNKS - 1).astype(jnp.int32)
                for j in range(HALF):
                    take(known, h * HALF_TILES, j, blocks, h * HALF + j)

        @pl.when(t < HALF - early)
        def _():
            stats(early + t)

    loop(0, CHUNKS + LAG * last, step)
    for h in range(2):
        loop(0 if h == 0 else up_window, up_window if h == 0 else CHUNKS, lambda k: copy_x(k).wait_recv())
        for j in range(HALF):
            take(got_x, h * HALF_TILES, j, blocks, COLUMN + h * HALF + j)

    def drain(k):
        copy_x(k).wait_send()

        @pl.when((z == 1) | (z == 2) | ((z == 0) & (k < up_window)))
        def _():
            copy_up(k, own).wait_send()

        @pl.when((z == 1) | (z == 2) | ((z == last) & (k >= down_window)))
        def _():
            copy_down(k, own).wait_send()

    loop(0, CHUNKS, drain)


def apply_step(table, fixes, grads, small, states, moves):
    n_dp, n_grp = lax.axis_size("dp"), lax.axis_size("grp")
    held = pltpu.VMEM((HALF, SIDE, SIDE), jnp.float32)
    line = pltpu.VMEM((TILES, ROWS, TILE), jnp.bfloat16)
    moved = pltpu.VMEM((tiles_of(moves), ROWS, TILE), jnp.bfloat16)
    return pl.pallas_call(
        lambda *refs: step_kernel(moves, *refs),
        out_shape=(
            *([held] * 5),
            jax.ShapeDtypeStruct((BIAS_ROWS, SMALL_WIDE), jnp.float32),
            pltpu.VMEM((2 * COLUMN, SIDE, SIDE), jnp.bfloat16),
        ),
        in_specs=[smem()] * 2 + [vmem()] * 2 + [hbm()] * 7,
        out_specs=[vmem()] * 7,
        scratch_shapes=[
            *([held] * 2),
            pltpu.VMEM((1, SMALL_ROWS, SMALL_WIDE), jnp.float32),
            pltpu.VMEM((n_dp - 1, SMALL_ROWS, SMALL_WIDE), jnp.float32),
            pltpu.VMEM((n_grp, SMALL_ROWS - BIAS_ROWS, SMALL_WIDE), jnp.float32),
            pltpu.VMEM((HALF + MOVES, SIDE, SIDE), jnp.bfloat16),
            moved,
            moved,
            *([line] * 5),
            pltpu.SemaphoreType.DMA((7,)),
            pltpu.SemaphoreType.DMA((2, n_dp - 1)),
            pltpu.SemaphoreType.DMA((2, n_grp - 1)),
            pltpu.SemaphoreType.DMA((2,)),
            pltpu.SemaphoreType.DMA((6, CHUNKS)),
        ],
        compiler_params=pltpu.CompilerParams(
            collective_id=1 if moves == MOVES else 3,
            has_side_effects=True,
            vmem_limit_bytes=STEP_LIMIT,
        ),
    )(table, fixes, grads, small, *states)


def finish_kernel(cols_q, rows_q, rows_p, table, blocks, *refs):
    given, kept = refs[:5], refs[5:10]
    qkv, proj, bands, copy_sems, band_sems = refs[10:]
    stores = []
    for n, (ref, into) in enumerate(zip(given, kept)):
        stores.append(pltpu.make_async_copy(ref, into.at[0], copy_sems.at[n]))
        stores[-1].start()
    for n in range(cols_q + rows_p):
        first, stride = (n, cols_q) if n < cols_q else (cols_q * rows_q + (n - cols_q) * rows_q, 1)
        parts = [
            blocks[table[SEEN, first + k * stride]].astype(jnp.float32) for k in range(rows_q)
        ]
        bands[n] = jnp.concatenate(parts, axis=1).astype(jnp.bfloat16)
        into = qkv.at[n] if n < cols_q else proj.at[n - cols_q]
        stores.append(pltpu.make_async_copy(bands.at[n], into, band_sems.at[n]))
        stores[-1].start()
    for copy in stores:
        copy.wait()


def finish(blocks, table, states, rows_q, cols_q, rows_p):
    across = rows_q * SIDE
    state = jax.ShapeDtypeStruct((1, HALF, SIDE, SIDE), jnp.float32)
    return pl.pallas_call(
        lambda *refs: finish_kernel(cols_q, rows_q, rows_p, *refs),
        out_shape=(
            *([state] * 5),
            jax.ShapeDtypeStruct((cols_q, SIDE, across), jnp.bfloat16),
            jax.ShapeDtypeStruct((rows_p, SIDE, across), jnp.bfloat16),
        ),
        in_specs=[smem()] + [vmem()] * 6,
        out_specs=[hbm()] * 7,
        scratch_shapes=[
            pltpu.VMEM((cols_q + rows_p, SIDE, across), jnp.bfloat16),
            pltpu.SemaphoreType.DMA((5,)),
            pltpu.SemaphoreType.DMA((cols_q + rows_p,)),
        ],
        compiler_params=pltpu.CompilerParams(vmem_limit_bytes=LAST_LIMIT),
    )(table, blocks, *states)


def on_device(
    x_in,
    attn_in,
    grad_qkv,
    grad_out,
    owner,
    step,
    master,
    moment,
    second,
    stat_left,
    stat_right,
    root_left,
    root_right,
    qkv_bias,
    qkv_bias_m,
    qkv_bias_v,
    proj_bias,
    proj_bias_m,
    proj_bias_v,
):
    groups = lax.axis_size("dp")
    slot_count, side = master.shape[1], master.shape[2]
    if (groups, slot_count, side, owner.shape[0]) != (2 * PLANES, HALF, SIDE, 2 * COLUMN):
        return on_device_any(
            x_in, attn_in, grad_qkv, grad_out, owner, step, master, moment, second, stat_left, stat_right,
            root_left, root_right, qkv_bias, qkv_bias_m, qkv_bias_v, proj_bias, proj_bias_m, proj_bias_v,
        )
    depth = x_in.shape[0]
    tokens = depth * groups
    rows_q = D // SIDE
    cols_q = grad_qkv.shape[1] // SIDE
    rows_p = attn_in.shape[1] // SIDE
    count_f = step[0].astype(jnp.float32)
    fix_one = 1.0 - jnp.power(jnp.float32(beta_one), count_f)
    fix_two = 1.0 - jnp.power(jnp.float32(beta_two), count_f)
    table = layout_tables(owner, cols_q, rows_q)
    tiles = (
        x_in.T.reshape(rows_q, SIDE, depth),
        attn_in.T.reshape(rows_p, SIDE, depth),
        grad_qkv.T.reshape(cols_q, SIDE, depth),
        grad_out.T.reshape(rows_q, SIDE, depth),
    )
    states = (master, moment, second, stat_left, stat_right, root_left, root_right)
    fixes = fix_two.reshape(1)

    def path(moves):
        def run(table, fixes, tiles, states):
            grads, small = reduce_tiles(table, *tiles, tokens, moves)
            *stepped, small_sum, blocks = apply_step(table, fixes, grads, small, states, moves)
            return *finish(blocks, table, stepped, rows_q, cols_q, rows_p), small_sum

        return run

    few = table[EDGES, MOST] <= FEW
    *stepped, qkv, proj, small_sum = lax.cond(
        few, path(FEW), path(MOVES), table, fixes, tiles, states
    )
    master_new, moment_new, second_new, left_new, right_new = stepped
    qkv_weight = qkv.reshape(cols_q * SIDE, rows_q * SIDE).T
    proj_weight = proj.reshape(rows_p * SIDE, rows_q * SIDE)
    qkv_total = small_sum[:cols_q, :SIDE].reshape(-1)
    proj_total = small_sum[cols_q : cols_q + rows_q, :SIDE].reshape(-1)
    qb_new, qm_new, qv_new = adamw(
        qkv_bias, qkv_bias_m, qkv_bias_v, qkv_total / tokens, fix_one, fix_two
    )
    pb_new, pm_new, pv_new = adamw(
        proj_bias, proj_bias_m, proj_bias_v, proj_total / tokens, fix_one, fix_two
    )
    return (
        master_new,
        moment_new,
        second_new,
        left_new,
        right_new,
        qkv_weight,
        proj_weight,
        qb_new,
        qm_new,
        qv_new,
        pb_new,
        pm_new,
        pv_new,
    )


def solution(mesh):
    return jax.shard_map(
        on_device,
        mesh=mesh,
        in_specs=(
            P("dp", None),
            P("dp", "grp"),
            P("dp", "grp"),
            P("dp", None),
            P(),
            P(),
            P("grp", "dp", None, None),
            P("grp", "dp", None, None),
            P("grp", "dp", None, None),
            P("grp", "dp", None, None),
            P("grp", "dp", None, None),
            P("grp", "dp", None, None),
            P("grp", "dp", None, None),
            P("grp"),
            P("grp"),
            P("grp"),
            P(),
            P(),
            P(),
        ),
        out_specs=(
            P("grp", "dp", None, None),
            P("grp", "dp", None, None),
            P("grp", "dp", None, None),
            P("grp", "dp", None, None),
            P("grp", "dp", None, None),
            P(None, "grp"),
            P("grp", None),
            P("grp"),
            P("grp"),
            P("grp"),
            P(),
            P(),
            P(),
        ),
        check_vma=False,
    )
```
